32 devices in a mesh: expert: 16 (over z, y, core), half: 2 (over x).
Axes of the slice: x: 2, y: 2, z: 4, core: 2. Of those that a mesh axis runs over, the one named last changes fastest.
Arguments:
- tokens: bfloat16 [256, 2048], P('expert', 'half'), may hold values from -6 to 6
- upstream: bfloat16 [256, 2048], P('expert', 'half'), may hold values from -6 to 6
- expert_ids: int32 [256, 8], P('expert'), may hold values from 0 to 15, all different within a row; in each aligned block of 16 rows (0 to 15, 16 to 31, ...) at most 16 rows name the same one
- gate_probs: float32 [256, 8], P('expert'), may hold values from 0.01 to 1
- pad_mask: int32 [256], P('expert'), may hold values 0 or 1
- gate_weight: bfloat16 [16, 2048, 1536], P('expert', None, 'half'), may hold values from -0.125 to 0.125
- up_weight: bfloat16 [16, 2048, 1536], P('expert', None, 'half'), may hold values from -0.125 to 0.125
- down_weight: bfloat16 [16, 1536, 2048], P('expert', 'half'), may hold values from -0.15625 to 0.15625
Outputs:
- layer_out: bfloat16 [256, 2048], P('expert', 'half')
- grad_tokens: bfloat16 [256, 2048], P('expert', 'half')
The draws below stay inside these ranges and needn't reach their ends.
Inputs may be any that keep to these rules, and one draw needn't show every extreme that they name: `expert_ids`: each row names 8 different experts. In the rows of one device (aligned blocks of 16 rows) no expert is named more than 16 times, a bound that some block reaches.
All inputs are finite; a program needn't handle non-finite values. No bound on the sum of `pad_mask` on one device may be relied on, other than what follows from the above.
Results may differ from the reference program's by a relative error of at most 0.025.
Values may be sent and summed in bfloat16 or wider, within the bound.
A program may use at most 64 MiB of HBM per device.

```python
import math
import jax
import jax.numpy as jnp
import numpy as np
from jax import lax

D = 2048
HID = 1536
TOPK = 8
TOK_DEV = 16
EXPERTS = 16
CAP = 16
TOKENS = 256
N_EXPERT = 16
N_HALF = 2


def touch_ends(entries, rng, least, high):
    longest = entries.shape.index(max(entries.shape))
    spots = []
    for shift in (0, 1):
        where = [jax.random.randint(jax.random.fold_in(rng, axis), (), 0, length) for axis, length in enumerate(entries.shape)]
        where[longest] = (where[longest] + shift) % entries.shape[longest]
        spots.append(tuple(where))
    return entries.at[spots[0]].set(least).at[spots[1]].set(high)


def shard_levels(rng, shape, split, least, high):
    level, own = 1.0, jax.random.fold_in(rng, 6)
    for dim, shards_of in split:
        heights = jnp.exp(jax.random.uniform(jax.random.fold_in(own, dim), (shards_of,), jnp.float32, least / len(split), high / len(split)))
        level = level * jnp.repeat(heights, shape[dim] // shards_of).reshape([-1 if axis == dim else 1 for axis in range(len(shape))])
    return level


def shared_out(key, own, number, rows, count, top, most, slope):
    sequence = jax.random.permutation(key, count)
    heavy_load, usual = portions_of(count, rows * top, most, slope, True), portions_of(count, rows * top, most, slope, False)
    places = jnp.arange(count)

    def named(lengths, offset_by):
        used = int((lengths > 0).sum())
        fixed = max(1, used // 4)
        moved = fixed + (places - fixed + offset_by * (used - fixed)) % max(1, count - fixed)
        return jnp.zeros((count,), jnp.int32).at[sequence[jnp.where(places < fixed, places, moved)]].set(jnp.asarray(lengths, jnp.int32))

    lengths = jnp.where(number % 4 == 0, named(heavy_load, number // 4), named(usual, number - number // 4 - 1))
    mixed = jax.random.permutation(jax.random.fold_in(own, 3), count)
    source_of, sink = mixed[0:count // 2 * 2:2], mixed[1:count // 2 * 2:2]
    margin = jnp.minimum(lengths[source_of] - 1, most - lengths[sink]) // 2
    margin = jnp.where((source_of == sequence[0]) | (sink == sequence[0]) | (lengths[sink] == 0), 0, jnp.maximum(margin, 0))
    moved = jax.random.randint(jax.random.fold_in(own, 4), (count // 2,), 0, 1 << 20) % (margin + 1)
    lengths = lengths.at[source_of].add(-moved).at[sink].add(moved)
    items = jnp.searchsorted(jnp.cumsum(lengths), jnp.arange(rows * top), side="right").astype(jnp.int32)
    listing = items.reshape(top, rows).T
    listing = listing[jax.random.permutation(jax.random.fold_in(own, 1), rows)]
    offset_by = jax.random.randint(jax.random.fold_in(own, 2), (rows, 1), 0, top)
    return jnp.take_along_axis(listing, (jnp.arange(top)[None, :] + offset_by) % top, axis=1)


def portions_of(count, total, reach, skew, full):
    weights = [(1 << 20) // math.isqrt(rank ** skew) + 1 for rank in range(1, count + 1)]
    largest = reach if full else min(reach, max(-(-total // count), total * weights[0] // sum(weights)))
    least = 1 if total - largest >= count - 1 else 0
    counts, surplus = [largest] + [least] * (count - 1), total - largest - least * (count - 1)
    while surplus > 0:
        movable = [i for i in range(1, count) if counts[i] < largest] or [i for i in range(1, count) if counts[i] < reach]
        pool, budget = sum([weights[i] for i in movable]), surplus
        for i in movable:
            extra = min(reach - counts[i], max(1, budget * weights[i] // pool), surplus)
            counts[i] = counts[i] + extra
            surplus = surplus - extra
    return np.array(counts)


def noise(key, extent, scale, bound, shards=(), kind=jnp.bfloat16):
    drawn = jax.random.normal(key, extent, jnp.float32) * scale
    if len(shards) > 0:
        drawn = shard_levels(key, extent, shards, -0.22, 0.18) * drawn
    return jnp.clip(drawn, min=-bound, max=bound).astype(kind)


def setup_inputs(seed: int = 0) -> dict:
    key_of = jax.random.split(jax.random.key(seed), 9)
    tokens = noise(key_of[0], (TOKENS, D), 1.0, 6.0, ((0, 16), (1, 2)))
    upstream = noise(key_of[1], (TOKENS, D), 1.0, 6.0, ((0, 16), (1, 2)))
    expert_ids_keys = jax.random.split(jax.random.fold_in(key_of[2], 1), TOKENS // TOK_DEV)
    expert_ids_turns = jax.random.permutation(jax.random.fold_in(key_of[2], 3), TOKENS // TOK_DEV)
    expert_ids = jax.vmap(lambda own, number: shared_out(jax.random.fold_in(key_of[2], 2), own, number, TOK_DEV, EXPERTS, TOPK, CAP, 2))(expert_ids_keys, expert_ids_turns).reshape((TOKENS, TOPK))
    gate_probs = jnp.clip(jnp.exp(math.log(1.0) - 4.6051702 * jax.random.uniform(key_of[3], (TOKENS, TOPK), jnp.float32) ** shard_levels(key_of[3], (TOKENS, TOPK), ((0, 16),), -0.2, 0.2)), 0.01, 1.0)
    pad_mask = touch_ends((jax.random.randint(key_of[4], (TOKENS,), 0, 8) < 7).astype(jnp.int32), jax.random.fold_in(key_of[4], 1), 0, 1)
    gate_weight = noise(key_of[5], (EXPERTS, D, HID), D ** -0.5, 0.125, ((0, 16), (2, 2)))
    up_weight = noise(key_of[6], (EXPERTS, D, HID), D ** -0.5, 0.125, ((0, 16), (2, 2)))
    down_weight = noise(key_of[7], (EXPERTS, HID, D), HID ** -0.5, 0.15625, ((0, 16), (1, 2)))
    return {"tokens": tokens, "upstream": upstream, "expert_ids": expert_ids, "gate_probs": gate_probs, "pad_mask": pad_mask, "gate_weight": gate_weight, "up_weight": up_weight, "down_weight": down_weight}


orth_weight = 0.25

def slot_numbers(expert_ids):
    blocks = expert_ids.reshape(N_EXPERT, TOK_DEV * TOPK)
    onehot = (blocks[:, :, None] == jnp.arange(EXPERTS, dtype=jnp.int32)[None, None, :]).astype(jnp.int32)
    before = jnp.cumsum(onehot, axis=1) - onehot
    slot_index = lax.optimization_barrier(jnp.sum(before * onehot, axis=2))
    return slot_index.reshape(TOKENS * TOPK).astype(jnp.int32)

def rounded(value):
    return lax.optimization_barrier(value.astype(jnp.bfloat16)).astype(jnp.float32)

def reference(tokens, upstream, expert_ids, gate_probs, pad_mask, gate_weight, up_weight, down_weight):
    piece_width = HID // N_HALF
    slot_index = slot_numbers(expert_ids)
    flat_ids = expert_ids.reshape(TOKENS * TOPK).astype(jnp.int32)
    item_index = jnp.arange(TOKENS * TOPK, dtype=jnp.int32)
    source = item_index // (TOK_DEV * TOPK)
    table = jnp.full((EXPERTS, N_EXPERT * CAP), -1, jnp.int32)
    table = table.at[flat_ids, source * CAP + slot_index].set(item_index)

    def expert_inputs(row_ids):
        valid = row_ids >= 0
        safe = jnp.where(valid, row_ids, 0)
        rows_in = jnp.where(valid[:, None], tokens[safe // TOPK], jnp.zeros((), jnp.bfloat16))
        return (valid, safe, rows_in)

    def forward(carry, packed):
        row_ids, weight_gate, weight_up, weight_down = packed
        valid, safe, rows_in = expert_inputs(row_ids)
        gate_val = jnp.dot(rows_in, weight_gate, preferred_element_type=jnp.float32)
        up_val = jnp.dot(rows_in, weight_up, preferred_element_type=jnp.float32)
        hidden_act = (jax.nn.silu(gate_val) * up_val).astype(jnp.bfloat16)
        total = jnp.zeros((N_EXPERT * CAP, D), jnp.float32)
        for piece in range(N_HALF):
            lower = piece * piece_width
            term = jnp.dot(hidden_act[:, lower:lower + piece_width], weight_down[lower:lower + piece_width], preferred_element_type=jnp.float32)
            total = total + rounded(term)
        out_rows = total.astype(jnp.bfloat16)
        target = jnp.where(valid, safe, TOKENS * TOPK)
        carry = carry.at[target].set(out_rows, mode='drop')
        return (carry, None)
    outputs, _ = lax.scan(forward, jnp.zeros((TOKENS * TOPK, D), jnp.bfloat16), (table, gate_weight, up_weight, down_weight))
    out_float = outputs.reshape(TOKENS, TOPK, D).astype(jnp.float32)
    shares = gate_probs / lax.optimization_barrier(jnp.sum(gate_probs, axis=1, keepdims=True))
    layer_out = lax.optimization_barrier(jnp.sum(shares[:, :, None] * out_float, axis=1)).astype(jnp.bfloat16)
    gram = jnp.einsum('tjd,tkd->tjk', out_float, out_float) / jnp.sqrt(jnp.float32(D))
    off_diag = 1.0 - jnp.eye(TOPK, dtype=jnp.float32)
    coeffs = orth_weight * gram * off_diag
    grad_out = pad_mask.astype(jnp.float32)[:, None, None] * (shares[:, :, None] * upstream.astype(jnp.float32)[:, None, :] + jnp.einsum('tjk,tkd->tjd', coeffs, out_float))
    grad_items = grad_out.astype(jnp.bfloat16).reshape(TOKENS * TOPK, D)

    def backward(carry, packed):
        row_ids, weight_gate, weight_up, weight_down = packed
        valid, safe, rows_in = expert_inputs(row_ids)
        gate_val = jnp.dot(rows_in, weight_gate, preferred_element_type=jnp.float32)
        up_val = jnp.dot(rows_in, weight_up, preferred_element_type=jnp.float32)
        grad_rows = jnp.where(valid[:, None], grad_items[safe], jnp.zeros((), jnp.bfloat16))
        grad_act = jnp.dot(grad_rows, weight_down.T, preferred_element_type=jnp.float32)
        sigma = jax.nn.sigmoid(gate_val)
        grad_gate = (grad_act * up_val * sigma * (1.0 + gate_val * (1.0 - sigma))).astype(jnp.bfloat16)
        grad_up = (grad_act * gate_val * sigma).astype(jnp.bfloat16)
        total = jnp.zeros((N_EXPERT * CAP, D), jnp.float32)
        for piece in range(N_HALF):
            lower = piece * piece_width
            term = jnp.dot(grad_gate[:, lower:lower + piece_width], weight_gate[:, lower:lower + piece_width].T, preferred_element_type=jnp.float32)
            term = term + jnp.dot(grad_up[:, lower:lower + piece_width], weight_up[:, lower:lower + piece_width].T, preferred_element_type=jnp.float32)
            total = total + rounded(term)
        grad_in_rows = total.astype(jnp.bfloat16).astype(jnp.float32)
        target = jnp.where(valid, safe // TOPK, TOKENS)
        carry = carry.at[target].add(grad_in_rows, mode='drop')
        return (carry, None)
    grad_sum, _ = lax.scan(backward, jnp.zeros((TOKENS, D), jnp.float32), (table, gate_weight, up_weight, down_weight))
    return (layer_out, grad_sum.astype(jnp.bfloat16))
```

```python
import functools
import math

import jax
import jax.numpy as jnp
from jax import lax
from jax.experimental import pallas as pl
from jax.experimental.pallas import tpu as pltpu
from jax.sharding import PartitionSpec as P

orth_weight = 0.25


def assign_slots(expert_ids, experts, capacity):
    tok_count, top_count = expert_ids.shape
    flat_ids = expert_ids.reshape(tok_count * top_count)
    onehot = (flat_ids[:, None] == jnp.arange(experts, dtype=jnp.int32)[None, :]).astype(jnp.int32)
    before = jnp.cumsum(onehot, axis=0) - onehot
    slot_index = jnp.sum(before * onehot, axis=1)
    return flat_ids * capacity + slot_index


def placement_matrix(slot_dest, slots_total):
    row_index = jnp.arange(slots_total, dtype=jnp.int32)
    return (row_index[:, None] == slot_dest[None, :]).astype(jnp.bfloat16)


def to_experts(place, items):
    whole = lax.all_gather(items, "half", axis=1, tiled=True)
    buckets = jnp.dot(place, whole, preferred_element_type=jnp.float32).astype(jnp.bfloat16)
    return lax.all_to_all(buckets, "expert", split_axis=0, concat_axis=0, tiled=True)


def to_homes(partial_value):
    summed = lax.psum_scatter(
        partial_value.astype(jnp.bfloat16), "half", scatter_dimension=1, tiled=True
    )
    return lax.all_to_all(summed, "expert", split_axis=0, concat_axis=0, tiled=True)


def block_of(width, most):
    return next((b for b in (1024, 512, 256, 128) if b <= most and width % b == 0), width)


def tiles(width, body, most=256):
    size = block_of(width, most)

    def step(j, carry):
        body(pl.ds(pl.multiple_of(j * size, size), size), size)
        return carry

    lax.fori_loop(0, width // size, step, 0)


def dot(a, b):
    return jnp.dot(a, b, preferred_element_type=jnp.float32)


def dot_t(a, b):
    return lax.dot_general(a, b, (((1,), (1,)), ((), ())), preferred_element_type=jnp.float32)


def copy_kernel(a_ref, b_ref, a_out, b_out):
    a_out[...] = a_ref[...]
    b_out[...] = b_ref[...]


def fused_kernel(
    n, halves,
    tok_hbm, up_hbm, ids_hbm, probs_hbm, pad_hbm, wg_hbm, wu_hbm, wd_hbm,
    layer_ref, gtok_ref,
    up_ref, ids_ref, probs_ref, pad_ref,
    tok_buf, wg, wu, wd, gate_v, up_v, act_v, hid, gg, gu,
    osend, orecv, ored, xrecv, xs, gram_s, whole_s, gsend, grows, psend, prec, fsend, frecv, rsend, fin,
    w_sem, tok_ss, tok_rs, part_ss, part_rs, out_ss, out_rs, gram_ss, gram_rs,
    grad_ss, grad_rs, relay_ss, pair_ss, pair_rs, fpart_ss, fpart_rs, fin_ss, fin_rs,
):
    e = lax.axis_index("expert")
    h = lax.axis_index("half")
    tok, width = up_ref.shape
    hidden = wg.shape[1]
    rows = n * tok
    chips = n // 2
    group = min(n, 8)
    parity = lax.rem(e, 2)
    chip = lax.div(e, 2)
    sibling = e + 1 - 2 * parity
    full = halves * width

    def remote(src, dst, ssem, rsem, pe, ph):
        return pltpu.make_async_remote_copy(
            src_ref=src, dst_ref=dst, send_sem=ssem, recv_sem=rsem,
            device_id=(pe, ph), device_id_type=pl.DeviceIdType.MESH,
        )

    def wrap(a, d, size):
        return lax.rem(a + d, size)

    def flip(a, d):
        bit = 1
        out = a
        while bit <= d:
            if d & bit:
                out = out + bit * (1 - 2 * lax.rem(lax.div(a, bit), 2))
            bit *= 2
        return out

    def arrived(slot, rsem):
        remote(slot, slot, pair_ss.at[0], rsem, sibling, h).wait_recv()

    sends = []

    def send(*args):
        c = remote(*args)
        c.start()
        sends.append(c)

    moves = (
        (tok_hbm, tok_buf.at[h, e]), (ids_hbm, ids_ref), (probs_hbm, probs_ref),
        (pad_hbm, pad_ref), (up_hbm, up_ref),
        (wg_hbm.at[0], wg), (wu_hbm.at[0], wu), (wd_hbm.at[0], wd),
    )
    loads = [pltpu.make_async_copy(src, dst, w_sem.at[i]) for i, (src, dst) in enumerate(moves)]
    for c in loads:
        c.start()

    others = list(range(1, halves))
    near = list(range(1, n))
    outer = near[::-1]
    chips_near = list(range(1, chips))
    chips_far = chips_near[::-1]

    barrier = pltpu.get_barrier_semaphore()
    for d in outer:
        pl.semaphore_signal(
            barrier, inc=1, device_id=(flip(e, d), h), device_id_type=pl.DeviceIdType.MESH
        )
    for d in others:
        pl.semaphore_signal(
            barrier, inc=1, device_id=(e, wrap(h, d, halves)), device_id_type=pl.DeviceIdType.MESH
        )
    pl.semaphore_wait(barrier, len(outer) + len(others))

    loads[0].wait()
    k = 0
    mine = tok_buf.at[h, e]
    for d in chips_far:
        send(mine, mine, tok_ss.at[k], tok_rs.at[h, e], 2 * flip(chip, d) + parity, h)
        k += 1
    for d in others:
        send(mine, mine, tok_ss.at[k], tok_rs.at[h, e], e, wrap(h, d, halves))
        k += 1
    send(mine, mine, tok_ss.at[k], tok_rs.at[h, e], sibling, h)
    k += 1
    for d in chips_near:
        pe = 2 * flip(chip, d) + parity
        slot = tok_buf.at[h, pe]
        arrived(slot, tok_rs.at[h, pe])
        for dh in others:
            send(slot, slot, tok_ss.at[k], tok_rs.at[h, pe], e, wrap(h, dh, halves))
            k += 1
        send(slot, slot, tok_ss.at[k], tok_rs.at[h, pe], sibling, h)
        k += 1
    for d in [0] + chips_near:
        pe = 2 * flip(chip, d) + parity
        for dh in others:
            ph = wrap(h, halves - dh, halves)
            slot = tok_buf.at[ph, pe]
            arrived(slot, tok_rs.at[ph, pe])
            send(slot, slot, tok_ss.at[k], tok_rs.at[ph, pe], sibling, h)
            k += 1
    for c in loads[1:7]:
        c.wait()
    for dh in [0] + others:
        ph = wrap(h, halves - dh, halves)
        for d in [0] + chips_near:
            pe = 2 * flip(chip, d) + 1 - parity
            arrived(tok_buf.at[ph, pe], tok_rs.at[ph, pe])

        def hidden_step(cols, size, ph=ph, dh=dh):
            at = pl.ds(pl.multiple_of(ph * width, width), width)
            x = tok_buf[ph].reshape(rows, width)
            gate = dot(x, wg[at, cols])
            up = dot(x, wu[at, cols])
            if dh:
                gate = gate + gate_v[:, cols]
                up = up + up_v[:, cols]
            gate_v[:, cols] = gate
            up_v[:, cols] = up
            if dh == halves - 1:
                hid[:, cols] = (gate / (1.0 + jnp.exp(-gate)) * up).astype(jnp.bfloat16)

        tiles(hidden, hidden_step)
    loads[7].wait()

    for dh in others + [0]:
        ph = wrap(h, dh, halves)

        def down_step(cols, size, ph=ph, dh=dh):
            at = pl.ds(pl.multiple_of(cols.start + ph * width, size), size)
            part = dot(hid[...], wd[:, at])
            osend[dh, :, :, cols] = part.reshape(n, tok, size).astype(jnp.bfloat16)

        tiles(width, down_step, 1024)
        if dh:
            for j, d in enumerate(outer + [0]):
                pe = flip(e, d)
                send(
                    osend.at[dh, pe], orecv.at[halves - dh, pe],
                    part_ss.at[dh, j], part_rs.at[halves - dh, j], e, ph,
                )

    eye = (
        lax.broadcasted_iota(jnp.int32, (tok, tok), 0)
        == lax.broadcasted_iota(jnp.int32, (tok, tok), 1)
    )
    top = ids_ref.shape[0]
    lane = lax.broadcasted_iota(jnp.int32, (tok, top), 1)

    def column(row):
        return jnp.sum(jnp.where(eye, jnp.broadcast_to(row, (tok, tok)), 0.0), axis=1, keepdims=True)

    ids = jnp.zeros((tok, top), jnp.float32)
    probs = jnp.zeros((tok, top), jnp.float32)
    for j in range(top):
        ids = jnp.where(lane == j, column(ids_ref[j:j + 1, :].astype(jnp.float32)), ids)
        probs = jnp.where(lane == j, column(probs_ref[j:j + 1, :]), probs)
    pad = column(pad_ref[...].astype(jnp.float32))
    shares = probs / jnp.sum(probs, axis=1, keepdims=True)
    for j, d in enumerate(outer + [0]):
        pe = flip(e, d)
        total = osend[0, pe].astype(jnp.float32)
        for dh in others:
            arrived(orecv.at[dh, pe], part_rs.at[dh, j])
            total = total + orecv[dh, pe].astype(jnp.float32)
        if d:
            ored[pe] = total.astype(jnp.bfloat16)
            send(ored.at[pe], xrecv.at[e], out_ss.at[j], out_rs.at[e], pe, h)
        else:
            xrecv[e] = total.astype(jnp.bfloat16)
    def share_of(i):
        listed = (ids == i.astype(jnp.float32)).astype(jnp.float32)
        return jnp.sum(listed * shares, axis=1, keepdims=True), jnp.sum(listed, axis=1, keepdims=True)

    layer = jnp.zeros((tok, width), jnp.float32)
    for d in [0] + near:
        pe = flip(e, d)
        share, listed = share_of(pe)
        if d:
            arrived(xrecv.at[pe], out_rs.at[pe])
        value = jnp.where(listed > 0.0, xrecv[pe].astype(jnp.float32), 0.0)
        xs[pe] = value.astype(jnp.bfloat16)
        layer = layer + share * value

    x_all = xs[...].reshape(rows, width)
    same = (
        lax.rem(lax.broadcasted_iota(jnp.int32, (tok, rows), 1), tok)
        == lax.broadcasted_iota(jnp.int32, (tok, rows), 0)
    ).astype(jnp.float32)
    gram = dot_t(x_all, x_all).reshape(n, tok, rows) * same[None]
    gram_s[h] = jnp.sum(gram, axis=1)
    for dh in range(1, halves):
        send(gram_s.at[h], gram_s.at[h], gram_ss.at[dh], gram_rs.at[h], e, wrap(h, dh, halves))
    for dh in range(1, halves):
        ph = wrap(h, halves - dh, halves)
        arrived(gram_s.at[ph], gram_rs.at[ph])
    whole = gram_s[0]
    for i in range(1, halves):
        whole = whole + gram_s[i]
    apart = (
        lax.div(lax.broadcasted_iota(jnp.int32, (n, rows), 1), tok)
        != lax.broadcasted_iota(jnp.int32, (n, rows), 0)
    ).astype(jnp.float32)
    whole = whole * (apart * (orth_weight / math.sqrt(full)))
    whole_s[...] = whole
    x_all = xs[...].reshape(rows, width)
    upstream = up_ref[...].astype(jnp.float32)
    for g in range(n // group):
        first = pl.multiple_of(flip(lax.div(e, group), g) * group, group)
        coeffs = whole_s[pl.ds(first, group), :][:, None, :] * same[None]
        coeffs = coeffs.reshape(group * tok, rows)
        high = coeffs.astype(jnp.bfloat16)
        low = (coeffs - high.astype(jnp.float32)).astype(jnp.bfloat16)
        mixed = (dot(high, x_all) + dot(low, x_all)).reshape(group, tok, width)
        for i in range(group):
            share, _ = share_of(first + i)
            gsend[first + i] = (pad * (share * upstream + mixed[i])).astype(jnp.bfloat16)
        for d in range(max(1, g * group), (g + 1) * group):
            pe = flip(e, d)
            send(gsend.at[pe], grows.at[h, e], grad_ss.at[d], grad_rs.at[h, e], pe, h)
        if g == 0:
            for dh in others:
                send(
                    gsend.at[e], grows.at[h, e], relay_ss.at[dh - 1], grad_rs.at[h, e],
                    e, wrap(h, dh, halves),
                )
    layer_ref[...] = layer.astype(jnp.bfloat16)
    k = len(others)
    grows[h, e] = gsend[e]
    for d in near:
        pe = flip(e, d)
        slot = grows.at[h, pe]
        arrived(slot, grad_rs.at[h, pe])
        for dh in others:
            send(slot, slot, relay_ss.at[k], grad_rs.at[h, pe], e, wrap(h, dh, halves))
            k += 1
    for dh in [0] + others:
        ph = wrap(h, halves - dh, halves)
        if dh:
            for d in [0] + near:
                pe = flip(e, d)
                arrived(grows.at[ph, pe], grad_rs.at[ph, pe])

        def act_step(cols, size, ph=ph, dh=dh):
            at = pl.ds(pl.multiple_of(ph * width, width), width)
            act = dot_t(grows[ph].reshape(rows, width), wd[cols, at])
            if dh:
                act = act + act_v[:, cols]
            if dh < halves - 1:
                act_v[:, cols] = act
            else:
                gate = gate_v[:, cols]
                sigma = 1.0 / (1.0 + jnp.exp(-gate))
                gg[:, cols] = (
                    act * up_v[:, cols] * sigma * (1.0 + gate * (1.0 - sigma))
                ).astype(jnp.bfloat16)
                gu[:, cols] = (act * gate * sigma).astype(jnp.bfloat16)

        tiles(hidden, act_step)

    for dh in others + [0]:
        ph = wrap(h, dh, halves)

        def back_step(cols, size, ph=ph, dh=dh):
            at = pl.ds(pl.multiple_of(cols.start + ph * width, size), size)
            part = dot_t(gg[...], wg[at, :]) + dot_t(gu[...], wu[at, :])
            part = part.astype(jnp.bfloat16).reshape(chips, 2, tok, size)
            for q in range(2):
                psend[dh, q, :, :, cols] = part[:, q]

        tiles(width, back_step, 1024)
        send(psend.at[dh, 1 - parity], prec.at[dh], pair_ss.at[dh], pair_rs.at[dh], sibling, h)
    order = chips_far + [0]
    for dh in others:
        arrived(prec.at[dh], pair_rs.at[dh])
        for j, d in enumerate(order):
            pm = flip(chip, d)
            fsend[dh, pm] = (
                psend[dh, parity, pm].astype(jnp.float32) + prec[dh, pm].astype(jnp.float32)
            ).astype(jnp.bfloat16)
            send(
                fsend.at[dh, pm], frecv.at[halves - dh, pm],
                fpart_ss.at[dh, j], fpart_rs.at[halves - dh, j], e, wrap(h, dh, halves),
            )
    arrived(prec.at[0], pair_rs.at[0])
    for j, d in enumerate(order):
        pm = flip(chip, d)
        total = psend[0, parity, pm].astype(jnp.float32) + prec[0, pm].astype(jnp.float32)
        for dh in others:
            arrived(frecv.at[dh, pm], fpart_rs.at[dh, j])
            total = total + frecv[dh, pm].astype(jnp.float32)
        if d:
            rsend[pm] = total.astype(jnp.bfloat16)
            send(rsend.at[pm], fin.at[chip], fin_ss.at[j], fin_rs.at[chip], 2 * pm + parity, h)
    for d in chips_near:
        pm = flip(chip, d)
        arrived(fin.at[pm], fin_rs.at[pm])
        total = total + fin[pm].astype(jnp.float32)
    gtok_ref[...] = total.astype(jnp.bfloat16)
    for c in sends:
        c.wait_send()


def fused(tokens, upstream, expert_ids, gate_probs, pad_mask, gate_weight, up_weight, down_weight):
    n, halves = lax.axis_size("expert"), lax.axis_size("half")
    tok, width = tokens.shape
    hidden = gate_weight.shape[2]
    rows, full, chips = n * tok, halves * width, n // 2
    top = expert_ids.shape[1]
    low, wide = jnp.bfloat16, jnp.float32
    vmem, dma = pltpu.VMEM, pltpu.SemaphoreType.DMA
    local = pl.BlockSpec(memory_space=pltpu.VMEM)
    remain = pl.BlockSpec(memory_space=pl.ANY)
    result = [jax.ShapeDtypeStruct((tok, width), low)] * 2
    outs = pl.pallas_call(
        functools.partial(fused_kernel, n, halves),
        out_shape=result,
        in_specs=[remain] * 8,
        out_specs=[local] * 2,
        scratch_shapes=[
            vmem((tok, width), low),
            vmem((top, tok), jnp.int32),
            vmem((top, tok), wide),
            vmem((1, tok), jnp.int32),
            vmem((halves, n, tok, width), low),
            vmem((full, hidden), low),
            vmem((full, hidden), low),
            vmem((hidden, full), low),
            vmem((rows, hidden), wide),
            vmem((rows, hidden), wide),
            vmem((rows, hidden), wide),
            vmem((rows, hidden), low),
            vmem((rows, hidden), low),
            vmem((rows, hidden), low),
            vmem((halves, n, tok, width), low),
            vmem((halves, n, tok, width), low),
            vmem((n, tok, width), low),
            vmem((n, tok, width), low),
            vmem((n, tok, width), low),
            vmem((halves, n, rows), wide),
            vmem((n, rows), wide),
            vmem((n, tok, width), low),
            vmem((halves, n, tok, width), low),
            vmem((halves, 2, chips, tok, width), low),
            vmem((halves, chips, tok, width), low),
            vmem((halves, chips, tok, width), low),
            vmem((halves, chips, tok, width), low),
            vmem((chips, tok, width), low),
            vmem((chips, tok, width), low),
            dma((8,)),
            dma((2 * halves * n,)),
            dma((halves, n)),
            dma((halves, n)),
            dma((halves, n)),
            dma((n,)),
            dma((n,)),
            dma((halves,)),
            dma((halves,)),
            dma((n,)),
            dma((halves, n)),
            dma((halves * n,)),
            dma((halves,)),
            dma((halves,)),
            dma((halves, chips)),
            dma((halves, chips)),
            dma((chips,)),
            dma((chips,)),
        ],
        compiler_params=pltpu.CompilerParams(
            collective_id=0, has_side_effects=True, vmem_limit_bytes=56 * 1024 * 1024
        ),
        name="experts",
    )(
        tokens, upstream, expert_ids.T, gate_probs.T, pad_mask.reshape(1, tok),
        gate_weight, up_weight, down_weight,
    )
    return pl.pallas_call(
        copy_kernel, out_shape=result, in_specs=[local] * 2, out_specs=[local] * 2, name="results"
    )(*outs)


def shards(tokens, upstream, expert_ids, gate_probs, pad_mask, gate_weight, up_weight, down_weight):
    tok_count, top_count = expert_ids.shape
    experts = lax.axis_size("expert")
    capacity = min(tok_count, 2 * tok_count * top_count // experts)
    if capacity == tok_count and experts > 1 and experts & (experts - 1) == 0:
        return fused(
            tokens, upstream, expert_ids, gate_probs, pad_mask, gate_weight, up_weight, down_weight
        )
    slots_total = experts * capacity
    full_width = tokens.shape[1] * lax.axis_size("half")
    slot_dest = assign_slots(expert_ids, experts, capacity)
    place_items = placement_matrix(slot_dest, slots_total)
    place_tokens = jnp.sum(place_items.reshape(slots_total, tok_count, top_count), axis=2)
    weight_gate = gate_weight[0]
    weight_up = up_weight[0]
    weight_down = down_weight[0]
    rows_in = to_experts(place_tokens, tokens)
    gate_val = jnp.dot(rows_in, weight_gate, preferred_element_type=jnp.float32)
    up_val = jnp.dot(rows_in, weight_up, preferred_element_type=jnp.float32)
    hidden_act = (jax.nn.silu(gate_val) * up_val).astype(jnp.bfloat16)
    partial_value = jnp.dot(hidden_act, weight_down, preferred_element_type=jnp.float32)
    out_home = to_homes(partial_value)
    outputs = jnp.take(out_home, slot_dest, axis=0).reshape(tok_count, top_count, -1)
    out_float = outputs.astype(jnp.float32)
    shares = gate_probs / jnp.sum(gate_probs, axis=1, keepdims=True)
    layer_out = jnp.sum(shares[:, :, None] * out_float, axis=1).astype(jnp.bfloat16)
    gram_part = jnp.einsum("tjd,tkd->tjk", out_float, out_float) / math.sqrt(full_width)
    gram = lax.psum(gram_part, "half")
    off_diag = 1.0 - jnp.eye(top_count, dtype=jnp.float32)
    coeffs = orth_weight * gram * off_diag
    grad_out = pad_mask.astype(jnp.float32)[:, None, None] * (
        shares[:, :, None] * upstream.astype(jnp.float32)[:, None, :]
        + jnp.einsum("tjk,tkd->tjd", coeffs, out_float)
    )
    grad_items = grad_out.astype(jnp.bfloat16).reshape(tok_count * top_count, -1)
    grad_rows = to_experts(place_items, grad_items)
    grad_act = jnp.einsum("rd,hd->rh", grad_rows, weight_down, preferred_element_type=jnp.float32)
    sigma = jax.nn.sigmoid(gate_val)
    grad_gate = (grad_act * up_val * sigma * (1.0 + gate_val * (1.0 - sigma))).astype(jnp.bfloat16)
    grad_up = (grad_act * gate_val * sigma).astype(jnp.bfloat16)
    grad_partial = jnp.einsum(
        "rh,dh->rd", grad_gate, weight_gate, preferred_element_type=jnp.float32
    )
    grad_partial = grad_partial + jnp.einsum(
        "rh,dh->rd", grad_up, weight_up, preferred_element_type=jnp.float32
    )
    grad_home = to_homes(grad_partial)
    grad_pairs = jnp.take(grad_home, slot_dest, axis=0).reshape(tok_count, top_count, -1)
    grad_tokens = jnp.sum(grad_pairs.astype(jnp.float32), axis=1).astype(jnp.bfloat16)
    return (layer_out, grad_tokens)


def solution(mesh):
    in_specs = (
        P("expert", "half"),
        P("expert", "half"),
        P("expert", None),
        P("expert", None),
        P("expert"),
        P("expert", None, "half"),
        P("expert", None, "half"),
        P("expert", "half", None),
    )
    out_specs = (P("expert", "half"), P("expert", "half"))
    return jax.shard_map(shards, mesh=mesh, in_specs=in_specs, out_specs=out_specs, check_vma=False)
```

```python
import functools
import math

import jax
import jax.numpy as jnp
from jax import lax
from jax.experimental import pallas as pl
from jax.experimental.pallas import tpu as pltpu
from jax.sharding import PartitionSpec as P

orth_weight = 0.25


def assign_slots(expert_ids, experts, capacity):
    tok_count, top_count = expert_ids.shape
    flat_ids = expert_ids.reshape(tok_count * top_count)
    onehot = (flat_ids[:, None] == jnp.arange(experts, dtype=jnp.int32)[None, :]).astype(jnp.int32)
    before = jnp.cumsum(onehot, axis=0) - onehot
    slot_index = jnp.sum(before * onehot, axis=1)
    return flat_ids * capacity + slot_index


def placement_matrix(slot_dest, slots_total):
    row_index = jnp.arange(slots_total, dtype=jnp.int32)
    return (row_index[:, None] == slot_dest[None, :]).astype(jnp.bfloat16)


def to_experts(place, items):
    whole = lax.all_gather(items, "half", axis=1, tiled=True)
    buckets = jnp.dot(place, whole, preferred_element_type=jnp.float32).astype(jnp.bfloat16)
    return lax.all_to_all(buckets, "expert", split_axis=0, concat_axis=0, tiled=True)


def to_homes(partial_value):
    summed = lax.psum_scatter(
        partial_value.astype(jnp.bfloat16), "half", scatter_dimension=1, tiled=True
    )
    return lax.all_to_all(summed, "expert", split_axis=0, concat_axis=0, tiled=True)


def block_of(width, most):
    return next((b for b in (1024, 512, 256, 128) if b <= most and width % b == 0), width)


def tiles(width, body, most=256):
    size = block_of(width, most)

    def step(j, carry):
        body(pl.ds(pl.multiple_of(j * size, size), size), size)
        return carry

    lax.fori_loop(0, width // size, step, 0)


def dot(a, b):
    return jnp.dot(a, b, preferred_element_type=jnp.float32)


def dot_t(a, b):
    return lax.dot_general(a, b, (((1,), (1,)), ((), ())), preferred_element_type=jnp.float32)


def copy_kernel(a_ref, b_ref, a_out, b_out):
    a_out[...] = a_ref[...]
    b_out[...] = b_ref[...]


def fused_kernel(
    n, groups,
    tok_hbm, up_hbm, ids_hbm, probs_hbm, pad_hbm, wg_hbm, wu_hbm, wd_hbm,
    layer_ref, gtok_ref,
    up_ref, ids_ref, probs_ref, pad_ref,
    tok_buf, wg, wu, wd, gate_v, up_v, act_v, hid, gg, gu,
    osend, orecv, ored, xrecv, xs, gram_s, share_s, gsend, grows, psend, prec, fsend, frecv, rsend, fin,
    w_sem, plane_ss, cross_ss, twin_ss, tok_rs, twin_rs, part_ss, part_rs, out_ss, out_rs, gram_ss, gram_rs,
    grad_ss, grad_rs, relay_ss, relay_rs, pair_ss, pair_rs, fpart_ss, fpart_rs, fin_ss, fin_rs,
):
    e = lax.axis_index("expert")
    h = lax.axis_index("half")
    sub, width = tok_buf.shape[3:]
    hidden = wg.shape[1]
    tok = groups * sub
    rows = n * sub
    chips = n // 2
    parity = lax.rem(e, 2)
    chip = lax.div(e, 2)
    sibling = e + 1 - 2 * parity
    other = 1 - h
    full = 2 * width

    def remote(src, dst, ssem, rsem, pe, ph):
        return pltpu.make_async_remote_copy(
            src_ref=src, dst_ref=dst, send_sem=ssem, recv_sem=rsem,
            device_id=(pe, ph), device_id_type=pl.DeviceIdType.MESH,
        )

    def send(*args):
        remote(*args).start()

    def flip(a, d):
        bit = 1
        out = a
        while bit <= d:
            if d & bit:
                out = out + bit * (1 - 2 * lax.rem(lax.div(a, bit), 2))
            bit *= 2
        return out

    def arrived(slot, rsem):
        remote(slot, slot, pair_ss.at[0], rsem, sibling, h).wait_recv()

    def drained(sent, ssem):
        remote(sent, sent, ssem, pair_rs.at[0], sibling, h).wait_send()

    moves = [(tok_hbm.at[pl.ds(g * sub, sub)], tok_buf.at[g, h, e]) for g in range(groups)]
    moves += [(ids_hbm, ids_ref), (probs_hbm, probs_ref), (pad_hbm, pad_ref)]
    moves += [(up_hbm.at[pl.ds(g * sub, sub)], up_ref.at[g]) for g in range(groups)]
    moves += [(wg_hbm.at[0], wg), (wu_hbm.at[0], wu), (wd_hbm.at[0], wd)]
    loads = [pltpu.make_async_copy(src, dst, w_sem.at[i]) for i, (src, dst) in enumerate(moves)]
    for c in loads:
        c.start()

    near = list(range(1, n))
    outer = near[::-1]
    chips_near = list(range(1, chips))
    chips_far = chips_near[::-1]

    barrier = pltpu.get_barrier_semaphore()
    for d in outer:
        pl.semaphore_signal(
            barrier, inc=1, device_id=(flip(e, d), h), device_id_type=pl.DeviceIdType.MESH
        )
    pl.semaphore_signal(barrier, inc=1, device_id=(e, other), device_id_type=pl.DeviceIdType.MESH)
    pl.semaphore_wait(barrier, n)

    def peer(d):
        return 2 * flip(chip, d) + parity

    for g in range(groups):
        loads[g].wait()
        mine = tok_buf.at[g, h, e]
        for d in chips_far:
            send(mine, mine, plane_ss.at[g], tok_rs.at[g, h, e], peer(d), h)
        send(mine, mine, cross_ss.at[g], tok_rs.at[g, h, e], e, other)
        send(mine, mine, twin_ss.at[g], twin_rs.at[g, h], sibling, h)

    for c in loads[groups:-3]:
        c.wait()
    eye = (
        lax.broadcasted_iota(jnp.int32, (tok, tok), 0)
        == lax.broadcasted_iota(jnp.int32, (tok, tok), 1)
    )
    top = ids_ref.shape[0]
    lane = lax.broadcasted_iota(jnp.int32, (tok, top), 1)

    def column(row):
        return jnp.sum(jnp.where(eye, jnp.broadcast_to(row, (tok, tok)), 0.0), axis=1, keepdims=True)

    ids = jnp.zeros((tok, top), jnp.float32)
    probs = jnp.zeros((tok, top), jnp.float32)
    for j in range(top):
        ids = jnp.where(lane == j, column(ids_ref[j:j + 1, :].astype(jnp.float32)), ids)
        probs = jnp.where(lane == j, column(probs_ref[j:j + 1, :]), probs)
    pad = column(pad_ref[...].astype(jnp.float32))
    shares = probs / jnp.sum(probs, axis=1, keepdims=True)
    for i in range(n):
        share = jnp.sum(jnp.where(ids == float(i), shares, 0.0), axis=1, keepdims=True)
        share_s[i] = jnp.broadcast_to(share, (tok, share_s.shape[2]))

    for g in range(groups):
        for d in chips_near:
            slot = tok_buf.at[g, h, peer(d)]
            arrived(slot, tok_rs.at[g, h, peer(d)])
            send(slot, slot, cross_ss.at[g], tok_rs.at[g, h, peer(d)], e, other)
            send(slot, slot, twin_ss.at[g], twin_rs.at[g, h], sibling, h)

    def gathered(g):
        for d in [0] + chips_near:
            slot = tok_buf.at[g, other, peer(d)]
            arrived(slot, tok_rs.at[g, other, peer(d)])
            send(slot, slot, twin_ss.at[g], twin_rs.at[g, other], sibling, h)
        for ph in range(2):
            arrived(tok_buf.at[g, ph, pl.ds(0, chips)], twin_rs.at[g, ph])

    def hidden_rows(g):
        at = pl.ds(g * rows, rows)

        def hidden_step(cols, size):
            gate = up = None
            for ph in range(2):
                depth = pl.ds(ph * width, width)
                x = tok_buf[g, ph].reshape(rows, width)
                gate_part = dot(x, wg[depth, cols])
                up_part = dot(x, wu[depth, cols])
                gate = gate_part if gate is None else gate + gate_part
                up = up_part if up is None else up + up_part
            gate_v[at, cols] = gate
            up_v[at, cols] = up
            hid[at, cols] = (gate / (1.0 + jnp.exp(-gate)) * up).astype(jnp.bfloat16)

        tiles(hidden, hidden_step)

    def down(g, far):
        start = (other if far else h) * width

        def down_step(cols, size):
            at = pl.ds(pl.multiple_of(cols.start + start, size), size)
            part = dot(hid[pl.ds(g * rows, rows), :], wd[:, at])
            osend[g, far, :, :, cols] = part.reshape(n, sub, size).astype(jnp.bfloat16)

        tiles(width, down_step, 1024)

    def cross_parts(g):
        for d in outer + [0]:
            pe = flip(e, d)
            send(osend.at[g, 1, pe], orecv.at[g, pe], part_ss.at[g], part_rs.at[g, pe], e, other)

    def forward(g, first, last):
        for d in (outer + [0])[first:last]:
            pe = flip(e, d)
            arrived(orecv.at[g, pe], part_rs.at[g, pe])
            total = osend[g, 0, pe].astype(jnp.float32) + orecv[g, pe].astype(jnp.float32)
            total = total.astype(jnp.bfloat16)
            if d:
                ored[g, pe] = total
                send(ored.at[g, pe], xrecv.at[g, e], out_ss.at[g], out_rs.at[g, e], pe, h)
            else:
                xrecv[g, e] = total

    same = (
        lax.rem(lax.broadcasted_iota(jnp.int32, (sub, rows), 1), sub)
        == lax.broadcasted_iota(jnp.int32, (sub, rows), 0)
    ).astype(jnp.float32)
    apart = (
        lax.div(lax.broadcasted_iota(jnp.int32, (n, rows), 1), sub)
        != lax.broadcasted_iota(jnp.int32, (n, rows), 0)
    ).astype(jnp.float32)

    def share_of(g, i):
        return share_s[i, pl.ds(g * sub, sub), :][:, :1]

    def products(g):
        layer = jnp.zeros((sub, width), jnp.float32)
        for d in [0] + near:
            pe = flip(e, d)
            share = share_of(g, pe)
            if d:
                arrived(xrecv.at[g, pe], out_rs.at[g, pe])
            value = jnp.where(share > 0.0, xrecv[g, pe].astype(jnp.float32), 0.0)
            xs[g, pe] = value.astype(jnp.bfloat16)
            layer = layer + share * value
        x_all = xs[g].reshape(rows, width)
        gram = dot_t(x_all, x_all).reshape(n, sub, rows) * same[None]
        gram_s[g, h] = jnp.sum(gram, axis=1)
        send(gram_s.at[g, h], gram_s.at[g, h], gram_ss.at[g], gram_rs.at[g], e, other)
        return layer

    def mix(g):
        arrived(gram_s.at[g, other], gram_rs.at[g])
        whole = (gram_s[g, 0] + gram_s[g, 1]) * (apart * (orth_weight / math.sqrt(full)))
        x_all = xs[g].reshape(rows, width)
        coeffs = (whole[:, None, :] * same[None]).reshape(rows, rows)
        high = coeffs.astype(jnp.bfloat16)
        low = (coeffs - high.astype(jnp.float32)).astype(jnp.bfloat16)
        mixed = (dot(high, x_all) + dot(low, x_all)).reshape(n, sub, width)
        upstream = up_ref[g].astype(jnp.float32)
        real = pad[g * sub:(g + 1) * sub]
        for i in range(n):
            gsend[g, i] = (real * (share_of(g, i) * upstream + mixed[i])).astype(jnp.bfloat16)
        for d in near:
            pe = flip(e, d)
            send(gsend.at[g, pe], grows.at[h, g, e], grad_ss.at[g], grad_rs.at[g, e], pe, h)
        send(gsend.at[g, e], grows.at[h, g, e], relay_ss.at[g], relay_rs.at[g], e, other)
        grows[h, g, e] = gsend[g, e]

    def relay(g, first, last):
        for d in near[first:last]:
            pe = flip(e, d)
            slot = grows.at[h, g, pe]
            arrived(slot, grad_rs.at[g, pe])
            send(slot, slot, relay_ss.at[g], relay_rs.at[g], e, other)

    gathered(0)
    for c in loads[-3:-1]:
        c.wait()
    hidden_rows(0)
    loads[-1].wait()
    down(0, 1)
    cross_parts(0)
    gathered(1)
    hidden_rows(1)
    down(1, 1)
    cross_parts(1)
    down(0, 0)
    down(1, 0)
    forward(0, 0, n)
    forward(1, 0, n // 4)
    layer_a = products(0)
    forward(1, n // 4, 9 * n // 16)
    mix(0)
    forward(1, 9 * n // 16, n)
    layer_b = products(1)
    relay(0, 0, n // 4)
    mix(1)
    layer_ref[...] = jnp.concatenate([layer_a, layer_b], axis=0).astype(jnp.bfloat16)
    relay(0, n // 4, n - 1)
    relay(1, 0, n - 1)

    for dh in range(2):
        ph = lax.rem(h + dh, 2)
        if dh:
            for g in range(groups):
                arrived(grows.at[other, g], relay_rs.at[g])

        def act_step(cols, size, ph=ph, dh=dh):
            at = pl.ds(pl.multiple_of(ph * width, width), width)
            act = dot_t(grows[ph].reshape(groups * rows, width), wd[cols, at])
            if dh:
                act = act + act_v[:, cols]
                gate = gate_v[:, cols]
                sigma = 1.0 / (1.0 + jnp.exp(-gate))
                gg[:, cols] = (
                    act * up_v[:, cols] * sigma * (1.0 + gate * (1.0 - sigma))
                ).astype(jnp.bfloat16)
                gu[:, cols] = (act * gate * sigma).astype(jnp.bfloat16)
            else:
                act_v[:, cols] = act

        tiles(hidden, act_step)

    for far in (1, 0):
        start = (other if far else h) * width

        def back_step(cols, size, start=start, far=far):
            at = pl.ds(pl.multiple_of(cols.start + start, size), size)
            part = dot_t(gg[...], wg[at, :]) + dot_t(gu[...], wu[at, :])
            part = part.astype(jnp.bfloat16).reshape(groups, chips, 2, sub, size)
            for g in range(groups):
                for q in range(2):
                    psend[far, q, :, g, :, cols] = part[g, :, q]

        tiles(width, back_step, 1024)
        send(psend.at[far, 1 - parity], prec.at[far], pair_ss.at[far], pair_rs.at[far], sibling, h)
    order = chips_far + [0]
    arrived(prec.at[1], pair_rs.at[1])
    for d in order:
        pm = flip(chip, d)
        fsend[pm] = (
            psend[1, parity, pm].astype(jnp.float32) + prec[1, pm].astype(jnp.float32)
        ).astype(jnp.bfloat16)
        send(fsend.at[pm], frecv.at[pm], fpart_ss, fpart_rs.at[pm], e, other)
    arrived(prec.at[0], pair_rs.at[0])
    for d in order:
        pm = flip(chip, d)
        total = psend[0, parity, pm].astype(jnp.float32) + prec[0, pm].astype(jnp.float32)
        arrived(frecv.at[pm], fpart_rs.at[pm])
        total = total + frecv[pm].astype(jnp.float32)
        if d:
            rsend[pm] = total.astype(jnp.bfloat16)
            send(rsend.at[pm], fin.at[chip], fin_ss, fin_rs.at[chip], peer(d), h)
    for d in chips_near:
        pm = flip(chip, d)
        arrived(fin.at[pm], fin_rs.at[pm])
        total = total + fin[pm].astype(jnp.float32)
    gtok_ref[...] = total.reshape(tok, width).astype(jnp.bfloat16)
    for g in range(groups):
        drained(tok_buf.at[g, 0, pl.ds(0, chips - 1)], plane_ss.at[g])
        drained(tok_buf.at[g, 0, pl.ds(0, chips)], cross_ss.at[g])
        drained(tok_buf.at[g, 0], twin_ss.at[g])
        drained(osend.at[g, 1], part_ss.at[g])
        drained(ored.at[g, pl.ds(0, n - 1)], out_ss.at[g])
        drained(gram_s.at[g, 0], gram_ss.at[g])
        drained(gsend.at[g, pl.ds(0, n - 1)], grad_ss.at[g])
        drained(grows.at[0, g], relay_ss.at[g])
    for far in range(2):
        drained(psend.at[far, 0], pair_ss.at[far])
    drained(fsend, fpart_ss)
    drained(rsend.at[pl.ds(0, chips - 1)], fin_ss)


def fused(tokens, upstream, expert_ids, gate_probs, pad_mask, gate_weight, up_weight, down_weight):
    n, groups = lax.axis_size("expert"), 2
    tok, width = tokens.shape
    hidden = gate_weight.shape[2]
    sub, full, chips = tok // groups, 2 * width, n // 2
    every = n * tok
    top = expert_ids.shape[1]
    low, wide = jnp.bfloat16, jnp.float32
    vmem, dma = pltpu.VMEM, pltpu.SemaphoreType.DMA
    local = pl.BlockSpec(memory_space=pltpu.VMEM)
    remain = pl.BlockSpec(memory_space=pl.ANY)
    result = [jax.ShapeDtypeStruct((tok, width), low)] * 2
    outs = pl.pallas_call(
        functools.partial(fused_kernel, n, groups),
        out_shape=result,
        in_specs=[remain] * 8,
        out_specs=[local] * 2,
        scratch_shapes=[
            vmem((groups, sub, width), low),
            vmem((top, tok), jnp.int32),
            vmem((top, tok), wide),
            vmem((1, tok), jnp.int32),
            vmem((groups, 2, n, sub, width), low),
            vmem((full, hidden), low),
            vmem((full, hidden), low),
            vmem((hidden, full), low),
            vmem((every, hidden), wide),
            vmem((every, hidden), wide),
            vmem((every, hidden), wide),
            vmem((every, hidden), low),
            vmem((every, hidden), low),
            vmem((every, hidden), low),
            vmem((groups, 2, n, sub, width), low),
            vmem((groups, n, sub, width), low),
            vmem((groups, n, sub, width), low),
            vmem((groups, n, sub, width), low),
            vmem((groups, n, sub, width), low),
            vmem((groups, 2, n, n * sub), wide),
            vmem((n, tok, 128), wide),
            vmem((groups, n, sub, width), low),
            vmem((2, groups, n, sub, width), low),
            vmem((2, 2, chips, groups, sub, width), low),
            vmem((2, chips, groups, sub, width), low),
            vmem((chips, groups, sub, width), low),
            vmem((chips, groups, sub, width), low),
            vmem((chips, groups, sub, width), low),
            vmem((chips, groups, sub, width), low),
            dma((2 * groups + 6,)),
            dma((groups,)),
            dma((groups,)),
            dma((groups,)),
            dma((groups, 2, n)),
            dma((groups, 2)),
            dma((groups,)),
            dma((groups, n)),
            dma((groups,)),
            dma((groups, n)),
            dma((groups,)),
            dma((groups,)),
            dma((groups,)),
            dma((groups, n)),
            dma((groups,)),
            dma((groups,)),
            dma((2,)),
            dma((2,)),
            dma(()),
            dma((chips,)),
            dma(()),
            dma((chips,)),
        ],
        compiler_params=pltpu.CompilerParams(
            collective_id=0, has_side_effects=True, vmem_limit_bytes=56 * 1024 * 1024
        ),
        name="experts",
    )(
        tokens, upstream, expert_ids.T, gate_probs.T, pad_mask.reshape(1, tok),
        gate_weight, up_weight, down_weight,
    )
    return pl.pallas_call(
        copy_kernel, out_shape=result, in_specs=[local] * 2, out_specs=[local] * 2, name="results"
    )(*outs)


def shards(tokens, upstream, expert_ids, gate_probs, pad_mask, gate_weight, up_weight, down_weight):
    tok_count, top_count = expert_ids.shape
    experts = lax.axis_size("expert")
    capacity = min(tok_count, 2 * tok_count * top_count // experts)
    paired = experts > 3 and experts & (experts - 1) == 0 and lax.axis_size("half") == 2
    if capacity == tok_count and tok_count % 16 == 0 and paired:
        return fused(
            tokens, upstream, expert_ids, gate_probs, pad_mask, gate_weight, up_weight, down_weight
        )
    slots_total = experts * capacity
    full_width = tokens.shape[1] * lax.axis_size("half")
    slot_dest = assign_slots(expert_ids, experts, capacity)
    place_items = placement_matrix(slot_dest, slots_total)
    place_tokens = jnp.sum(place_items.reshape(slots_total, tok_count, top_count), axis=2)
    weight_gate = gate_weight[0]
    weight_up = up_weight[0]
    weight_down = down_weight[0]
    rows_in = to_experts(place_tokens, tokens)
    gate_val = jnp.dot(rows_in, weight_gate, preferred_element_type=jnp.float32)
    up_val = jnp.dot(rows_in, weight_up, preferred_element_type=jnp.float32)
    hidden_act = (jax.nn.silu(gate_val) * up_val).astype(jnp.bfloat16)
    partial_value = jnp.dot(hidden_act, weight_down, preferred_element_type=jnp.float32)
    out_home = to_homes(partial_value)
    outputs = jnp.take(out_home, slot_dest, axis=0).reshape(tok_count, top_count, -1)
    out_float = outputs.astype(jnp.float32)
    shares = gate_probs / jnp.sum(gate_probs, axis=1, keepdims=True)
    layer_out = jnp.sum(shares[:, :, None] * out_float, axis=1).astype(jnp.bfloat16)
    gram_part = jnp.einsum("tjd,tkd->tjk", out_float, out_float) / math.sqrt(full_width)
    gram = lax.psum(gram_part, "half")
    off_diag = 1.0 - jnp.eye(top_count, dtype=jnp.float32)
    coeffs = orth_weight * gram * off_diag
    grad_out = pad_mask.astype(jnp.float32)[:, None, None] * (
        shares[:, :, None] * upstream.astype(jnp.float32)[:, None, :]
        + jnp.einsum("tjk,tkd->tjd", coeffs, out_float)
    )
    grad_items = grad_out.astype(jnp.bfloat16).reshape(tok_count * top_count, -1)
    grad_rows = to_experts(place_items, grad_items)
    grad_act = jnp.einsum("rd,hd->rh", grad_rows, weight_down, preferred_element_type=jnp.float32)
    sigma = jax.nn.sigmoid(gate_val)
    grad_gate = (grad_act * up_val * sigma * (1.0 + gate_val * (1.0 - sigma))).astype(jnp.bfloat16)
    grad_up = (grad_act * gate_val * sigma).astype(jnp.bfloat16)
    grad_partial = jnp.einsum(
        "rh,dh->rd", grad_gate, weight_gate, preferred_element_type=jnp.float32
    )
    grad_partial = grad_partial + jnp.einsum(
        "rh,dh->rd", grad_up, weight_up, preferred_element_type=jnp.float32
    )
    grad_home = to_homes(grad_partial)
    grad_pairs = jnp.take(grad_home, slot_dest, axis=0).reshape(tok_count, top_count, -1)
    grad_tokens = jnp.sum(grad_pairs.astype(jnp.float32), axis=1).astype(jnp.bfloat16)
    return (layer_out, grad_tokens)


def solution(mesh):
    in_specs = (
        P("expert", "half"),
        P("expert", "half"),
        P("expert", None),
        P("expert", None),
        P("expert"),
        P("expert", None, "half"),
        P("expert", None, "half"),
        P("expert", "half", None),
    )
    out_specs = (P("expert", "half"), P("expert", "half"))
    return jax.shard_map(shards, mesh=mesh, in_specs=in_specs, out_specs=out_specs, check_vma=False)
```

```python
import functools
import math

import jax
import jax.numpy as jnp
from jax import lax
from jax.experimental import pallas as pl
from jax.experimental.pallas import tpu as pltpu
from jax.sharding import PartitionSpec as P

orth_weight = 0.25


def assign_slots(expert_ids, experts, capacity):
    tok_count, top_count = expert_ids.shape
    flat_ids = expert_ids.reshape(tok_count * top_count)
    onehot = (flat_ids[:, None] == jnp.arange(experts, dtype=jnp.int32)[None, :]).astype(jnp.int32)
    before = jnp.cumsum(onehot, axis=0) - onehot
    slot_index = jnp.sum(before * onehot, axis=1)
    return flat_ids * capacity + slot_index


def placement_matrix(slot_dest, slots_total):
    row_index = jnp.arange(slots_total, dtype=jnp.int32)
    return (row_index[:, None] == slot_dest[None, :]).astype(jnp.bfloat16)


def to_experts(place, items):
    whole = lax.all_gather(items, "half", axis=1, tiled=True)
    buckets = jnp.dot(place, whole, preferred_element_type=jnp.float32).astype(jnp.bfloat16)
    return lax.all_to_all(buckets, "expert", split_axis=0, concat_axis=0, tiled=True)


def to_homes(partial_value):
    summed = lax.psum_scatter(
        partial_value.astype(jnp.bfloat16), "half", scatter_dimension=1, tiled=True
    )
    return lax.all_to_all(summed, "expert", split_axis=0, concat_axis=0, tiled=True)


def block_of(width, most):
    return next((b for b in (1024, 512, 256, 128) if b <= most and width % b == 0), width)


def tiles(width, body, most=256):
    size = block_of(width, most)

    def step(j, carry):
        body(pl.ds(pl.multiple_of(j * size, size), size), size)
        return carry

    lax.fori_loop(0, width // size, step, 0)


def dot(a, b):
    return jnp.dot(a, b, preferred_element_type=jnp.float32)


def dot_t(a, b):
    return lax.dot_general(a, b, (((1,), (1,)), ((), ())), preferred_element_type=jnp.float32)


def copy_kernel(a_ref, b_ref, a_out, b_out):
    a_out[...] = a_ref[...]
    b_out[...] = b_ref[...]


def fused_kernel(
    n, groups,
    tok_hbm, up_hbm, ids_hbm, probs_hbm, pad_hbm, wg_hbm, wu_hbm, wd_hbm,
    layer_ref, gtok_ref,
    up_ref, ids_ref, probs_ref, pad_ref,
    tok_buf, wg, wu, wd, gate_v, up_v, act_v, hid, gg, gu,
    osend, orecv, ored, xrecv, xs, gram_s, share_s, gsend, grows, psend, prec, fsend, frecv, rsend, fin,
    w_sem, line_ss, quad_ss, twin_ss, line_rs, quad_rs, twin_rs, part_ss, part_rs, out_ss, out_rs,
    gram_ss, gram_rs, grad_ss, grad_rs, relay_ss, relay_rs, pair_ss, pair_rs, fpart_ss, fpart_rs, fin_ss, fin_rs,
):
    e = lax.axis_index("expert")
    h = lax.axis_index("half")
    sub, width = tok_buf.shape[5:]
    hidden = wg.shape[1]
    tok = groups * sub
    rows = n * sub
    chips = n // 2
    columns = chips // 2
    parity = lax.rem(e, 2)
    chip = lax.div(e, 2)
    y = lax.rem(chip, 2)
    z = lax.div(chip, 2)
    sibling = e + 1 - 2 * parity
    other = 1 - h
    full = 2 * width

    def remote(src, dst, ssem, rsem, pe, ph):
        return pltpu.make_async_remote_copy(
            src_ref=src, dst_ref=dst, send_sem=ssem, recv_sem=rsem,
            device_id=(pe, ph), device_id_type=pl.DeviceIdType.MESH,
        )

    def send(*args):
        remote(*args).start()

    def flip(a, d):
        bit = 1
        out = a
        while bit <= d:
            if d & bit:
                out = out + bit * (1 - 2 * lax.rem(lax.div(a, bit), 2))
            bit *= 2
        return out

    def arrived(slot, rsem):
        remote(slot, slot, line_ss, rsem, sibling, h).wait_recv()

    def drained(sent, ssem):
        remote(sent, sent, ssem, twin_rs.at[0, 0], sibling, h).wait_send()

    moves = [(tok_hbm.at[pl.ds(g * sub, sub)], tok_buf.at[h, g, z, y, parity]) for g in range(groups)]
    moves += [(ids_hbm, ids_ref), (probs_hbm, probs_ref), (pad_hbm, pad_ref)]
    moves += [(up_hbm.at[pl.ds(g * sub, sub)], up_ref.at[g]) for g in range(groups)]
    moves += [(wg_hbm.at[0], wg), (wu_hbm.at[0], wu), (wd_hbm.at[0], wd)]
    loads = [pltpu.make_async_copy(src, dst, w_sem.at[i]) for i, (src, dst) in enumerate(moves)]
    for c in loads:
        c.start()

    near = list(range(1, chips))
    outer = near[::-1]

    barrier = pltpu.get_barrier_semaphore()
    for d in reversed(range(1, n)):
        pl.semaphore_signal(
            barrier, inc=1, device_id=(flip(e, d), h), device_id_type=pl.DeviceIdType.MESH
        )
    for pe in (e, 4 * z + 2 * (1 - y) + parity):
        pl.semaphore_signal(
            barrier, inc=1, device_id=(pe, other), device_id_type=pl.DeviceIdType.MESH
        )
    pl.semaphore_wait(barrier, n + 1)

    across = 4 * z + 2 * (1 - y) + parity

    def spread(g, zz):
        slot = tok_buf.at[h, g, zz, y, parity]
        send(slot, slot, quad_ss.at[2], quad_rs.at[g, 2], across, other)
        send(slot, slot, quad_ss.at[0], quad_rs.at[g, 0], across, h)
        send(slot, slot, quad_ss.at[1], quad_rs.at[g, 1], e, other)
        send(slot, slot, twin_ss, twin_rs.at[g, h], sibling, h)

    for g in range(groups):
        loads[g].wait()
        mine = tok_buf.at[h, g, z, y, parity]
        for dz in reversed(range(1, columns)):
            send(mine, mine, line_ss, line_rs.at[g, dz], 4 * flip(z, dz) + 2 * y + parity, h)
        spread(g, z)

    for c in loads[groups:-3]:
        c.wait()
    eye = (
        lax.broadcasted_iota(jnp.int32, (tok, tok), 0)
        == lax.broadcasted_iota(jnp.int32, (tok, tok), 1)
    )
    top = ids_ref.shape[0]
    lane = lax.broadcasted_iota(jnp.int32, (tok, top), 1)

    def column(row):
        return jnp.sum(jnp.where(eye, jnp.broadcast_to(row, (tok, tok)), 0.0), axis=1, keepdims=True)

    ids = jnp.zeros((tok, top), jnp.float32)
    probs = jnp.zeros((tok, top), jnp.float32)
    for j in range(top):
        ids = jnp.where(lane == j, column(ids_ref[j:j + 1, :].astype(jnp.float32)), ids)
        probs = jnp.where(lane == j, column(probs_ref[j:j + 1, :]), probs)
    pad = column(pad_ref[...].astype(jnp.float32))
    shares = probs / jnp.sum(probs, axis=1, keepdims=True)
    for i in range(n):
        share = jnp.sum(jnp.where(ids == float(i), shares, 0.0), axis=1, keepdims=True)
        for g in range(groups):
            share_s[g, i // 2, i % 2] = jnp.broadcast_to(
                share[g * sub:(g + 1) * sub], (sub, share_s.shape[4])
            )

    def lines(g):
        for dz in range(1, columns):
            zz = flip(z, dz)
            arrived(tok_buf.at[h, g, zz, y, parity], line_rs.at[g, dz])
            spread(g, zz)

    def gathered(g):
        for k, ph, yy in ((0, h, 1 - y), (1, other, y), (2, other, 1 - y)):
            slots = tok_buf.at[ph, g, :, yy, parity]
            arrived(slots, quad_rs.at[g, k])
            send(slots, slots, twin_ss, twin_rs.at[g, ph], sibling, h)

    def twins(g):
        for ph in range(2):
            arrived(tok_buf.at[ph, g, :, :, 0], twin_rs.at[g, ph])

    def hidden_rows(g):
        at = pl.ds(g * rows, rows)

        def hidden_step(cols, size):
            near_x = tok_buf[0, g].reshape(rows, width)
            far_x = tok_buf[1, g].reshape(rows, width)
            gate = dot(near_x, wg[:width, cols]) + dot(far_x, wg[width:, cols])
            up = dot(near_x, wu[:width, cols]) + dot(far_x, wu[width:, cols])
            gate_v[at, cols] = gate
            up_v[at, cols] = up
            hid[at, cols] = (gate / (1.0 + jnp.exp(-gate)) * up).astype(jnp.bfloat16)

        tiles(hidden, hidden_step)

    def down(g, far):
        start = (other if far else h) * width

        def down_step(cols, size):
            at = pl.ds(pl.multiple_of(cols.start + start, size), size)
            part = dot(hid[pl.ds(g * rows, rows), :], wd[:, at])
            osend[g, far, :, :, :, cols] = part.reshape(chips, 2, sub, size).astype(jnp.bfloat16)

        tiles(width, down_step, 1024)

    def cross_parts(g):
        for d in outer + [0]:
            pm = flip(chip, d)
            send(osend.at[g, 1, pm], orecv.at[g, pm], part_ss, part_rs.at[g, d], e, other)

    def forward(g, first, last):
        for d in (outer + [0])[first:last]:
            pm = flip(chip, d)
            arrived(orecv.at[g, pm], part_rs.at[g, d])
            total = osend[g, 0, pm].astype(jnp.float32) + orecv[g, pm].astype(jnp.float32)
            ored[g, pm] = total.astype(jnp.bfloat16)
            home = xrecv.at[g, chip, parity]
            if d:
                for q in range(2):
                    send(ored.at[g, pm, q], home, out_ss.at[0], out_rs.at[g, d], 2 * pm + q, h)
            else:
                send(ored.at[g, pm, 1 - parity], home, out_ss.at[1], out_rs.at[g, d], sibling, h)
                xrecv[g, chip, parity] = ored[g, chip, parity]

    same = (
        lax.rem(lax.broadcasted_iota(jnp.int32, (sub, rows), 1), sub)
        == lax.broadcasted_iota(jnp.int32, (sub, rows), 0)
    ).astype(jnp.float32)
    apart = (
        lax.div(lax.broadcasted_iota(jnp.int32, (n, rows), 1), sub)
        != lax.broadcasted_iota(jnp.int32, (n, rows), 0)
    ).astype(jnp.float32)

    def share_of(g, pm):
        return share_s[g, pm][:, :, :1]

    def products(g):
        layer = jnp.zeros((sub, width), jnp.float32)
        for d in [0] + near:
            pm = flip(chip, d)
            share = share_of(g, pm)
            arrived(xrecv.at[g, pm] if d else xrecv.at[g, chip, 1 - parity], out_rs.at[g, d])
            value = jnp.where(share > 0.0, xrecv[g, pm].astype(jnp.float32), 0.0)
            xs[g, pm] = value.astype(jnp.bfloat16)
            layer = layer + jnp.sum(share * value, axis=0)
        x_all = xs[g].reshape(rows, width)
        gram = dot_t(x_all, x_all).reshape(n, sub, rows) * same[None]
        gram_s[g, h] = jnp.sum(gram, axis=1)
        send(gram_s.at[g, h], gram_s.at[g, h], gram_ss, gram_rs.at[g], e, other)
        return layer

    def mix(g):
        arrived(gram_s.at[g, other], gram_rs.at[g])
        whole = (gram_s[g, 0] + gram_s[g, 1]) * (apart * (orth_weight / math.sqrt(full)))
        x_all = xs[g].reshape(rows, width)
        coeffs = (whole[:, None, :] * same[None]).reshape(rows, rows)
        high = coeffs.astype(jnp.bfloat16)
        low = (coeffs - high.astype(jnp.float32)).astype(jnp.bfloat16)
        mixed = (dot(high, x_all) + dot(low, x_all)).reshape(chips, 2, sub, width)
        upstream = up_ref[g].astype(jnp.float32)
        real = pad[g * sub:(g + 1) * sub]
        for i in range(chips):
            gsend[g, i] = (
                real[None] * (share_of(g, i) * upstream[None] + mixed[i])
            ).astype(jnp.bfloat16)
        slot = grows.at[h, g, chip, parity]
        send(gsend.at[g, chip, 1 - parity], slot, grad_ss.at[1], grad_rs.at[g, 0], sibling, h)
        send(gsend.at[g, chip, parity], slot, relay_ss, relay_rs.at[g], e, other)
        for d in near:
            pm = flip(chip, d)
            for q in range(2):
                send(gsend.at[g, pm, q], slot, grad_ss.at[0], grad_rs.at[g, d], 2 * pm + q, h)
        grows[h, g, chip, parity] = gsend[g, chip, parity]

    def relay(g, first, last):
        for d in range(first, last):
            slot = grows.at[h, g, flip(chip, d)] if d else grows.at[h, g, chip, 1 - parity]
            arrived(slot, grad_rs.at[g, d])
            send(slot, slot, relay_ss, relay_rs.at[g], e, other)

    def act(g, dh):
        ph = lax.rem(h + dh, 2)
        at = pl.ds(g * rows, rows)
        if dh:
            arrived(grows.at[other, g], relay_rs.at[g])

        def act_step(cols, size):
            depth = pl.ds(pl.multiple_of(ph * width, width), width)
            act = dot_t(grows[ph, g].reshape(rows, width), wd[cols, depth])
            if dh:
                act = act + act_v[at, cols]
                gate = gate_v[at, cols]
                sigma = 1.0 / (1.0 + jnp.exp(-gate))
                gg[at, cols] = (
                    act * up_v[at, cols] * sigma * (1.0 + gate * (1.0 - sigma))
                ).astype(jnp.bfloat16)
                gu[at, cols] = (act * gate * sigma).astype(jnp.bfloat16)
            else:
                act_v[at, cols] = act

        tiles(hidden, act_step)

    def back(g, far, piece, pieces):
        size = width // pieces
        start = (other if far else h) * width + piece * size
        rows_at = pl.ds(g * rows, rows)
        at = pl.ds(pl.multiple_of(start, size), size)
        part = dot_t(gg[rows_at, :], wg[at, :]) + dot_t(gu[rows_at, :], wu[at, :])
        part = part.astype(jnp.bfloat16).reshape(columns, 2, 2, sub, size)
        for q in range(2):
            psend[g, far, q, :, :, :, piece * size:(piece + 1) * size] = part[:, :, q]
        if piece == pieces - 1:
            send(
                psend.at[g, far, 1 - parity], prec.at[g, far],
                pair_ss, pair_rs.at[g, far], sibling, h,
            )

    def pairs(g):
        arrived(prec.at[g, 1], pair_rs.at[g, 1])
        for dz in reversed(range(columns)):
            zz = flip(z, dz)
            fsend[g, zz] = (
                psend[g, 1, parity, zz].astype(jnp.float32) + prec[g, 1, zz].astype(jnp.float32)
            ).astype(jnp.bfloat16)
            send(fsend.at[g, zz], frecv.at[g, zz], fpart_ss, fpart_rs.at[g, dz], e, other)

    def finish(g):
        arrived(prec.at[g, 0], pair_rs.at[g, 0])
        for dz in reversed(range(columns)):
            zz = flip(z, dz)
            total = psend[g, 0, parity, zz].astype(jnp.float32) + prec[g, 0, zz].astype(jnp.float32)
            arrived(frecv.at[g, zz], fpart_rs.at[g, dz])
            rsend[g, zz] = (total + frecv[g, zz].astype(jnp.float32)).astype(jnp.bfloat16)
            for dy in (1, 0):
                yy = flip(y, dy)
                if dz or dy:
                    send(
                        rsend.at[g, zz, yy], fin.at[g, chip],
                        fin_ss, fin_rs.at[g], 4 * zz + 2 * yy + parity, h,
                    )
                else:
                    fin[g, chip] = rsend[g, z, y]

    def collect(g):
        arrived(fin.at[g, pl.ds(0, chips - 1)], fin_rs.at[g])
        return jnp.sum(fin[g].astype(jnp.float32), axis=0)

    lines(0)
    lines(1)
    gathered(0)
    twins(0)
    for c in loads[-3:-1]:
        c.wait()
    hidden_rows(0)
    loads[-1].wait()
    down(0, 1)
    cross_parts(0)
    gathered(1)
    down(0, 0)
    twins(1)
    hidden_rows(1)
    forward(0, 0, chips // 4)
    down(1, 1)
    cross_parts(1)
    forward(0, chips // 4, chips)
    down(1, 0)
    forward(1, 0, 5 * chips // 8)
    layer_a = products(0)
    forward(1, 5 * chips // 8, chips)
    mix(0)
    layer_b = products(1)
    relay(0, 0, chips // 4)
    mix(1)
    layer_ref[...] = jnp.concatenate([layer_a, layer_b], axis=0).astype(jnp.bfloat16)
    relay(0, chips // 4, chips)
    act(0, 0)
    relay(1, 0, chips // 2)
    act(0, 1)
    relay(1, chips // 2, 5 * chips // 8)
    back(0, 1, 0, 2)
    relay(1, 5 * chips // 8, 6 * chips // 8)
    back(0, 1, 1, 2)
    relay(1, 6 * chips // 8, 7 * chips // 8)
    back(0, 0, 0, 2)
    relay(1, 7 * chips // 8, chips)
    back(0, 0, 1, 2)
    pairs(0)
    act(1, 0)
    act(1, 1)
    back(1, 1, 0, 1)
    back(1, 0, 0, 1)
    pairs(1)
    finish(0)
    finish(1)
    total_a = collect(0)
    total_b = collect(1)
    gtok_ref[...] = jnp.concatenate([total_a, total_b], axis=0).astype(jnp.bfloat16)
    drained(tok_buf.at[0, :, pl.ds(0, columns - 1), 0, 0], line_ss)
    for k in range(3):
        drained(tok_buf.at[0, :, :, 0, 0], quad_ss.at[k])
    drained(tok_buf.at[0], twin_ss)
    drained(osend.at[:, 1], part_ss)
    drained(ored.at[:, pl.ds(0, chips - 1)], out_ss.at[0])
    drained(ored.at[:, 0, 0], out_ss.at[1])
    drained(gram_s.at[:, 0], gram_ss)
    drained(gsend.at[:, pl.ds(0, chips - 1)], grad_ss.at[0])
    drained(gsend.at[:, 0, 0], grad_ss.at[1])
    drained(grows.at[0], relay_ss)
    drained(psend.at[:, :, 0], pair_ss)
    drained(fsend, fpart_ss)
    drained(fin.at[:, pl.ds(0, chips - 1)], fin_ss)


def fused(tokens, upstream, expert_ids, gate_probs, pad_mask, gate_weight, up_weight, down_weight):
    n, groups = lax.axis_size("expert"), 2
    tok, width = tokens.shape
    hidden = gate_weight.shape[2]
    sub, full, chips = tok // groups, 2 * width, n // 2
    columns, every = chips // 2, n * tok
    top = expert_ids.shape[1]
    low, wide = jnp.bfloat16, jnp.float32
    vmem, dma = pltpu.VMEM, pltpu.SemaphoreType.DMA
    local = pl.BlockSpec(memory_space=pltpu.VMEM)
    remain = pl.BlockSpec(memory_space=pl.ANY)
    outs = pl.pallas_call(
        functools.partial(fused_kernel, n, groups),
        out_shape=[vmem((tok, width), low)] * 2,
        in_specs=[remain] * 8,
        out_specs=[local] * 2,
        scratch_shapes=[
            vmem((groups, sub, width), low),
            vmem((top, tok), jnp.int32),
            vmem((top, tok), wide),
            vmem((1, tok), jnp.int32),
            vmem((2, groups, columns, 2, 2, sub, width), low),
            vmem((full, hidden), low),
            vmem((full, hidden), low),
            vmem((hidden, full), low),
            vmem((every, hidden), wide),
            vmem((every, hidden), wide),
            vmem((every, hidden), wide),
            vmem((every, hidden), low),
            vmem((every, hidden), low),
            vmem((every, hidden), low),
            vmem((groups, 2, chips, 2, sub, width), low),
            vmem((groups, chips, 2, sub, width), low),
            vmem((groups, chips, 2, sub, width), low),
            vmem((groups, chips, 2, sub, width), low),
            vmem((groups, chips, 2, sub, width), low),
            vmem((groups, 2, n, n * sub), wide),
            vmem((groups, chips, 2, sub, 128), wide),
            vmem((groups, chips, 2, sub, width), low),
            vmem((2, groups, chips, 2, sub, width), low),
            vmem((groups, 2, 2, columns, 2, sub, width), low),
            vmem((groups, 2, columns, 2, sub, width), low),
            vmem((groups, columns, 2, sub, width), low),
            vmem((groups, columns, 2, sub, width), low),
            vmem((groups, columns, 2, sub, width), low),
            vmem((groups, chips, sub, width), low),
            dma((2 * groups + 6,)),
            dma(()),
            dma((3,)),
            dma(()),
            dma((groups, columns)),
            dma((groups, 3)),
            dma((groups, 2)),
            dma(()),
            dma((groups, chips)),
            dma((2,)),
            dma((groups, chips)),
            dma(()),
            dma((groups,)),
            dma((2,)),
            dma((groups, chips)),
            dma(()),
            dma((groups,)),
            dma(()),
            dma((groups, 2)),
            dma(()),
            dma((groups, columns)),
            dma(()),
            dma((groups,)),
        ],
        compiler_params=pltpu.CompilerParams(
            collective_id=0, has_side_effects=True, vmem_limit_bytes=56 * 1024 * 1024
        ),
        name="experts",
    )(
        tokens, upstream, expert_ids.T, gate_probs.T, pad_mask.reshape(1, tok),
        gate_weight, up_weight, down_weight,
    )
    result = [jax.ShapeDtypeStruct((tok, width), low)] * 2
    return pl.pallas_call(
        copy_kernel, out_shape=result, in_specs=[local] * 2, out_specs=[local] * 2, name="results"
    )(*[pltpu.with_memory_space_constraint(out, pltpu.VMEM) for out in outs])


def shards(tokens, upstream, expert_ids, gate_probs, pad_mask, gate_weight, up_weight, down_weight):
    tok_count, top_count = expert_ids.shape
    experts = lax.axis_size("expert")
    capacity = min(tok_count, 2 * tok_count * top_count // experts)
    paired = experts > 3 and experts & (experts - 1) == 0 and lax.axis_size("half") == 2
    if capacity == tok_count and tok_count % 16 == 0 and paired:
        return fused(
            tokens, upstream, expert_ids, gate_probs, pad_mask, gate_weight, up_weight, down_weight
        )
    slots_total = experts * capacity
    full_width = tokens.shape[1] * lax.axis_size("half")
    slot_dest = assign_slots(expert_ids, experts, capacity)
    place_items = placement_matrix(slot_dest, slots_total)
    place_tokens = jnp.sum(place_items.reshape(slots_total, tok_count, top_count), axis=2)
    weight_gate = gate_weight[0]
    weight_up = up_weight[0]
    weight_down = down_weight[0]
    rows_in = to_experts(place_tokens, tokens)
    gate_val = jnp.dot(rows_in, weight_gate, preferred_element_type=jnp.float32)
    up_val = jnp.dot(rows_in, weight_up, preferred_element_type=jnp.float32)
    hidden_act = (jax.nn.silu(gate_val) * up_val).astype(jnp.bfloat16)
    partial_value = jnp.dot(hidden_act, weight_down, preferred_element_type=jnp.float32)
    out_home = to_homes(partial_value)
    outputs = jnp.take(out_home, slot_dest, axis=0).reshape(tok_count, top_count, -1)
    out_float = outputs.astype(jnp.float32)
    shares = gate_probs / jnp.sum(gate_probs, axis=1, keepdims=True)
    layer_out = jnp.sum(shares[:, :, None] * out_float, axis=1).astype(jnp.bfloat16)
    gram_part = jnp.einsum("tjd,tkd->tjk", out_float, out_float) / math.sqrt(full_width)
    gram = lax.psum(gram_part, "half")
    off_diag = 1.0 - jnp.eye(top_count, dtype=jnp.float32)
    coeffs = orth_weight * gram * off_diag
    grad_out = pad_mask.astype(jnp.float32)[:, None, None] * (
        shares[:, :, None] * upstream.astype(jnp.float32)[:, None, :]
        + jnp.einsum("tjk,tkd->tjd", coeffs, out_float)
    )
    grad_items = grad_out.astype(jnp.bfloat16).reshape(tok_count * top_count, -1)
    grad_rows = to_experts(place_items, grad_items)
    grad_act = jnp.einsum("rd,hd->rh", grad_rows, weight_down, preferred_element_type=jnp.float32)
    sigma = jax.nn.sigmoid(gate_val)
    grad_gate = (grad_act * up_val * sigma * (1.0 + gate_val * (1.0 - sigma))).astype(jnp.bfloat16)
    grad_up = (grad_act * gate_val * sigma).astype(jnp.bfloat16)
    grad_partial = jnp.einsum(
        "rh,dh->rd", grad_gate, weight_gate, preferred_element_type=jnp.float32
    )
    grad_partial = grad_partial + jnp.einsum(
        "rh,dh->rd", grad_up, weight_up, preferred_element_type=jnp.float32
    )
    grad_home = to_homes(grad_partial)
    grad_pairs = jnp.take(grad_home, slot_dest, axis=0).reshape(tok_count, top_count, -1)
    grad_tokens = jnp.sum(grad_pairs.astype(jnp.float32), axis=1).astype(jnp.bfloat16)
    return (layer_out, grad_tokens)


def solution(mesh):
    in_specs = (
        P("expert", "half"),
        P("expert", "half"),
        P("expert", None),
        P("expert", None),
        P("expert"),
        P("expert", None, "half"),
        P("expert", None, "half"),
        P("expert", "half", None),
    )
    out_specs = (P("expert", "half"), P("expert", "half"))
    return jax.shard_map(shards, mesh=mesh, in_specs=in_specs, out_specs=out_specs, check_vma=False)
```

```python
import functools
import math

import jax
import jax.numpy as jnp
from jax import lax
from jax.experimental import pallas as pl
from jax.experimental.pallas import tpu as pltpu
from jax.sharding import PartitionSpec as P

orth_weight = 0.25


def assign_slots(expert_ids, experts, capacity):
    tok_count, top_count = expert_ids.shape
    flat_ids = expert_ids.reshape(tok_count * top_count)
    onehot = (flat_ids[:, None] == jnp.arange(experts, dtype=jnp.int32)[None, :]).astype(jnp.int32)
    before = jnp.cumsum(onehot, axis=0) - onehot
    slot_index = jnp.sum(before * onehot, axis=1)
    return flat_ids * capacity + slot_index


def placement_matrix(slot_dest, slots_total):
    row_index = jnp.arange(slots_total, dtype=jnp.int32)
    return (row_index[:, None] == slot_dest[None, :]).astype(jnp.bfloat16)


def to_experts(place, items):
    whole = lax.all_gather(items, "half", axis=1, tiled=True)
    buckets = jnp.dot(place, whole, preferred_element_type=jnp.float32).astype(jnp.bfloat16)
    return lax.all_to_all(buckets, "expert", split_axis=0, concat_axis=0, tiled=True)


def to_homes(partial_value):
    summed = lax.psum_scatter(
        partial_value.astype(jnp.bfloat16), "half", scatter_dimension=1, tiled=True
    )
    return lax.all_to_all(summed, "expert", split_axis=0, concat_axis=0, tiled=True)


def block_of(width, most):
    return next((b for b in (1024, 512, 384, 256, 128) if b <= most and width % b == 0), width)


def tiles(width, body, most=256):
    size = block_of(width, most)

    def step(j, carry):
        body(pl.ds(pl.multiple_of(j * size, size), size), size)
        return carry

    lax.fori_loop(0, width // size, step, 0)


def dot(a, b):
    return jnp.dot(a, b, preferred_element_type=jnp.float32)


def dot_t(a, b):
    return lax.dot_general(a, b, (((1,), (1,)), ((), ())), preferred_element_type=jnp.float32)


def copy_kernel(a_ref, b_ref, a_out, b_out):
    a_out[...] = a_ref[...]
    b_out[...] = b_ref[...]


def fused_kernel(
    n, groups,
    tok_hbm, up_hbm, ids_hbm, probs_hbm, pad_hbm, wg_hbm, wu_hbm, wd_hbm,
    layer_ref, gtok_ref,
    up_ref, ids_ref, probs_ref, pad_ref,
    tok_buf, wg, wu, wd, gate_v, up_v, act_v, hid, gg, gu,
    wg_t, wu_t, wd_t,
    osend, orecv, ored, xrecv, xs, gram_s, share_s, gsend, grows, psend, prec,
    lsend, lrecv, lsum, lfin, rsend, rrecv, rsum, rfin,
    w_sem, line_ss, quad_ss, twin_ss, line_rs, quad_rs, twin_rs, part_ss, part_rs, out_ss, out_rs,
    gram_ss, gram_rs, grad_ss, grad_rs, relay_ss, relay_rs, pair_ss, pair_rs, lpart_ss, lpart_rs, rpart_ss, rpart_rs, fin_ss, fin_rs,
):
    e = lax.axis_index("expert")
    h = lax.axis_index("half")
    sub, width = tok_buf.shape[5:]
    hidden = wg.shape[1]
    tok = groups * sub
    rows = n * sub
    chips = n // 2
    columns = chips // 2
    parity = lax.rem(e, 2)
    chip = lax.div(e, 2)
    y = lax.rem(chip, 2)
    z = lax.div(chip, 2)
    sibling = e + 1 - 2 * parity
    other = 1 - h
    full = 2 * width
    half_width = width // 2
    block = columns // 2
    own_block = lax.div(z, block)

    def blocks(far):
        return pl.ds((1 - own_block if far else own_block) * block, block)

    def remote(src, dst, ssem, rsem, pe, ph):
        return pltpu.make_async_remote_copy(
            src_ref=src, dst_ref=dst, send_sem=ssem, recv_sem=rsem,
            device_id=(pe, ph), device_id_type=pl.DeviceIdType.MESH,
        )

    def send(*args):
        remote(*args).start()

    def flip(a, d):
        bit = 1
        out = a
        while bit <= d:
            if d & bit:
                out = out + bit * (1 - 2 * lax.rem(lax.div(a, bit), 2))
            bit *= 2
        return out

    def arrived(slot, rsem):
        remote(slot, slot, line_ss, rsem, sibling, h).wait_recv()

    def drained(sent, ssem):
        remote(sent, sent, ssem, twin_rs.at[0, 0], sibling, h).wait_send()

    moves = [(tok_hbm.at[pl.ds(g * sub, sub)], tok_buf.at[h, g, z, y, parity]) for g in range(groups)]
    moves += [(ids_hbm, ids_ref), (probs_hbm, probs_ref), (pad_hbm, pad_ref)]
    moves += [(up_hbm.at[pl.ds(g * sub, sub)], up_ref.at[g]) for g in range(groups)]
    moves += [(wg_hbm.at[0], wg), (wu_hbm.at[0], wu), (wd_hbm.at[0], wd)]
    loads = [pltpu.make_async_copy(src, dst, w_sem.at[i]) for i, (src, dst) in enumerate(moves)]
    for c in loads:
        c.start()

    near = list(range(1, chips))
    outer = near[::-1]

    barrier = pltpu.get_barrier_semaphore()
    for d in reversed(range(1, n)):
        pl.semaphore_signal(
            barrier, inc=1, device_id=(flip(e, d), h), device_id_type=pl.DeviceIdType.MESH
        )
    for pe in (e, 4 * z + 2 * (1 - y) + parity):
        pl.semaphore_signal(
            barrier, inc=1, device_id=(pe, other), device_id_type=pl.DeviceIdType.MESH
        )
    pl.semaphore_wait(barrier, n + 1)

    across = 4 * z + 2 * (1 - y) + parity

    def spread(g, dz):
        slot = tok_buf.at[h, g, flip(z, dz), y, parity]
        k = dz // block
        send(slot, slot, quad_ss.at[2], quad_rs.at[g, 2, k], across, other)
        send(slot, slot, quad_ss.at[0], quad_rs.at[g, 0, k], across, h)
        send(slot, slot, quad_ss.at[1], quad_rs.at[g, 1, k], e, other)
        send(slot, slot, twin_ss, twin_rs.at[g, h], sibling, h)

    for g in range(groups):
        loads[g].wait()
        mine = tok_buf.at[h, g, z, y, parity]
        for dz in reversed(range(1, columns)):
            send(mine, mine, line_ss, line_rs.at[g, dz], 4 * flip(z, dz) + 2 * y + parity, h)
        spread(g, 0)

    for c in loads[groups:-3]:
        c.wait()
    eye = (
        lax.broadcasted_iota(jnp.int32, (tok, tok), 0)
        == lax.broadcasted_iota(jnp.int32, (tok, tok), 1)
    )
    top = ids_ref.shape[0]
    lane = lax.broadcasted_iota(jnp.int32, (tok, top), 1)

    def column(row):
        return jnp.sum(jnp.where(eye, jnp.broadcast_to(row, (tok, tok)), 0.0), axis=1, keepdims=True)

    ids = jnp.zeros((tok, top), jnp.float32)
    probs = jnp.zeros((tok, top), jnp.float32)
    for j in range(top):
        ids = jnp.where(lane == j, column(ids_ref[j:j + 1, :].astype(jnp.float32)), ids)
        probs = jnp.where(lane == j, column(probs_ref[j:j + 1, :]), probs)
    pad = column(pad_ref[...].astype(jnp.float32))
    shares = probs / jnp.sum(probs, axis=1, keepdims=True)
    for i in range(n):
        share = jnp.sum(jnp.where(ids == float(i), shares, 0.0), axis=1, keepdims=True)
        for g in range(groups):
            share_s[g, i // 2, i % 2] = jnp.broadcast_to(
                share[g * sub:(g + 1) * sub], (sub, share_s.shape[4])
            )

    def lines(g):
        for dz in range(1, columns):
            zz = flip(z, dz)
            arrived(tok_buf.at[h, g, zz, y, parity], line_rs.at[g, dz])
            spread(g, dz)

    def gathered(g):
        for far in range(2):
            for k, ph, yy in ((0, h, 1 - y), (1, other, y), (2, other, 1 - y)):
                slots = tok_buf.at[ph, g, blocks(far), yy, parity]
                arrived(slots, quad_rs.at[g, k, far])
                send(slots, slots, twin_ss, twin_rs.at[g, ph], sibling, h)

    def twins(g):
        for ph in range(2):
            arrived(tok_buf.at[ph, g, :, :, 0], twin_rs.at[g, ph])

    def hidden_rows(g, first, last):
        at = pl.ds(g * rows, rows)
        size = block_of(hidden, 256)

        def hidden_step(cols):
            near_x = tok_buf[0, g].reshape(rows, width)
            far_x = tok_buf[1, g].reshape(rows, width)
            gate = dot(near_x, wg[:width, cols]) + dot(far_x, wg[width:, cols])
            up = dot(near_x, wu[:width, cols]) + dot(far_x, wu[width:, cols])
            gate_v[at, cols] = gate
            up_v[at, cols] = up
            hid[at, cols] = (gate / (1.0 + jnp.exp(-gate)) * up).astype(jnp.bfloat16)

        count = hidden // size
        for i in range(first * count // 3, last * count // 3):
            hidden_step(slice(i * size, (i + 1) * size))

    def down(g, far):
        start = (other if far else h) * width

        def down_step(cols, size):
            at = pl.ds(pl.multiple_of(cols.start + start, size), size)
            part = dot(hid[pl.ds(g * rows, rows), :], wd[:, at])
            osend[g, far, :, :, :, cols] = part.reshape(chips, 2, sub, size).astype(jnp.bfloat16)

        tiles(width, down_step, 1024)

    def cross_parts(g):
        for d in outer + [0]:
            pm = flip(chip, d)
            send(osend.at[g, 1, pm], orecv.at[g, pm], part_ss, part_rs.at[g, d], e, other)

    def forward(g, first, last):
        for d in (outer + [0])[first:last]:
            pm = flip(chip, d)
            arrived(orecv.at[g, pm], part_rs.at[g, d])
            total = osend[g, 0, pm].astype(jnp.float32) + orecv[g, pm].astype(jnp.float32)
            ored[g, pm] = total.astype(jnp.bfloat16)
            home = xrecv.at[g, chip, parity]
            if d:
                for q in range(2):
                    send(ored.at[g, pm, q], home, out_ss.at[0], out_rs.at[g, d], 2 * pm + q, h)
            else:
                send(ored.at[g, pm, 1 - parity], home, out_ss.at[1], out_rs.at[g, d], sibling, h)
                xrecv[g, chip, parity] = ored[g, chip, parity]

    same = (
        lax.rem(lax.broadcasted_iota(jnp.int32, (sub, rows), 1), sub)
        == lax.broadcasted_iota(jnp.int32, (sub, rows), 0)
    ).astype(jnp.float32)
    apart = (
        lax.div(lax.broadcasted_iota(jnp.int32, (n, rows), 1), sub)
        != lax.broadcasted_iota(jnp.int32, (n, rows), 0)
    ).astype(jnp.float32)

    def share_of(g, pm):
        return share_s[g, pm][:, :, :1]

    def products(g):
        layer = jnp.zeros((sub, width), jnp.float32)
        for d in [0] + near:
            pm = flip(chip, d)
            share = share_of(g, pm)
            arrived(xrecv.at[g, pm] if d else xrecv.at[g, chip, 1 - parity], out_rs.at[g, d])
            value = jnp.where(share > 0.0, xrecv[g, pm].astype(jnp.float32), 0.0)
            xs[g, pm] = value.astype(jnp.bfloat16)
            layer = layer + jnp.sum(share * value, axis=0)
        x_all = xs[g].reshape(rows, width)
        gram = dot_t(x_all, x_all).reshape(n, sub, rows) * same[None]
        gram_s[g, h] = jnp.sum(gram, axis=1)
        send(gram_s.at[g, h], gram_s.at[g, h], gram_ss, gram_rs.at[g], e, other)
        return layer

    def mix(g):
        arrived(gram_s.at[g, other], gram_rs.at[g])
        whole = (gram_s[g, 0] + gram_s[g, 1]) * (apart * (orth_weight / math.sqrt(full)))
        x_all = xs[g].reshape(rows, width)
        coeffs = (whole[:, None, :] * same[None]).reshape(rows, rows)
        high = coeffs.astype(jnp.bfloat16)
        low = (coeffs - high.astype(jnp.float32)).astype(jnp.bfloat16)
        mixed = (dot(high, x_all) + dot(low, x_all)).reshape(chips, 2, sub, width)
        upstream = up_ref[g].astype(jnp.float32)
        real = pad[g * sub:(g + 1) * sub]
        for i in range(chips):
            gsend[g, i] = (
                real[None] * (share_of(g, i) * upstream[None] + mixed[i])
            ).astype(jnp.bfloat16)
        slot = grows.at[h, g, chip, parity]
        send(gsend.at[g, chip, 1 - parity], slot, grad_ss.at[1], grad_rs.at[g, 0], sibling, h)
        send(gsend.at[g, chip, parity], slot, relay_ss, relay_rs.at[g], e, other)
        for d in near:
            pm = flip(chip, d)
            for q in range(2):
                send(gsend.at[g, pm, q], slot, grad_ss.at[0], grad_rs.at[g, d], 2 * pm + q, h)
        grows[h, g, chip, parity] = gsend[g, chip, parity]

    def relay(g, first, last):
        for d in range(first, last):
            slot = grows.at[h, g, flip(chip, d)] if d else grows.at[h, g, chip, 1 - parity]
            arrived(slot, grad_rs.at[g, d])
            send(slot, slot, relay_ss, relay_rs.at[g], e, other)

    def act(g, dh):
        ph = lax.rem(h + dh, 2)
        at = pl.ds(g * rows, rows)
        if dh:
            arrived(grows.at[other, g], relay_rs.at[g])

        def act_step(cols, size):
            depth = pl.ds(pl.multiple_of(ph * width, width), width)
            act = dot(grows[ph, g].reshape(rows, width), wd_t[depth, cols])
            if dh:
                act = act + act_v[at, cols]
                gate = gate_v[at, cols]
                sigma = 1.0 / (1.0 + jnp.exp(-gate))
                gg[at, cols] = (
                    act * up_v[at, cols] * sigma * (1.0 + gate * (1.0 - sigma))
                ).astype(jnp.bfloat16)
                gu[at, cols] = (act * gate * sigma).astype(jnp.bfloat16)
            else:
                act_v[at, cols] = act

        tiles(hidden, act_step, 384)

    def turn(first, last):
        for i in range(first, last):
            at = slice((i // 3) * half_width, (i // 3 + 1) * half_width)
            if i % 3 == 0:
                wd_t[at, :] = wd[:, at].T
            elif i % 3 == 1:
                wg_t[:, at] = wg[at, :].T
            else:
                wu_t[:, at] = wu[at, :].T

    def back(g, far):
        rows_at = pl.ds(g * rows, rows)
        at = pl.ds(pl.multiple_of((other if far else h) * width, width), width)
        part = dot(gg[rows_at, :], wg_t[:, at]) + dot(gu[rows_at, :], wu_t[:, at])
        part = part.astype(jnp.bfloat16).reshape(columns, 2, 2, sub, width)
        for q in range(2):
            psend[g, far, q] = part[:, :, q]
        send(
            psend.at[g, far, 1 - parity], prec.at[g, far],
            pair_ss, pair_rs.at[g, far], sibling, h,
        )

    left, right = slice(0, half_width), slice(half_width, width)

    def pairs(g):
        arrived(prec.at[g, 1], pair_rs.at[g, 1])
        for dz in reversed(range(columns)):
            zz = flip(z, dz)
            lsend[g, zz] = (
                psend[g, 1, parity, zz, :, :, left].astype(jnp.float32)
                + prec[g, 1, zz, :, :, left].astype(jnp.float32)
            ).astype(jnp.bfloat16)
            send(lsend.at[g, zz], lrecv.at[g, zz], lpart_ss, lpart_rs.at[g, dz], e, other)
        for far in (1, 0):
            if not far:
                arrived(prec.at[g, 0], pair_rs.at[g, 0])
            for k in (1, 0):
                zs = blocks(k)
                rsend[g, far, zs] = (
                    psend[g, far, parity, zs, 1 - y, :, right].astype(jnp.float32)
                    + prec[g, far, zs, 1 - y, :, right].astype(jnp.float32)
                ).astype(jnp.bfloat16)
                send(
                    rsend.at[g, far, zs], rrecv.at[g, far, zs],
                    rpart_ss, rpart_rs.at[g, far, k], across, h,
                )

    def finish_left(g, dz):
        zz = flip(z, dz)
        total = (
            psend[g, 0, parity, zz, :, :, left].astype(jnp.float32)
            + prec[g, 0, zz, :, :, left].astype(jnp.float32)
        )
        arrived(lrecv.at[g, zz], lpart_rs.at[g, dz])
        lsum[g, zz] = (total + lrecv[g, zz].astype(jnp.float32)).astype(jnp.bfloat16)
        for dy in (1, 0):
            yy = flip(y, dy)
            if dz or dy:
                send(
                    lsum.at[g, zz, yy], lfin.at[g, chip],
                    fin_ss.at[0], fin_rs.at[g, 0], 4 * zz + 2 * yy + parity, h,
                )
            else:
                lfin[g, chip] = lsum[g, z, y]

    def finish_right(g, far, k):
        zs = blocks(k)
        total = (
            psend[g, far, parity, zs, y, :, right].astype(jnp.float32)
            + prec[g, far, zs, y, :, right].astype(jnp.float32)
        )
        arrived(rrecv.at[g, far, zs], rpart_rs.at[g, far, k])
        rsum[g, far, zs] = (total + rrecv[g, far, zs].astype(jnp.float32)).astype(jnp.bfloat16)
        for dz in reversed(range(k * block, (k + 1) * block)):
            zz = flip(z, dz)
            if dz or far:
                send(
                    rsum.at[g, far, zz], rfin.at[g, columns * h + z],
                    fin_ss.at[1], fin_rs.at[g, 1], 4 * zz + 2 * y + parity, other if far else h,
                )
            else:
                rfin[g, columns * h + z] = rsum[g, far, z]

    def finish(g):
        for k in (1, 0):
            for far in (1, 0):
                for dz in reversed(range((2 * k + far) * block // 2, (2 * k + far + 1) * block // 2)):
                    finish_left(g, dz)
                finish_right(g, far, k)

    def collect(g):
        arrived(lfin.at[g, pl.ds(0, chips - 1)], fin_rs.at[g, 0])
        arrived(rfin.at[g, pl.ds(0, chips - 1)], fin_rs.at[g, 1])
        return [jnp.sum(fin[g].astype(jnp.float32), axis=0) for fin in (lfin, rfin)]

    lines(0)
    lines(1)
    gathered(0)
    twins(0)
    for c in loads[-3:-1]:
        c.wait()
    hidden_rows(0, 0, 3)
    loads[-1].wait()
    down(0, 1)
    cross_parts(0)
    gathered(1)
    down(0, 0)
    twins(1)
    hidden_rows(1, 0, 2)
    forward(0, 0, chips // 8)
    hidden_rows(1, 2, 3)
    forward(0, chips // 8, 3 * chips // 8)
    down(1, 1)
    cross_parts(1)
    turn(0, 1)
    forward(0, 3 * chips // 8, chips // 2)
    turn(1, 2)
    forward(0, chips // 2, 5 * chips // 8)
    turn(2, 3)
    forward(0, 5 * chips // 8, 3 * chips // 4)
    turn(3, 4)
    forward(0, 3 * chips // 4, 7 * chips // 8)
    turn(4, 5)
    forward(0, 7 * chips // 8, chips)
    down(1, 0)
    forward(1, 0, chips // 8)
    turn(5, 6)
    forward(1, chips // 8, chips // 4)
    turn(6, 7)
    forward(1, chips // 4, 3 * chips // 8)
    turn(7, 8)
    forward(1, 3 * chips // 8, chips // 2)
    turn(8, 9)
    forward(1, chips // 2, 5 * chips // 8)
    turn(9, 10)
    layer_a = products(0)
    forward(1, 5 * chips // 8, chips)
    turn(10, 12)
    mix(0)
    layer_b = products(1)
    relay(0, 0, 3 * chips // 8)
    mix(1)
    layer_ref[...] = jnp.concatenate([layer_a, layer_b], axis=0).astype(jnp.bfloat16)
    relay(0, 3 * chips // 8, chips)
    act(0, 0)
    relay(1, 0, 5 * chips // 8)
    act(0, 1)
    relay(1, 5 * chips // 8, 6 * chips // 8)
    back(0, 1)
    relay(1, 6 * chips // 8, 7 * chips // 8)
    back(0, 0)
    relay(1, 7 * chips // 8, chips)
    act(1, 0)
    pairs(0)
    act(1, 1)
    back(1, 1)
    back(1, 0)
    finish(0)
    pairs(1)
    finish(1)
    total_a = collect(0)
    total_b = collect(1)
    for k, at in enumerate((left, right)):
        gtok_ref[:, at] = jnp.concatenate([total_a[k], total_b[k]], axis=0).astype(jnp.bfloat16)
    drained(tok_buf.at[0, :, pl.ds(0, columns - 1), 0, 0], line_ss)
    for k in range(3):
        drained(tok_buf.at[0, :, :, 0, 0], quad_ss.at[k])
    drained(tok_buf.at[0], twin_ss)
    drained(osend.at[:, 1], part_ss)
    drained(ored.at[:, pl.ds(0, chips - 1)], out_ss.at[0])
    drained(ored.at[:, 0, 0], out_ss.at[1])
    drained(gram_s.at[:, 0], gram_ss)
    drained(gsend.at[:, pl.ds(0, chips - 1)], grad_ss.at[0])
    drained(gsend.at[:, 0, 0], grad_ss.at[1])
    drained(grows.at[0], relay_ss)
    drained(psend.at[:, :, 0], pair_ss)
    drained(lsend, lpart_ss)
    drained(rsend, rpart_ss)
    drained(lfin.at[:, pl.ds(0, chips - 1)], fin_ss.at[0])
    drained(rfin.at[:, pl.ds(0, chips - 1)], fin_ss.at[1])


def fused(tokens, upstream, expert_ids, gate_probs, pad_mask, gate_weight, up_weight, down_weight):
    n, groups = lax.axis_size("expert"), 2
    tok, width = tokens.shape
    hidden = gate_weight.shape[2]
    sub, full, chips = tok // groups, 2 * width, n // 2
    columns, every = chips // 2, n * tok
    top = expert_ids.shape[1]
    low, wide = jnp.bfloat16, jnp.float32
    vmem, dma = pltpu.VMEM, pltpu.SemaphoreType.DMA
    local = pl.BlockSpec(memory_space=pltpu.VMEM)
    remain = pl.BlockSpec(memory_space=pl.ANY)
    outs = pl.pallas_call(
        functools.partial(fused_kernel, n, groups),
        out_shape=[vmem((tok, width), low)] * 2,
        in_specs=[remain] * 8,
        out_specs=[local] * 2,
        scratch_shapes=[
            vmem((groups, sub, width), low),
            vmem((top, tok), jnp.int32),
            vmem((top, tok), wide),
            vmem((1, tok), jnp.int32),
            vmem((2, groups, columns, 2, 2, sub, width), low),
            vmem((full, hidden), low),
            vmem((full, hidden), low),
            vmem((hidden, full), low),
            vmem((every, hidden), wide),
            vmem((every, hidden), wide),
            vmem((every, hidden), wide),
            vmem((every, hidden), low),
            vmem((every, hidden), low),
            vmem((every, hidden), low),
            vmem((hidden, full), low),
            vmem((hidden, full), low),
            vmem((full, hidden), low),
            vmem((groups, 2, chips, 2, sub, width), low),
            vmem((groups, chips, 2, sub, width), low),
            vmem((groups, chips, 2, sub, width), low),
            vmem((groups, chips, 2, sub, width), low),
            vmem((groups, chips, 2, sub, width), low),
            vmem((groups, 2, n, n * sub), wide),
            vmem((groups, chips, 2, sub, 128), wide),
            vmem((groups, chips, 2, sub, width), low),
            vmem((2, groups, chips, 2, sub, width), low),
            vmem((groups, 2, 2, columns, 2, sub, width), low),
            vmem((groups, 2, columns, 2, sub, width), low),
            vmem((groups, columns, 2, sub, width // 2), low),
            vmem((groups, columns, 2, sub, width // 2), low),
            vmem((groups, columns, 2, sub, width // 2), low),
            vmem((groups, chips, sub, width // 2), low),
            vmem((groups, 2, columns, sub, width // 2), low),
            vmem((groups, 2, columns, sub, width // 2), low),
            vmem((groups, 2, columns, sub, width // 2), low),
            vmem((groups, chips, sub, width // 2), low),
            dma((2 * groups + 6,)),
            dma(()),
            dma((3,)),
            dma(()),
            dma((groups, columns)),
            dma((groups, 3, 2)),
            dma((groups, 2)),
            dma(()),
            dma((groups, chips)),
            dma((2,)),
            dma((groups, chips)),
            dma(()),
            dma((groups,)),
            dma((2,)),
            dma((groups, chips)),
            dma(()),
            dma((groups,)),
            dma(()),
            dma((groups, 2)),
            dma(()),
            dma((groups, columns)),
            dma(()),
            dma((groups, 2, 2)),
            dma((2,)),
            dma((groups, 2)),
        ],
        compiler_params=pltpu.CompilerParams(
            collective_id=0, has_side_effects=True, vmem_limit_bytes=56 * 1024 * 1024
        ),
        name="experts",
    )(
        tokens, upstream, expert_ids.T, gate_probs.T, pad_mask.reshape(1, tok),
        gate_weight, up_weight, down_weight,
    )
    result = [jax.ShapeDtypeStruct((tok, width), low)] * 2
    return pl.pallas_call(
        copy_kernel, out_shape=result, in_specs=[local] * 2, out_specs=[local] * 2, name="results"
    )(*[pltpu.with_memory_space_constraint(out, pltpu.VMEM) for out in outs])


def shards(tokens, upstream, expert_ids, gate_probs, pad_mask, gate_weight, up_weight, down_weight):
    tok_count, top_count = expert_ids.shape
    experts = lax.axis_size("expert")
    capacity = min(tok_count, 2 * tok_count * top_count // experts)
    paired = experts > 15 and experts & (experts - 1) == 0 and lax.axis_size("half") == 2
    if capacity == tok_count and tok_count % 16 == 0 and paired:
        return fused(
            tokens, upstream, expert_ids, gate_probs, pad_mask, gate_weight, up_weight, down_weight
        )
    slots_total = experts * capacity
    full_width = tokens.shape[1] * lax.axis_size("half")
    slot_dest = assign_slots(expert_ids, experts, capacity)
    place_items = placement_matrix(slot_dest, slots_total)
    place_tokens = jnp.sum(place_items.reshape(slots_total, tok_count, top_count), axis=2)
    weight_gate = gate_weight[0]
    weight_up = up_weight[0]
    weight_down = down_weight[0]
    rows_in = to_experts(place_tokens, tokens)
    gate_val = jnp.dot(rows_in, weight_gate, preferred_element_type=jnp.float32)
    up_val = jnp.dot(rows_in, weight_up, preferred_element_type=jnp.float32)
    hidden_act = (jax.nn.silu(gate_val) * up_val).astype(jnp.bfloat16)
    partial_value = jnp.dot(hidden_act, weight_down, preferred_element_type=jnp.float32)
    out_home = to_homes(partial_value)
    outputs = jnp.take(out_home, slot_dest, axis=0).reshape(tok_count, top_count, -1)
    out_float = outputs.astype(jnp.float32)
    shares = gate_probs / jnp.sum(gate_probs, axis=1, keepdims=True)
    layer_out = jnp.sum(shares[:, :, None] * out_float, axis=1).astype(jnp.bfloat16)
    gram_part = jnp.einsum("tjd,tkd->tjk", out_float, out_float) / math.sqrt(full_width)
    gram = lax.psum(gram_part, "half")
    off_diag = 1.0 - jnp.eye(top_count, dtype=jnp.float32)
    coeffs = orth_weight * gram * off_diag
    grad_out = pad_mask.astype(jnp.float32)[:, None, None] * (
        shares[:, :, None] * upstream.astype(jnp.float32)[:, None, :]
        + jnp.einsum("tjk,tkd->tjd", coeffs, out_float)
    )
    grad_items = grad_out.astype(jnp.bfloat16).reshape(tok_count * top_count, -1)
    grad_rows = to_experts(place_items, grad_items)
    grad_act = jnp.einsum("rd,hd->rh", grad_rows, weight_down, preferred_element_type=jnp.float32)
    sigma = jax.nn.sigmoid(gate_val)
    grad_gate = (grad_act * up_val * sigma * (1.0 + gate_val * (1.0 - sigma))).astype(jnp.bfloat16)
    grad_up = (grad_act * gate_val * sigma).astype(jnp.bfloat16)
    grad_partial = jnp.einsum(
        "rh,dh->rd", grad_gate, weight_gate, preferred_element_type=jnp.float32
    )
    grad_partial = grad_partial + jnp.einsum(
        "rh,dh->rd", grad_up, weight_up, preferred_element_type=jnp.float32
    )
    grad_home = to_homes(grad_partial)
    grad_pairs = jnp.take(grad_home, slot_dest, axis=0).reshape(tok_count, top_count, -1)
    grad_tokens = jnp.sum(grad_pairs.astype(jnp.float32), axis=1).astype(jnp.bfloat16)
    return (layer_out, grad_tokens)


def solution(mesh):
    in_specs = (
        P("expert", "half"),
        P("expert", "half"),
        P("expert", None),
        P("expert", None),
        P("expert"),
        P("expert", None, "half"),
        P("expert", None, "half"),
        P("expert", "half", None),
    )
    out_specs = (P("expert", "half"), P("expert", "half"))
    return jax.shard_map(shards, mesh=mesh, in_specs=in_specs, out_specs=out_specs, check_vma=False)
```

```python
import functools
import math

import jax
import jax.numpy as jnp
from jax import lax
from jax.experimental import pallas as pl
from jax.experimental.pallas import tpu as pltpu
from jax.sharding import PartitionSpec as P

orth_weight = 0.25


def assign_slots(expert_ids, experts, capacity):
    tok_count, top_count = expert_ids.shape
    flat_ids = expert_ids.reshape(tok_count * top_count)
    onehot = (flat_ids[:, None] == jnp.arange(experts, dtype=jnp.int32)[None, :]).astype(jnp.int32)
    before = jnp.cumsum(onehot, axis=0) - onehot
    slot_index = jnp.sum(before * onehot, axis=1)
    return flat_ids * capacity + slot_index


def placement_matrix(slot_dest, slots_total):
    row_index = jnp.arange(slots_total, dtype=jnp.int32)
    return (row_index[:, None] == slot_dest[None, :]).astype(jnp.bfloat16)


def to_experts(place, items):
    whole = lax.all_gather(items, "half", axis=1, tiled=True)
    buckets = jnp.dot(place, whole, preferred_element_type=jnp.float32).astype(jnp.bfloat16)
    return lax.all_to_all(buckets, "expert", split_axis=0, concat_axis=0, tiled=True)


def to_homes(partial_value):
    summed = lax.psum_scatter(
        partial_value.astype(jnp.bfloat16), "half", scatter_dimension=1, tiled=True
    )
    return lax.all_to_all(summed, "expert", split_axis=0, concat_axis=0, tiled=True)


def block_of(width, most):
    return next((b for b in (1024, 512, 384, 256, 128) if b <= most and width % b == 0), width)


def tiles(width, body, most=256):
    size = block_of(width, most)

    def step(j, carry):
        body(pl.ds(pl.multiple_of(j * size, size), size), size)
        return carry

    lax.fori_loop(0, width // size, step, 0)


def dot(a, b):
    return jnp.dot(a, b, preferred_element_type=jnp.float32)


def dot_t(a, b):
    return lax.dot_general(a, b, (((1,), (1,)), ((), ())), preferred_element_type=jnp.float32)


def copy_kernel(a_ref, b_ref, a_out, b_out):
    a_out[...] = a_ref[...]
    b_out[...] = b_ref[...]


def fused_kernel(
    n, groups,
    tok_hbm, up_hbm, ids_hbm, probs_hbm, pad_hbm, wg_hbm, wu_hbm, wd_hbm,
    layer_ref, gtok_ref,
    up_ref, ids_ref, probs_ref, pad_ref,
    tok_buf, wg, wu, wd, gate_v, up_v, act_v, hid, gg, gu,
    wg_t, wu_t, wd_t,
    osend, orecv, ored, xrecv, xs, gram_s, share_s, gsend, grows, psend, prec,
    lsend, lrecv, lsum, lfin, rsend, rrecv, rsum, rfin,
    w_sem, line_ss, quad_ss, twin_ss, line_rs, quad_rs, twin_rs, part_ss, part_rs, out_ss, out_rs,
    gram_ss, gram_rs, grad_ss, grad_rs, relay_ss, relay_rs, pair_ss, pair_rs, lpart_ss, lpart_rs, rpart_ss, rpart_rs, fin_ss, fin_rs,
):
    e = lax.axis_index("expert")
    h = lax.axis_index("half")
    sub, width = tok_buf.shape[5:]
    hidden = wg.shape[1]
    tok = groups * sub
    rows = n * sub
    chips = n // 2
    columns = chips // 2
    parity = lax.rem(e, 2)
    chip = lax.div(e, 2)
    y = lax.rem(chip, 2)
    z = lax.div(chip, 2)
    sibling = e + 1 - 2 * parity
    other = 1 - h
    full = 2 * width
    half_width = width // 2
    block = columns // 2
    own_block = lax.div(z, block)

    def blocks(far):
        return pl.ds((1 - own_block if far else own_block) * block, block)

    def remote(src, dst, ssem, rsem, pe, ph):
        return pltpu.make_async_remote_copy(
            src_ref=src, dst_ref=dst, send_sem=ssem, recv_sem=rsem,
            device_id=(pe, ph), device_id_type=pl.DeviceIdType.MESH,
        )

    def send(*args):
        remote(*args).start()

    def flip(a, d):
        bit = 1
        out = a
        while bit <= d:
            if d & bit:
                out = out + bit * (1 - 2 * lax.rem(lax.div(a, bit), 2))
            bit *= 2
        return out

    def arrived(slot, rsem):
        remote(slot, slot, line_ss, rsem, sibling, h).wait_recv()

    def drained(sent, ssem):
        remote(sent, sent, ssem, twin_rs.at[0, 0], sibling, h).wait_send()

    moves = [(tok_hbm.at[pl.ds(g * sub, sub)], tok_buf.at[h, g, z, y, parity]) for g in range(groups)]
    moves += [(ids_hbm, ids_ref), (probs_hbm, probs_ref), (pad_hbm, pad_ref)]
    moves += [(up_hbm.at[pl.ds(g * sub, sub)], up_ref.at[g]) for g in range(groups)]
    moves += [(wg_hbm.at[0], wg), (wu_hbm.at[0], wu), (wd_hbm.at[0], wd)]
    loads = [pltpu.make_async_copy(src, dst, w_sem.at[i]) for i, (src, dst) in enumerate(moves)]
    for c in loads:
        c.start()

    near = list(range(1, chips))
    outer = near[::-1]

    barrier = pltpu.get_barrier_semaphore()
    for d in reversed(range(1, n)):
        pl.semaphore_signal(
            barrier, inc=1, device_id=(flip(e, d), h), device_id_type=pl.DeviceIdType.MESH
        )
    for pe in (e, 4 * z + 2 * (1 - y) + parity):
        pl.semaphore_signal(
            barrier, inc=1, device_id=(pe, other), device_id_type=pl.DeviceIdType.MESH
        )
    pl.semaphore_wait(barrier, n + 1)

    across = 4 * z + 2 * (1 - y) + parity

    def spread(g, dz):
        slot = tok_buf.at[h, g, flip(z, dz), y, parity]
        k = dz // block
        send(slot, slot, quad_ss.at[2], quad_rs.at[g, 2, k], across, other)
        send(slot, slot, quad_ss.at[0], quad_rs.at[g, 0, k], across, h)
        send(slot, slot, quad_ss.at[1], quad_rs.at[g, 1, k], e, other)
        send(slot, slot, twin_ss, twin_rs.at[g, h], sibling, h)

    for g in range(groups):
        loads[g].wait()
        mine = tok_buf.at[h, g, z, y, parity]
        for dz in reversed(range(1, columns)):
            send(mine, mine, line_ss, line_rs.at[g, dz], 4 * flip(z, dz) + 2 * y + parity, h)
        spread(g, 0)

    for c in loads[groups:-3]:
        c.wait()
    eye = (
        lax.broadcasted_iota(jnp.int32, (tok, tok), 0)
        == lax.broadcasted_iota(jnp.int32, (tok, tok), 1)
    )
    top = ids_ref.shape[0]
    lane = lax.broadcasted_iota(jnp.int32, (tok, top), 1)

    def column(row):
        return jnp.sum(jnp.where(eye, jnp.broadcast_to(row, (tok, tok)), 0.0), axis=1, keepdims=True)

    ids = jnp.zeros((tok, top), jnp.float32)
    probs = jnp.zeros((tok, top), jnp.float32)
    for j in range(top):
        ids = jnp.where(lane == j, column(ids_ref[j:j + 1, :].astype(jnp.float32)), ids)
        probs = jnp.where(lane == j, column(probs_ref[j:j + 1, :]), probs)
    pad = column(pad_ref[...].astype(jnp.float32))
    shares = probs / jnp.sum(probs, axis=1, keepdims=True)
    for i in range(n):
        share = jnp.sum(jnp.where(ids == float(i), shares, 0.0), axis=1, keepdims=True)
        for g in range(groups):
            share_s[g, i // 2, i % 2] = jnp.broadcast_to(
                share[g * sub:(g + 1) * sub], (sub, share_s.shape[4])
            )

    def lines(g):
        for dz in range(1, columns):
            zz = flip(z, dz)
            arrived(tok_buf.at[h, g, zz, y, parity], line_rs.at[g, dz])
            spread(g, dz)

    def gathered(g):
        for far in range(2):
            for k, ph, yy in ((0, h, 1 - y), (1, other, y), (2, other, 1 - y)):
                slots = tok_buf.at[ph, g, blocks(far), yy, parity]
                arrived(slots, quad_rs.at[g, k, far])
                send(slots, slots, twin_ss, twin_rs.at[g, ph], sibling, h)

    def twins(g, ph):
        arrived(tok_buf.at[ph, g, :, :, 0], twin_rs.at[g, ph])

    def column_tiles(size):
        return [slice(i, i + size) for i in range(0, hidden, size)]

    def own_rows(g):
        at = pl.ds(g * rows, rows)
        depth = pl.ds(pl.multiple_of(h * width, width), width)
        for cols in column_tiles(block_of(hidden, 256)):
            x = tok_buf[h, g].reshape(rows, width)
            gate_v[at, cols] = dot(x, wg[depth, cols])
            up_v[at, cols] = dot(x, wu[depth, cols])

    def hidden_rows(g, first, last):
        at = pl.ds(g * rows, rows)
        depth = pl.ds(pl.multiple_of(other * width, width), width)
        every = column_tiles(block_of(hidden, 256))
        for cols in every[first * len(every) // 3:last * len(every) // 3]:
            x = tok_buf[other, g].reshape(rows, width)
            gate = gate_v[at, cols] + dot(x, wg[depth, cols])
            up = up_v[at, cols] + dot(x, wu[depth, cols])
            gate_v[at, cols] = gate
            up_v[at, cols] = up
            hid[at, cols] = (gate / (1.0 + jnp.exp(-gate)) * up).astype(jnp.bfloat16)

    def down(g, far):
        start = (other if far else h) * width

        def down_step(cols, size):
            at = pl.ds(pl.multiple_of(cols.start + start, size), size)
            part = dot(hid[pl.ds(g * rows, rows), :], wd[:, at])
            osend[g, far, :, :, :, cols] = part.reshape(chips, 2, sub, size).astype(jnp.bfloat16)

        tiles(width, down_step, 1024)

    def cross_parts(g):
        for d in outer + [0]:
            pm = flip(chip, d)
            send(osend.at[g, 1, pm], orecv.at[g, pm], part_ss, part_rs.at[g, d], e, other)

    def forward(g, first, last):
        for d in (outer + [0])[first:last]:
            pm = flip(chip, d)
            arrived(orecv.at[g, pm], part_rs.at[g, d])
            total = osend[g, 0, pm].astype(jnp.float32) + orecv[g, pm].astype(jnp.float32)
            ored[g, pm] = total.astype(jnp.bfloat16)
            home = xrecv.at[g, chip, parity]
            if d:
                for q in range(2):
                    send(ored.at[g, pm, q], home, out_ss.at[0], out_rs.at[g, d], 2 * pm + q, h)
            else:
                send(ored.at[g, pm, 1 - parity], home, out_ss.at[1], out_rs.at[g, d], sibling, h)
                xrecv[g, chip, parity] = ored[g, chip, parity]

    same = (
        lax.rem(lax.broadcasted_iota(jnp.int32, (sub, rows), 1), sub)
        == lax.broadcasted_iota(jnp.int32, (sub, rows), 0)
    ).astype(jnp.float32)
    apart = (
        lax.div(lax.broadcasted_iota(jnp.int32, (n, rows), 1), sub)
        != lax.broadcasted_iota(jnp.int32, (n, rows), 0)
    ).astype(jnp.float32)

    def share_of(g, pm):
        return share_s[g, pm][:, :, :1]

    def products(g):
        layer = jnp.zeros((sub, width), jnp.float32)
        for d in [0] + near:
            pm = flip(chip, d)
            share = share_of(g, pm)
            arrived(xrecv.at[g, pm] if d else xrecv.at[g, chip, 1 - parity], out_rs.at[g, d])
            value = jnp.where(share > 0.0, xrecv[g, pm].astype(jnp.float32), 0.0)
            xs[g, pm] = value.astype(jnp.bfloat16)
            layer = layer + jnp.sum(share * value, axis=0)
        x_all = xs[g].reshape(rows, width)
        gram = dot_t(x_all, x_all).reshape(n, sub, rows) * same[None]
        gram_s[g, h] = jnp.sum(gram, axis=1)
        send(gram_s.at[g, h], gram_s.at[g, h], gram_ss, gram_rs.at[g], e, other)
        return layer

    def mix(g):
        arrived(gram_s.at[g, other], gram_rs.at[g])
        whole = (gram_s[g, 0] + gram_s[g, 1]) * (apart * (orth_weight / math.sqrt(full)))
        x_all = xs[g].reshape(rows, width)
        coeffs = (whole[:, None, :] * same[None]).reshape(rows, rows)
        mixed = dot(coeffs.astype(jnp.bfloat16), x_all).reshape(chips, 2, sub, width)
        upstream = up_ref[g].astype(jnp.float32)
        real = pad[g * sub:(g + 1) * sub]
        for i in range(chips):
            gsend[g, i] = (
                real[None] * (share_of(g, i) * upstream[None] + mixed[i])
            ).astype(jnp.bfloat16)
        slot = grows.at[h, g, chip, parity]
        send(gsend.at[g, chip, 1 - parity], slot, grad_ss.at[1], grad_rs.at[g, 0], sibling, h)
        send(gsend.at[g, chip, parity], slot, relay_ss, relay_rs.at[g], e, other)
        for d in near:
            pm = flip(chip, d)
            for q in range(2):
                send(gsend.at[g, pm, q], slot, grad_ss.at[0], grad_rs.at[g, d], 2 * pm + q, h)
        grows[h, g, chip, parity] = gsend[g, chip, parity]

    def relay(g, first, last):
        for d in range(first, last):
            slot = grows.at[h, g, flip(chip, d)] if d else grows.at[h, g, chip, 1 - parity]
            arrived(slot, grad_rs.at[g, d])
            send(slot, slot, relay_ss, relay_rs.at[g], e, other)

    def act(g, dh):
        ph = lax.rem(h + dh, 2)
        at = pl.ds(g * rows, rows)
        if dh:
            arrived(grows.at[other, g], relay_rs.at[g])

        depth = pl.ds(pl.multiple_of(ph * width, width), width)
        for cols in column_tiles(block_of(hidden, 384)):
            part = dot(grows[ph, g].reshape(rows, width), wd_t[depth, cols])
            if dh:
                part = part + act_v[at, cols]
                gate = gate_v[at, cols]
                sigma = 1.0 / (1.0 + jnp.exp(-gate))
                gg[at, cols] = (
                    part * up_v[at, cols] * sigma * (1.0 + gate * (1.0 - sigma))
                ).astype(jnp.bfloat16)
                gu[at, cols] = (part * gate * sigma).astype(jnp.bfloat16)
            else:
                act_v[at, cols] = part

    def turn(first, last):
        for i in range(first, last):
            at = slice((i // 3) * half_width, (i // 3 + 1) * half_width)
            if i % 3 == 0:
                wd_t[at, :] = wd[:, at].T
            elif i % 3 == 1:
                wg_t[:, at] = wg[at, :].T
            else:
                wu_t[:, at] = wu[at, :].T

    def back(g, far):
        rows_at = pl.ds(g * rows, rows)
        at = pl.ds(pl.multiple_of((other if far else h) * width, width), width)
        part = dot(gg[rows_at, :], wg_t[:, at]) + dot(gu[rows_at, :], wu_t[:, at])
        part = part.astype(jnp.bfloat16).reshape(columns, 2, 2, sub, width)
        for q in range(2):
            psend[g, far, q] = part[:, :, q]
        send(
            psend.at[g, far, 1 - parity], prec.at[g, far],
            pair_ss, pair_rs.at[g, far], sibling, h,
        )

    left, right = slice(0, half_width), slice(half_width, width)

    def pairs(g):
        arrived(prec.at[g, 1], pair_rs.at[g, 1])
        for dz in reversed(range(columns)):
            zz = flip(z, dz)
            lsend[g, zz] = (
                psend[g, 1, parity, zz, :, :, left].astype(jnp.float32)
                + prec[g, 1, zz, :, :, left].astype(jnp.float32)
            ).astype(jnp.bfloat16)
            send(lsend.at[g, zz], lrecv.at[g, zz], lpart_ss, lpart_rs.at[g, dz], e, other)
        for far in (1, 0):
            if not far:
                arrived(prec.at[g, 0], pair_rs.at[g, 0])
            for k in (1, 0):
                zs = blocks(k)
                rsend[g, far, zs] = (
                    psend[g, far, parity, zs, 1 - y, :, right].astype(jnp.float32)
                    + prec[g, far, zs, 1 - y, :, right].astype(jnp.float32)
                ).astype(jnp.bfloat16)
                send(
                    rsend.at[g, far, zs], rrecv.at[g, far, zs],
                    rpart_ss, rpart_rs.at[g, far, k], across, h,
                )

    def finish_left(g, dz):
        zz = flip(z, dz)
        total = (
            psend[g, 0, parity, zz, :, :, left].astype(jnp.float32)
            + prec[g, 0, zz, :, :, left].astype(jnp.float32)
        )
        arrived(lrecv.at[g, zz], lpart_rs.at[g, dz])
        lsum[g, zz] = (total + lrecv[g, zz].astype(jnp.float32)).astype(jnp.bfloat16)
        for dy in (1, 0):
            yy = flip(y, dy)
            if dz or dy:
                send(
                    lsum.at[g, zz, yy], lfin.at[g, chip],
                    fin_ss.at[0], fin_rs.at[g, 0], 4 * zz + 2 * yy + parity, h,
                )
            else:
                lfin[g, chip] = lsum[g, z, y]

    def finish_right(g, far, k):
        zs = blocks(k)
        total = (
            psend[g, far, parity, zs, y, :, right].astype(jnp.float32)
            + prec[g, far, zs, y, :, right].astype(jnp.float32)
        )
        arrived(rrecv.at[g, far, zs], rpart_rs.at[g, far, k])
        rsum[g, far, zs] = (total + rrecv[g, far, zs].astype(jnp.float32)).astype(jnp.bfloat16)
        for dz in reversed(range(k * block, (k + 1) * block)):
            zz = flip(z, dz)
            if dz or far:
                send(
                    rsum.at[g, far, zz], rfin.at[g, columns * h + z],
                    fin_ss.at[1], fin_rs.at[g, 1], 4 * zz + 2 * y + parity, other if far else h,
                )
            else:
                rfin[g, columns * h + z] = rsum[g, far, z]

    def finish(g):
        for k in (1, 0):
            for far in (1, 0):
                for dz in reversed(range((2 * k + far) * block // 2, (2 * k + far + 1) * block // 2)):
                    finish_left(g, dz)
                finish_right(g, far, k)

    def collect(g):
        arrived(lfin.at[g, pl.ds(0, chips - 1)], fin_rs.at[g, 0])
        arrived(rfin.at[g, pl.ds(0, chips - 1)], fin_rs.at[g, 1])
        return [jnp.sum(fin[g].astype(jnp.float32), axis=0) for fin in (lfin, rfin)]

    lines(0)
    lines(1)
    gathered(0)
    twins(0, h)
    for c in loads[-3:-1]:
        c.wait()
    own_rows(0)
    twins(0, other)
    hidden_rows(0, 0, 3)
    loads[-1].wait()
    down(0, 1)
    cross_parts(0)
    gathered(1)
    down(0, 0)
    twins(1, h)
    own_rows(1)
    twins(1, other)
    hidden_rows(1, 0, 2)
    forward(0, 0, chips // 8)
    hidden_rows(1, 2, 3)
    forward(0, chips // 8, 3 * chips // 8)
    down(1, 1)
    cross_parts(1)
    turn(0, 1)
    forward(0, 3 * chips // 8, chips // 2)
    turn(1, 2)
    forward(0, chips // 2, 5 * chips // 8)
    turn(2, 3)
    forward(0, 5 * chips // 8, 3 * chips // 4)
    turn(3, 4)
    forward(0, 3 * chips // 4, 7 * chips // 8)
    turn(4, 5)
    forward(0, 7 * chips // 8, chips)
    down(1, 0)
    forward(1, 0, chips // 8)
    turn(5, 6)
    forward(1, chips // 8, chips // 4)
    turn(6, 7)
    forward(1, chips // 4, 3 * chips // 8)
    turn(7, 8)
    forward(1, 3 * chips // 8, chips // 2)
    turn(8, 9)
    layer_a = products(0)
    forward(1, chips // 2, chips)
    turn(9, 12)
    mix(0)
    layer_b = products(1)
    relay(0, 0, 3 * chips // 8)
    mix(1)
    layer_ref[...] = jnp.concatenate([layer_a, layer_b], axis=0).astype(jnp.bfloat16)
    relay(0, 3 * chips // 8, chips)
    relay(1, 0, 5 * chips // 8)
    act(0, 0)
    relay(1, 5 * chips // 8, 6 * chips // 8)
    act(0, 1)
    relay(1, 6 * chips // 8, chips)
    back(0, 1)
    back(0, 0)
    act(1, 0)
    pairs(0)
    act(1, 1)
    back(1, 1)
    back(1, 0)
    finish(0)
    pairs(1)
    finish(1)
    total_a = collect(0)
    total_b = collect(1)
    for k, at in enumerate((left, right)):
        gtok_ref[:, at] = jnp.concatenate([total_a[k], total_b[k]], axis=0).astype(jnp.bfloat16)
    drained(tok_buf.at[0, :, pl.ds(0, columns - 1), 0, 0], line_ss)
    for k in range(3):
        drained(tok_buf.at[0, :, :, 0, 0], quad_ss.at[k])
    drained(tok_buf.at[0], twin_ss)
    drained(osend.at[:, 1], part_ss)
    drained(ored.at[:, pl.ds(0, chips - 1)], out_ss.at[0])
    drained(ored.at[:, 0, 0], out_ss.at[1])
    drained(gram_s.at[:, 0], gram_ss)
    drained(gsend.at[:, pl.ds(0, chips - 1)], grad_ss.at[0])
    drained(gsend.at[:, 0, 0], grad_ss.at[1])
    drained(grows.at[0], relay_ss)
    drained(psend.at[:, :, 0], pair_ss)
    drained(lsend, lpart_ss)
    drained(rsend, rpart_ss)
    drained(lfin.at[:, pl.ds(0, chips - 1)], fin_ss.at[0])
    drained(rfin.at[:, pl.ds(0, chips - 1)], fin_ss.at[1])


def fused(tokens, upstream, expert_ids, gate_probs, pad_mask, gate_weight, up_weight, down_weight):
    n, groups = lax.axis_size("expert"), 2
    tok, width = tokens.shape
    hidden = gate_weight.shape[2]
    sub, full, chips = tok // groups, 2 * width, n // 2
    columns, every = chips // 2, n * tok
    top = expert_ids.shape[1]
    low, wide = jnp.bfloat16, jnp.float32
    vmem, dma = pltpu.VMEM, pltpu.SemaphoreType.DMA
    local = pl.BlockSpec(memory_space=pltpu.VMEM)
    remain = pl.BlockSpec(memory_space=pl.ANY)
    outs = pl.pallas_call(
        functools.partial(fused_kernel, n, groups),
        out_shape=[vmem((tok, width), low)] * 2,
        in_specs=[remain] * 8,
        out_specs=[local] * 2,
        scratch_shapes=[
            vmem((groups, sub, width), low),
            vmem((top, tok), jnp.int32),
            vmem((top, tok), wide),
            vmem((1, tok), jnp.int32),
            vmem((2, groups, columns, 2, 2, sub, width), low),
            vmem((full, hidden), low),
            vmem((full, hidden), low),
            vmem((hidden, full), low),
            vmem((every, hidden), wide),
            vmem((every, hidden), wide),
            vmem((every, hidden), wide),
            vmem((every, hidden), low),
            vmem((every, hidden), low),
            vmem((every, hidden), low),
            vmem((hidden, full), low),
            vmem((hidden, full), low),
            vmem((full, hidden), low),
            vmem((groups, 2, chips, 2, sub, width), low),
            vmem((groups, chips, 2, sub, width), low),
            vmem((groups, chips, 2, sub, width), low),
            vmem((groups, chips, 2, sub, width), low),
            vmem((groups, chips, 2, sub, width), low),
            vmem((groups, 2, n, n * sub), wide),
            vmem((groups, chips, 2, sub, 128), wide),
            vmem((groups, chips, 2, sub, width), low),
            vmem((2, groups, chips, 2, sub, width), low),
            vmem((groups, 2, 2, columns, 2, sub, width), low),
            vmem((groups, 2, columns, 2, sub, width), low),
            vmem((groups, columns, 2, sub, width // 2), low),
            vmem((groups, columns, 2, sub, width // 2), low),
            vmem((groups, columns, 2, sub, width // 2), low),
            vmem((groups, chips, sub, width // 2), low),
            vmem((groups, 2, columns, sub, width // 2), low),
            vmem((groups, 2, columns, sub, width // 2), low),
            vmem((groups, 2, columns, sub, width // 2), low),
            vmem((groups, chips, sub, width // 2), low),
            dma((2 * groups + 6,)),
            dma(()),
            dma((3,)),
            dma(()),
            dma((groups, columns)),
            dma((groups, 3, 2)),
            dma((groups, 2)),
            dma(()),
            dma((groups, chips)),
            dma((2,)),
            dma((groups, chips)),
            dma(()),
            dma((groups,)),
            dma((2,)),
            dma((groups, chips)),
            dma(()),
            dma((groups,)),
            dma(()),
            dma((groups, 2)),
            dma(()),
            dma((groups, columns)),
            dma(()),
            dma((groups, 2, 2)),
            dma((2,)),
            dma((groups, 2)),
        ],
        compiler_params=pltpu.CompilerParams(
            collective_id=0, has_side_effects=True, vmem_limit_bytes=56 * 1024 * 1024
        ),
        name="experts",
    )(
        tokens, upstream, expert_ids.T, gate_probs.T, pad_mask.reshape(1, tok),
        gate_weight, up_weight, down_weight,
    )
    result = [jax.ShapeDtypeStruct((tok, width), low)] * 2
    return pl.pallas_call(
        copy_kernel, out_shape=result, in_specs=[local] * 2, out_specs=[local] * 2, name="results"
    )(*[pltpu.with_memory_space_constraint(out, pltpu.VMEM) for out in outs])


def shards(tokens, upstream, expert_ids, gate_probs, pad_mask, gate_weight, up_weight, down_weight):
    tok_count, top_count = expert_ids.shape
    experts = lax.axis_size("expert")
    capacity = min(tok_count, 2 * tok_count * top_count // experts)
    paired = experts > 15 and experts & (experts - 1) == 0 and lax.axis_size("half") == 2
    if capacity == tok_count and tok_count % 16 == 0 and paired:
        return fused(
            tokens, upstream, expert_ids, gate_probs, pad_mask, gate_weight, up_weight, down_weight
        )
    slots_total = experts * capacity
    full_width = tokens.shape[1] * lax.axis_size("half")
    slot_dest = assign_slots(expert_ids, experts, capacity)
    place_items = placement_matrix(slot_dest, slots_total)
    place_tokens = jnp.sum(place_items.reshape(slots_total, tok_count, top_count), axis=2)
    weight_gate = gate_weight[0]
    weight_up = up_weight[0]
    weight_down = down_weight[0]
    rows_in = to_experts(place_tokens, tokens)
    gate_val = jnp.dot(rows_in, weight_gate, preferred_element_type=jnp.float32)
    up_val = jnp.dot(rows_in, weight_up, preferred_element_type=jnp.float32)
    hidden_act = (jax.nn.silu(gate_val) * up_val).astype(jnp.bfloat16)
    partial_value = jnp.dot(hidden_act, weight_down, preferred_element_type=jnp.float32)
    out_home = to_homes(partial_value)
    outputs = jnp.take(out_home, slot_dest, axis=0).reshape(tok_count, top_count, -1)
    out_float = outputs.astype(jnp.float32)
    shares = gate_probs / jnp.sum(gate_probs, axis=1, keepdims=True)
    layer_out = jnp.sum(shares[:, :, None] * out_float, axis=1).astype(jnp.bfloat16)
    gram_part = jnp.einsum("tjd,tkd->tjk", out_float, out_float) / math.sqrt(full_width)
    gram = lax.psum(gram_part, "half")
    off_diag = 1.0 - jnp.eye(top_count, dtype=jnp.float32)
    coeffs = orth_weight * gram * off_diag
    grad_out = pad_mask.astype(jnp.float32)[:, None, None] * (
        shares[:, :, None] * upstream.astype(jnp.float32)[:, None, :]
        + jnp.einsum("tjk,tkd->tjd", coeffs, out_float)
    )
    grad_items = grad_out.astype(jnp.bfloat16).reshape(tok_count * top_count, -1)
    grad_rows = to_experts(place_items, grad_items)
    grad_act = jnp.einsum("rd,hd->rh", grad_rows, weight_down, preferred_element_type=jnp.float32)
    sigma = jax.nn.sigmoid(gate_val)
    grad_gate = (grad_act * up_val * sigma * (1.0 + gate_val * (1.0 - sigma))).astype(jnp.bfloat16)
    grad_up = (grad_act * gate_val * sigma).astype(jnp.bfloat16)
    grad_partial = jnp.einsum(
        "rh,dh->rd", grad_gate, weight_gate, preferred_element_type=jnp.float32
    )
    grad_partial = grad_partial + jnp.einsum(
        "rh,dh->rd", grad_up, weight_up, preferred_element_type=jnp.float32
    )
    grad_home = to_homes(grad_partial)
    grad_pairs = jnp.take(grad_home, slot_dest, axis=0).reshape(tok_count, top_count, -1)
    grad_tokens = jnp.sum(grad_pairs.astype(jnp.float32), axis=1).astype(jnp.bfloat16)
    return (layer_out, grad_tokens)


def solution(mesh):
    in_specs = (
        P("expert", "half"),
        P("expert", "half"),
        P("expert", None),
        P("expert", None),
        P("expert"),
        P("expert", None, "half"),
        P("expert", None, "half"),
        P("expert", "half", None),
    )
    out_specs = (P("expert", "half"), P("expert", "half"))
    return jax.shard_map(shards, mesh=mesh, in_specs=in_specs, out_specs=out_specs, check_vma=False)
```

```python
import functools
import math

import jax
import jax.numpy as jnp
from jax import lax
from jax.experimental import pallas as pl
from jax.experimental.pallas import tpu as pltpu
from jax.sharding import PartitionSpec as P

orth_weight = 0.25


def assign_slots(expert_ids, experts, capacity):
    tok_count, top_count = expert_ids.shape
    flat_ids = expert_ids.reshape(tok_count * top_count)
    onehot = (flat_ids[:, None] == jnp.arange(experts, dtype=jnp.int32)[None, :]).astype(jnp.int32)
    before = jnp.cumsum(onehot, axis=0) - onehot
    slot_index = jnp.sum(before * onehot, axis=1)
    return flat_ids * capacity + slot_index


def placement_matrix(slot_dest, slots_total):
    row_index = jnp.arange(slots_total, dtype=jnp.int32)
    return (row_index[:, None] == slot_dest[None, :]).astype(jnp.bfloat16)


def to_experts(place, items):
    whole = lax.all_gather(items, "half", axis=1, tiled=True)
    buckets = jnp.dot(place, whole, preferred_element_type=jnp.float32).astype(jnp.bfloat16)
    return lax.all_to_all(buckets, "expert", split_axis=0, concat_axis=0, tiled=True)


def to_homes(partial_value):
    summed = lax.psum_scatter(
        partial_value.astype(jnp.bfloat16), "half", scatter_dimension=1, tiled=True
    )
    return lax.all_to_all(summed, "expert", split_axis=0, concat_axis=0, tiled=True)


def block_of(width, most):
    return next((b for b in (1024, 512, 384, 256, 128) if b <= most and width % b == 0), width)


def tiles(width, body, most=256):
    size = block_of(width, most)

    def step(j, carry):
        body(pl.ds(pl.multiple_of(j * size, size), size), size)
        return carry

    lax.fori_loop(0, width // size, step, 0)


def dot(a, b):
    return jnp.dot(a, b, preferred_element_type=jnp.float32)


def dot_t(a, b):
    return lax.dot_general(a, b, (((1,), (1,)), ((), ())), preferred_element_type=jnp.float32)


def copy_kernel(a_ref, b_ref, a_out, b_out):
    a_out[...] = a_ref[...]
    b_out[...] = b_ref[...]


def fused_kernel(
    n, groups,
    tok_hbm, up_hbm, ids_hbm, probs_hbm, pad_hbm, wg_hbm, wu_hbm, wd_hbm,
    layer_ref, gtok_ref,
    up_ref, ids_ref, probs_ref, pad_ref,
    tok_buf, wg, wu, wd, gate_v, up_v, act_v, hid, gg, gu,
    wg_t, wu_t, wd_t,
    osend, orecv, ored, xrecv, xs, gram_s, share_s, gsend, grows, psend, prec,
    lsend, lrecv, lsum, lfin, rsend, rrecv, rsum, rfin,
    w_sem, line_ss, quad_ss, twin_ss, line_rs, quad_rs, twin_rs, part_ss, part_rs, out_ss, out_rs,
    gram_ss, gram_rs, grad_ss, grad_rs, relay_ss, relay_rs, pair_ss, pair_rs, lpart_ss, lpart_rs, rpart_ss, rpart_rs, fin_ss, fin_rs,
):
    e = lax.axis_index("expert")
    h = lax.axis_index("half")
    sub, width = tok_buf.shape[5:]
    hidden = wg.shape[1]
    tok = groups * sub
    rows = n * sub
    chips = n // 2
    columns = chips // 2
    parity = lax.rem(e, 2)
    chip = lax.div(e, 2)
    y = lax.rem(chip, 2)
    z = lax.div(chip, 2)
    sibling = e + 1 - 2 * parity
    other = 1 - h
    full = 2 * width
    half_width = width // 2
    block = columns // 2
    own_block = lax.div(z, block)

    def blocks(far):
        return pl.ds((1 - own_block if far else own_block) * block, block)

    def remote(src, dst, ssem, rsem, pe, ph):
        return pltpu.make_async_remote_copy(
            src_ref=src, dst_ref=dst, send_sem=ssem, recv_sem=rsem,
            device_id=(pe, ph), device_id_type=pl.DeviceIdType.MESH,
        )

    def send(*args):
        remote(*args).start()

    def flip(a, d):
        bit = 1
        out = a
        while bit <= d:
            if d & bit:
                out = out + bit * (1 - 2 * lax.rem(lax.div(a, bit), 2))
            bit *= 2
        return out

    def arrived(slot, rsem):
        remote(slot, slot, line_ss, rsem, sibling, h).wait_recv()

    def drained(sent, ssem):
        remote(sent, sent, ssem, twin_rs.at[0, 0], sibling, h).wait_send()

    moves = [(tok_hbm.at[pl.ds(g * sub, sub)], tok_buf.at[h, g, z, y, parity]) for g in range(groups)]
    moves += [(ids_hbm, ids_ref), (probs_hbm, probs_ref), (pad_hbm, pad_ref)]
    moves += [(up_hbm.at[pl.ds(g * sub, sub)], up_ref.at[g]) for g in range(groups)]
    moves += [(wg_hbm.at[0], wg), (wu_hbm.at[0], wu), (wd_hbm.at[0], wd)]
    loads = [pltpu.make_async_copy(src, dst, w_sem.at[i]) for i, (src, dst) in enumerate(moves)]
    for c in loads:
        c.start()

    near = list(range(1, chips))
    outer = near[::-1]

    across = 4 * z + 2 * (1 - y) + parity
    barrier = pltpu.get_barrier_semaphore()
    partners = [(4 * flip(z, dz) + 2 * y + parity, h) for dz in reversed(range(1, columns))]
    partners += [(across, other), (across, h), (e, other), (sibling, h)]
    for partner in partners:
        pl.semaphore_signal(
            barrier, inc=1, device_id=partner, device_id_type=pl.DeviceIdType.MESH
        )
    pl.semaphore_wait(barrier, len(partners))

    def spread(g, dz):
        slot = tok_buf.at[h, g, flip(z, dz), y, parity]
        k = dz // block
        send(slot, slot, quad_ss.at[2], quad_rs.at[g, 2, k], across, other)
        send(slot, slot, quad_ss.at[0], quad_rs.at[g, 0, k], across, h)
        send(slot, slot, quad_ss.at[1], quad_rs.at[g, 1, k], e, other)
        send(slot, slot, twin_ss, twin_rs.at[g, h], sibling, h)

    for g in range(groups):
        loads[g].wait()
        mine = tok_buf.at[h, g, z, y, parity]
        for dz in reversed(range(1, columns)):
            send(mine, mine, line_ss, line_rs.at[g, dz], 4 * flip(z, dz) + 2 * y + parity, h)
        spread(g, 0)

    for c in loads[groups:-3]:
        c.wait()
    eye = (
        lax.broadcasted_iota(jnp.int32, (tok, tok), 0)
        == lax.broadcasted_iota(jnp.int32, (tok, tok), 1)
    )
    top = ids_ref.shape[0]
    lane = lax.broadcasted_iota(jnp.int32, (tok, top), 1)

    def column(row):
        return jnp.sum(jnp.where(eye, jnp.broadcast_to(row, (tok, tok)), 0.0), axis=1, keepdims=True)

    ids = jnp.zeros((tok, top), jnp.float32)
    probs = jnp.zeros((tok, top), jnp.float32)
    for j in range(top):
        ids = jnp.where(lane == j, column(ids_ref[j:j + 1, :].astype(jnp.float32)), ids)
        probs = jnp.where(lane == j, column(probs_ref[j:j + 1, :]), probs)
    pad = column(pad_ref[...].astype(jnp.float32))
    shares = probs / jnp.sum(probs, axis=1, keepdims=True)
    for i in range(n):
        share = jnp.sum(jnp.where(ids == float(i), shares, 0.0), axis=1, keepdims=True)
        for g in range(groups):
            share_s[g, i // 2, i % 2] = jnp.broadcast_to(
                share[g * sub:(g + 1) * sub], (sub, share_s.shape[4])
            )

    def lines(g):
        for dz in range(1, columns):
            zz = flip(z, dz)
            arrived(tok_buf.at[h, g, zz, y, parity], line_rs.at[g, dz])
            spread(g, dz)

    def gathered(g):
        for far in range(2):
            for k, ph, yy in ((0, h, 1 - y), (1, other, y), (2, other, 1 - y)):
                slots = tok_buf.at[ph, g, blocks(far), yy, parity]
                arrived(slots, quad_rs.at[g, k, far])
                send(slots, slots, twin_ss, twin_rs.at[g, ph], sibling, h)

    def twins(g, ph):
        arrived(tok_buf.at[ph, g, :, :, 0], twin_rs.at[g, ph])

    def column_tiles(size):
        return [slice(i, i + size) for i in range(0, hidden, size)]

    def own_rows(g):
        at = pl.ds(g * rows, rows)
        depth = pl.ds(pl.multiple_of(h * width, width), width)
        for cols in column_tiles(block_of(hidden, 256)):
            x = tok_buf[h, g].reshape(rows, width)
            gate_v[at, cols] = dot(x, wg[depth, cols])
            up_v[at, cols] = dot(x, wu[depth, cols])

    def hidden_rows(g, first, last):
        at = pl.ds(g * rows, rows)
        depth = pl.ds(pl.multiple_of(other * width, width), width)
        every = column_tiles(block_of(hidden, 256))
        for cols in every[first * len(every) // 3:last * len(every) // 3]:
            x = tok_buf[other, g].reshape(rows, width)
            gate = gate_v[at, cols] + dot(x, wg[depth, cols])
            up = up_v[at, cols] + dot(x, wu[depth, cols])
            gate_v[at, cols] = gate
            up_v[at, cols] = up
            hid[at, cols] = (gate / (1.0 + jnp.exp(-gate)) * up).astype(jnp.bfloat16)

    def down(g, far):
        start = (other if far else h) * width

        def down_step(cols, size):
            at = pl.ds(pl.multiple_of(cols.start + start, size), size)
            part = dot(hid[pl.ds(g * rows, rows), :], wd[:, at])
            osend[g, far, :, :, :, cols] = part.reshape(chips, 2, sub, size).astype(jnp.bfloat16)

        tiles(width, down_step, 1024)

    def cross_parts(g):
        for d in outer + [0]:
            pm = flip(chip, d)
            send(osend.at[g, 1, pm], orecv.at[g, pm], part_ss, part_rs.at[g, d], e, other)

    def forward(g, first, last):
        for d in (outer + [0])[first:last]:
            pm = flip(chip, d)
            arrived(orecv.at[g, pm], part_rs.at[g, d])
            total = osend[g, 0, pm].astype(jnp.float32) + orecv[g, pm].astype(jnp.float32)
            ored[g, pm] = total.astype(jnp.bfloat16)
            home = xrecv.at[g, chip, parity]
            if d:
                for q in range(2):
                    send(ored.at[g, pm, q], home, out_ss.at[0], out_rs.at[g, d], 2 * pm + q, h)
            else:
                send(ored.at[g, pm, 1 - parity], home, out_ss.at[1], out_rs.at[g, d], sibling, h)
                xrecv[g, chip, parity] = ored[g, chip, parity]

    same = (
        lax.rem(lax.broadcasted_iota(jnp.int32, (sub, rows), 1), sub)
        == lax.broadcasted_iota(jnp.int32, (sub, rows), 0)
    ).astype(jnp.float32)
    apart = (
        lax.div(lax.broadcasted_iota(jnp.int32, (n, rows), 1), sub)
        != lax.broadcasted_iota(jnp.int32, (n, rows), 0)
    ).astype(jnp.float32)

    def share_of(g, pm):
        return share_s[g, pm][:, :, :1]

    def products(g):
        layer = jnp.zeros((sub, width), jnp.float32)
        for d in [0] + near:
            pm = flip(chip, d)
            share = share_of(g, pm)
            arrived(xrecv.at[g, pm] if d else xrecv.at[g, chip, 1 - parity], out_rs.at[g, d])
            value = jnp.where(share > 0.0, xrecv[g, pm].astype(jnp.float32), 0.0)
            xs[g, pm] = value.astype(jnp.bfloat16)
            layer = layer + jnp.sum(share * value, axis=0)
        x_all = xs[g].reshape(rows, width)
        gram = dot_t(x_all, x_all).reshape(n, sub, rows) * same[None]
        gram_s[g, h] = jnp.sum(gram, axis=1)
        send(gram_s.at[g, h], gram_s.at[g, h], gram_ss, gram_rs.at[g], e, other)
        return layer

    def mix(g):
        arrived(gram_s.at[g, other], gram_rs.at[g])
        whole = (gram_s[g, 0] + gram_s[g, 1]) * (apart * (orth_weight / math.sqrt(full)))
        x_all = xs[g].reshape(rows, width)
        coeffs = (whole[:, None, :] * same[None]).reshape(rows, rows)
        mixed = dot(coeffs.astype(jnp.bfloat16), x_all).reshape(chips, 2, sub, width)
        upstream = up_ref[g].astype(jnp.float32)
        real = pad[g * sub:(g + 1) * sub]
        for i in range(chips):
            gsend[g, i] = (
                real[None] * (share_of(g, i) * upstream[None] + mixed[i])
            ).astype(jnp.bfloat16)
        slot = grows.at[h, g, chip, parity]
        send(gsend.at[g, chip, 1 - parity], slot, grad_ss.at[1], grad_rs.at[g, 0], sibling, h)
        send(gsend.at[g, chip, parity], slot, relay_ss, relay_rs.at[g], e, other)
        for d in near:
            pm = flip(chip, d)
            for q in range(2):
                send(gsend.at[g, pm, q], slot, grad_ss.at[0], grad_rs.at[g, d], 2 * pm + q, h)
        grows[h, g, chip, parity] = gsend[g, chip, parity]

    def relay(g, first, last):
        for d in range(first, last):
            slot = grows.at[h, g, flip(chip, d)] if d else grows.at[h, g, chip, 1 - parity]
            arrived(slot, grad_rs.at[g, d])
            send(slot, slot, relay_ss, relay_rs.at[g], e, other)

    def act(g, dh):
        ph = lax.rem(h + dh, 2)
        at = pl.ds(g * rows, rows)
        if dh:
            arrived(grows.at[other, g], relay_rs.at[g])

        depth = pl.ds(pl.multiple_of(ph * width, width), width)
        for cols in column_tiles(block_of(hidden, 384)):
            part = dot(grows[ph, g].reshape(rows, width), wd_t[depth, cols])
            if dh:
                part = part + act_v[at, cols]
                gate = gate_v[at, cols]
                sigma = 1.0 / (1.0 + jnp.exp(-gate))
                gg[at, cols] = (
                    part * up_v[at, cols] * sigma * (1.0 + gate * (1.0 - sigma))
                ).astype(jnp.bfloat16)
                gu[at, cols] = (part * gate * sigma).astype(jnp.bfloat16)
            else:
                act_v[at, cols] = part

    def turn(first, last):
        for i in range(first, last):
            at = slice((i // 3) * half_width, (i // 3 + 1) * half_width)
            if i % 3 == 0:
                wd_t[at, :] = wd[:, at].T
            elif i % 3 == 1:
                wg_t[:, at] = wg[at, :].T
            else:
                wu_t[:, at] = wu[at, :].T

    def back(g, far):
        rows_at = pl.ds(g * rows, rows)
        at = pl.ds(pl.multiple_of((other if far else h) * width, width), width)
        part = dot(gg[rows_at, :], wg_t[:, at]) + dot(gu[rows_at, :], wu_t[:, at])
        part = part.astype(jnp.bfloat16).reshape(columns, 2, 2, sub, width)
        for q in range(2):
            psend[g, far, q] = part[:, :, q]
        send(
            psend.at[g, far, 1 - parity], prec.at[g, far],
            pair_ss, pair_rs.at[g, far], sibling, h,
        )

    left, right = slice(0, half_width), slice(half_width, width)

    def pairs(g):
        arrived(prec.at[g, 1], pair_rs.at[g, 1])
        for dz in reversed(range(columns)):
            zz = flip(z, dz)
            lsend[g, zz] = (
                psend[g, 1, parity, zz, :, :, left].astype(jnp.float32)
                + prec[g, 1, zz, :, :, left].astype(jnp.float32)
            ).astype(jnp.bfloat16)
            send(lsend.at[g, zz], lrecv.at[g, zz], lpart_ss, lpart_rs.at[g, dz], e, other)
        for far in (1, 0):
            if not far:
                arrived(prec.at[g, 0], pair_rs.at[g, 0])
            for k in (1, 0):
                zs = blocks(k)
                rsend[g, far, zs] = (
                    psend[g, far, parity, zs, 1 - y, :, right].astype(jnp.float32)
                    + prec[g, far, zs, 1 - y, :, right].astype(jnp.float32)
                ).astype(jnp.bfloat16)
                send(
                    rsend.at[g, far, zs], rrecv.at[g, far, zs],
                    rpart_ss, rpart_rs.at[g, far, k], across, h,
                )

    def finish_left(g, dz):
        zz = flip(z, dz)
        total = (
            psend[g, 0, parity, zz, :, :, left].astype(jnp.float32)
            + prec[g, 0, zz, :, :, left].astype(jnp.float32)
        )
        arrived(lrecv.at[g, zz], lpart_rs.at[g, dz])
        lsum[g, zz] = (total + lrecv[g, zz].astype(jnp.float32)).astype(jnp.bfloat16)
        for dy in (1, 0):
            yy = flip(y, dy)
            if dz or dy:
                send(
                    lsum.at[g, zz, yy], lfin.at[g, chip],
                    fin_ss.at[0], fin_rs.at[g, 0], 4 * zz + 2 * yy + parity, h,
                )
            else:
                lfin[g, chip] = lsum[g, z, y]

    def finish_right(g, far, k):
        zs = blocks(k)
        total = (
            psend[g, far, parity, zs, y, :, right].astype(jnp.float32)
            + prec[g, far, zs, y, :, right].astype(jnp.float32)
        )
        arrived(rrecv.at[g, far, zs], rpart_rs.at[g, far, k])
        rsum[g, far, zs] = (total + rrecv[g, far, zs].astype(jnp.float32)).astype(jnp.bfloat16)
        for dz in reversed(range(k * block, (k + 1) * block)):
            zz = flip(z, dz)
            if dz or far:
                send(
                    rsum.at[g, far, zz], rfin.at[g, columns * h + z],
                    fin_ss.at[1], fin_rs.at[g, 1], 4 * zz + 2 * y + parity, other if far else h,
                )
            else:
                rfin[g, columns * h + z] = rsum[g, far, z]

    def finish(g):
        for k in (1, 0):
            for far in (1, 0):
                for dz in reversed(range((2 * k + far) * block // 2, (2 * k + far + 1) * block // 2)):
                    finish_left(g, dz)
                finish_right(g, far, k)

    def collect(g):
        arrived(lfin.at[g, pl.ds(0, chips - 1)], fin_rs.at[g, 0])
        arrived(rfin.at[g, pl.ds(0, chips - 1)], fin_rs.at[g, 1])
        return [jnp.sum(fin[g].astype(jnp.float32), axis=0) for fin in (lfin, rfin)]

    lines(0)
    lines(1)
    gathered(0)
    twins(0, h)
    for c in loads[-3:-1]:
        c.wait()
    own_rows(0)
    twins(0, other)
    hidden_rows(0, 0, 3)
    loads[-1].wait()
    down(0, 1)
    cross_parts(0)
    gathered(1)
    down(0, 0)
    twins(1, h)
    own_rows(1)
    twins(1, other)
    hidden_rows(1, 0, 2)
    forward(0, 0, chips // 8)
    hidden_rows(1, 2, 3)
    forward(0, chips // 8, 3 * chips // 8)
    down(1, 1)
    cross_parts(1)
    turn(0, 1)
    forward(0, 3 * chips // 8, chips // 2)
    turn(1, 2)
    forward(0, chips // 2, 5 * chips // 8)
    turn(2, 3)
    forward(0, 5 * chips // 8, 3 * chips // 4)
    turn(3, 4)
    forward(0, 3 * chips // 4, 7 * chips // 8)
    turn(4, 5)
    forward(0, 7 * chips // 8, chips)
    down(1, 0)
    forward(1, 0, chips // 8)
    turn(5, 6)
    forward(1, chips // 8, chips // 4)
    turn(6, 7)
    forward(1, chips // 4, 3 * chips // 8)
    turn(7, 8)
    forward(1, 3 * chips // 8, chips // 2)
    turn(8, 9)
    layer_a = products(0)
    forward(1, chips // 2, chips)
    mix(0)
    turn(9, 12)
    layer_b = products(1)
    relay(0, 0, 3 * chips // 8)
    mix(1)
    layer_ref[...] = jnp.concatenate([layer_a, layer_b], axis=0).astype(jnp.bfloat16)
    relay(0, 3 * chips // 8, chips)
    relay(1, 0, 5 * chips // 8)
    act(0, 0)
    relay(1, 5 * chips // 8, 6 * chips // 8)
    act(0, 1)
    relay(1, 6 * chips // 8, chips)
    back(0, 1)
    back(0, 0)
    act(1, 0)
    pairs(0)
    act(1, 1)
    back(1, 1)
    back(1, 0)
    finish(0)
    pairs(1)
    finish(1)
    total_a = collect(0)
    total_b = collect(1)
    for k, at in enumerate((left, right)):
        gtok_ref[:, at] = jnp.concatenate([total_a[k], total_b[k]], axis=0).astype(jnp.bfloat16)
    drained(tok_buf.at[0, :, pl.ds(0, columns - 1), 0, 0], line_ss)
    for k in range(3):
        drained(tok_buf.at[0, :, :, 0, 0], quad_ss.at[k])
    drained(tok_buf.at[0], twin_ss)
    drained(osend.at[:, 1], part_ss)
    drained(ored.at[:, pl.ds(0, chips - 1)], out_ss.at[0])
    drained(ored.at[:, 0, 0], out_ss.at[1])
    drained(gram_s.at[:, 0], gram_ss)
    drained(gsend.at[:, pl.ds(0, chips - 1)], grad_ss.at[0])
    drained(gsend.at[:, 0, 0], grad_ss.at[1])
    drained(grows.at[0], relay_ss)
    drained(psend.at[:, :, 0], pair_ss)
    drained(lsend, lpart_ss)
    drained(rsend, rpart_ss)
    drained(lfin.at[:, pl.ds(0, chips - 1)], fin_ss.at[0])
    drained(rfin.at[:, pl.ds(0, chips - 1)], fin_ss.at[1])


def fused(tokens, upstream, expert_ids, gate_probs, pad_mask, gate_weight, up_weight, down_weight):
    n, groups = lax.axis_size("expert"), 2
    tok, width = tokens.shape
    hidden = gate_weight.shape[2]
    sub, full, chips = tok // groups, 2 * width, n // 2
    columns, every = chips // 2, n * tok
    top = expert_ids.shape[1]
    low, wide = jnp.bfloat16, jnp.float32
    vmem, dma = pltpu.VMEM, pltpu.SemaphoreType.DMA
    local = pl.BlockSpec(memory_space=pltpu.VMEM)
    remain = pl.BlockSpec(memory_space=pl.ANY)
    outs = pl.pallas_call(
        functools.partial(fused_kernel, n, groups),
        out_shape=[vmem((tok, width), low)] * 2,
        in_specs=[remain] * 8,
        out_specs=[local] * 2,
        scratch_shapes=[
            vmem((groups, sub, width), low),
            vmem((top, tok), jnp.int32),
            vmem((top, tok), wide),
            vmem((1, tok), jnp.int32),
            vmem((2, groups, columns, 2, 2, sub, width), low),
            vmem((full, hidden), low),
            vmem((full, hidden), low),
            vmem((hidden, full), low),
            vmem((every, hidden), wide),
            vmem((every, hidden), wide),
            vmem((every, hidden), wide),
            vmem((every, hidden), low),
            vmem((every, hidden), low),
            vmem((every, hidden), low),
            vmem((hidden, full), low),
            vmem((hidden, full), low),
            vmem((full, hidden), low),
            vmem((groups, 2, chips, 2, sub, width), low),
            vmem((groups, chips, 2, sub, width), low),
            vmem((groups, chips, 2, sub, width), low),
            vmem((groups, chips, 2, sub, width), low),
            vmem((groups, chips, 2, sub, width), low),
            vmem((groups, 2, n, n * sub), wide),
            vmem((groups, chips, 2, sub, 128), wide),
            vmem((groups, chips, 2, sub, width), low),
            vmem((2, groups, chips, 2, sub, width), low),
            vmem((groups, 2, 2, columns, 2, sub, width), low),
            vmem((groups, 2, columns, 2, sub, width), low),
            vmem((groups, columns, 2, sub, width // 2), low),
            vmem((groups, columns, 2, sub, width // 2), low),
            vmem((groups, columns, 2, sub, width // 2), low),
            vmem((groups, chips, sub, width // 2), low),
            vmem((groups, 2, columns, sub, width // 2), low),
            vmem((groups, 2, columns, sub, width // 2), low),
            vmem((groups, 2, columns, sub, width // 2), low),
            vmem((groups, chips, sub, width // 2), low),
            dma((2 * groups + 6,)),
            dma(()),
            dma((3,)),
            dma(()),
            dma((groups, columns)),
            dma((groups, 3, 2)),
            dma((groups, 2)),
            dma(()),
            dma((groups, chips)),
            dma((2,)),
            dma((groups, chips)),
            dma(()),
            dma((groups,)),
            dma((2,)),
            dma((groups, chips)),
            dma(()),
            dma((groups,)),
            dma(()),
            dma((groups, 2)),
            dma(()),
            dma((groups, columns)),
            dma(()),
            dma((groups, 2, 2)),
            dma((2,)),
            dma((groups, 2)),
        ],
        compiler_params=pltpu.CompilerParams(
            collective_id=0, has_side_effects=True, vmem_limit_bytes=56 * 1024 * 1024
        ),
        name="experts",
    )(
        tokens, upstream, expert_ids.T, gate_probs.T, pad_mask.reshape(1, tok),
        gate_weight, up_weight, down_weight,
    )
    result = [jax.ShapeDtypeStruct((tok, width), low)] * 2
    return pl.pallas_call(
        copy_kernel, out_shape=result, in_specs=[local] * 2, out_specs=[local] * 2, name="results"
    )(*[pltpu.with_memory_space_constraint(out, pltpu.VMEM) for out in outs])


def shards(tokens, upstream, expert_ids, gate_probs, pad_mask, gate_weight, up_weight, down_weight):
    tok_count, top_count = expert_ids.shape
    experts = lax.axis_size("expert")
    capacity = min(tok_count, 2 * tok_count * top_count // experts)
    paired = experts > 15 and experts & (experts - 1) == 0 and lax.axis_size("half") == 2
    if capacity == tok_count and tok_count % 16 == 0 and paired:
        return fused(
            tokens, upstream, expert_ids, gate_probs, pad_mask, gate_weight, up_weight, down_weight
        )
    slots_total = experts * capacity
    full_width = tokens.shape[1] * lax.axis_size("half")
    slot_dest = assign_slots(expert_ids, experts, capacity)
    place_items = placement_matrix(slot_dest, slots_total)
    place_tokens = jnp.sum(place_items.reshape(slots_total, tok_count, top_count), axis=2)
    weight_gate = gate_weight[0]
    weight_up = up_weight[0]
    weight_down = down_weight[0]
    rows_in = to_experts(place_tokens, tokens)
    gate_val = jnp.dot(rows_in, weight_gate, preferred_element_type=jnp.float32)
    up_val = jnp.dot(rows_in, weight_up, preferred_element_type=jnp.float32)
    hidden_act = (jax.nn.silu(gate_val) * up_val).astype(jnp.bfloat16)
    partial_value = jnp.dot(hidden_act, weight_down, preferred_element_type=jnp.float32)
    out_home = to_homes(partial_value)
    outputs = jnp.take(out_home, slot_dest, axis=0).reshape(tok_count, top_count, -1)
    out_float = outputs.astype(jnp.float32)
    shares = gate_probs / jnp.sum(gate_probs, axis=1, keepdims=True)
    layer_out = jnp.sum(shares[:, :, None] * out_float, axis=1).astype(jnp.bfloat16)
    gram_part = jnp.einsum("tjd,tkd->tjk", out_float, out_float) / math.sqrt(full_width)
    gram = lax.psum(gram_part, "half")
    off_diag = 1.0 - jnp.eye(top_count, dtype=jnp.float32)
    coeffs = orth_weight * gram * off_diag
    grad_out = pad_mask.astype(jnp.float32)[:, None, None] * (
        shares[:, :, None] * upstream.astype(jnp.float32)[:, None, :]
        + jnp.einsum("tjk,tkd->tjd", coeffs, out_float)
    )
    grad_items = grad_out.astype(jnp.bfloat16).reshape(tok_count * top_count, -1)
    grad_rows = to_experts(place_items, grad_items)
    grad_act = jnp.einsum("rd,hd->rh", grad_rows, weight_down, preferred_element_type=jnp.float32)
    sigma = jax.nn.sigmoid(gate_val)
    grad_gate = (grad_act * up_val * sigma * (1.0 + gate_val * (1.0 - sigma))).astype(jnp.bfloat16)
    grad_up = (grad_act * gate_val * sigma).astype(jnp.bfloat16)
    grad_partial = jnp.einsum(
        "rh,dh->rd", grad_gate, weight_gate, preferred_element_type=jnp.float32
    )
    grad_partial = grad_partial + jnp.einsum(
        "rh,dh->rd", grad_up, weight_up, preferred_element_type=jnp.float32
    )
    grad_home = to_homes(grad_partial)
    grad_pairs = jnp.take(grad_home, slot_dest, axis=0).reshape(tok_count, top_count, -1)
    grad_tokens = jnp.sum(grad_pairs.astype(jnp.float32), axis=1).astype(jnp.bfloat16)
    return (layer_out, grad_tokens)


def solution(mesh):
    in_specs = (
        P("expert", "half"),
        P("expert", "half"),
        P("expert", None),
        P("expert", None),
        P("expert"),
        P("expert", None, "half"),
        P("expert", None, "half"),
        P("expert", "half", None),
    )
    out_specs = (P("expert", "half"), P("expert", "half"))
    return jax.shard_map(shards, mesh=mesh, in_specs=in_specs, out_specs=out_specs, check_vma=False)
```

```python
import functools
import math

import jax
import jax.numpy as jnp
from jax import lax
from jax.experimental import pallas as pl
from jax.experimental.pallas import tpu as pltpu
from jax.sharding import PartitionSpec as P

orth_weight = 0.25


def assign_slots(expert_ids, experts, capacity):
    tok_count, top_count = expert_ids.shape
    flat_ids = expert_ids.reshape(tok_count * top_count)
    onehot = (flat_ids[:, None] == jnp.arange(experts, dtype=jnp.int32)[None, :]).astype(jnp.int32)
    before = jnp.cumsum(onehot, axis=0) - onehot
    slot_index = jnp.sum(before * onehot, axis=1)
    return flat_ids * capacity + slot_index


def placement_matrix(slot_dest, slots_total):
    row_index = jnp.arange(slots_total, dtype=jnp.int32)
    return (row_index[:, None] == slot_dest[None, :]).astype(jnp.bfloat16)


def to_experts(place, items):
    whole = lax.all_gather(items, "half", axis=1, tiled=True)
    buckets = jnp.dot(place, whole, preferred_element_type=jnp.float32).astype(jnp.bfloat16)
    return lax.all_to_all(buckets, "expert", split_axis=0, concat_axis=0, tiled=True)


def to_homes(partial_value):
    summed = lax.psum_scatter(
        partial_value.astype(jnp.bfloat16), "half", scatter_dimension=1, tiled=True
    )
    return lax.all_to_all(summed, "expert", split_axis=0, concat_axis=0, tiled=True)


def block_of(width, most):
    return next((b for b in (1024, 512, 384, 256, 128) if b <= most and width % b == 0), width)


def tiles(width, body, most=256):
    size = block_of(width, most)

    def step(j, carry):
        body(pl.ds(pl.multiple_of(j * size, size), size), size)
        return carry

    lax.fori_loop(0, width // size, step, 0)


def dot(a, b):
    return jnp.dot(a, b, preferred_element_type=jnp.float32)


def dot_t(a, b):
    return lax.dot_general(a, b, (((1,), (1,)), ((), ())), preferred_element_type=jnp.float32)


def copy_kernel(a_ref, b_ref, a_out, b_out):
    a_out[...] = a_ref[...]
    b_out[...] = b_ref[...]


def fused_kernel(
    n, groups,
    tok_hbm, up_hbm, ids_hbm, probs_hbm, pad_hbm, wg_hbm, wu_hbm, wd_hbm,
    layer_ref, gtok_ref,
    up_ref, ids_ref, probs_ref, pad_ref,
    tok_buf, wg, wu, wd, gate_v, up_v, act_v, hid, gg, gu,
    wg_t, wu_t, wd_t,
    osend, orecv, ored, xrecv, xs, gram_s, share_s, layer_s, gsend, grows, psend, prec,
    lsend, lrecv, lsum, lfin, rsend, rrecv, rsum, rfin,
    w_sem, line_ss, quad_ss, twin_ss, line_rs, quad_rs, twin_rs, part_ss, part_rs, out_ss, out_rs,
    gram_ss, gram_rs, grad_ss, grad_rs, relay_ss, relay_rs, pair_ss, pair_rs, lpart_ss, rpart_ss, fin_ss,
):
    e = lax.axis_index("expert")
    h = lax.axis_index("half")
    sub, width = tok_buf.shape[5:]
    hidden = wg.shape[1]
    tok = groups * sub
    rows = n * sub
    chips = n // 2
    columns = chips // 2
    parity = lax.rem(e, 2)
    chip = lax.div(e, 2)
    y = lax.rem(chip, 2)
    z = lax.div(chip, 2)
    sibling = e + 1 - 2 * parity
    other = 1 - h
    full = 2 * width
    half_width = width // 2
    block = columns // 2
    own_block = lax.div(z, block)

    def blocks(far):
        return pl.ds((1 - own_block if far else own_block) * block, block)

    def remote(src, dst, ssem, rsem, pe, ph):
        return pltpu.make_async_remote_copy(
            src_ref=src, dst_ref=dst, send_sem=ssem, recv_sem=rsem,
            device_id=(pe, ph), device_id_type=pl.DeviceIdType.MESH,
        )

    def send(*args):
        remote(*args).start()

    def flip(a, d):
        bit = 1
        out = a
        while bit <= d:
            if d & bit:
                out = out + bit * (1 - 2 * lax.rem(lax.div(a, bit), 2))
            bit *= 2
        return out

    def arrived(slot, rsem):
        remote(slot, slot, line_ss, rsem, sibling, h).wait_recv()

    def drained(sent, ssem):
        remote(sent, sent, ssem, twin_rs.at[0, 0], sibling, h).wait_send()

    moves = [(tok_hbm.at[pl.ds(g * sub, sub)], tok_buf.at[h, g, z, y, parity]) for g in range(groups)]
    moves += [(ids_hbm, ids_ref), (probs_hbm, probs_ref), (pad_hbm, pad_ref)]
    moves += [(up_hbm.at[pl.ds(g * sub, sub)], up_ref.at[g]) for g in range(groups)]
    moves += [(wg_hbm.at[0], wg), (wu_hbm.at[0], wu), (wd_hbm.at[0], wd)]
    loads = [pltpu.make_async_copy(src, dst, w_sem.at[i]) for i, (src, dst) in enumerate(moves)]
    for c in loads:
        c.start()

    near = list(range(1, chips))
    outer = near[::-1]

    across = 4 * z + 2 * (1 - y) + parity
    barrier = pltpu.get_barrier_semaphore()
    partners = [(4 * flip(z, dz) + 2 * y + parity, h) for dz in reversed(range(1, columns))]
    partners += [(across, other), (across, h), (e, other), (sibling, h)]
    for partner in partners:
        pl.semaphore_signal(
            barrier, inc=1, device_id=partner, device_id_type=pl.DeviceIdType.MESH
        )
    pl.semaphore_wait(barrier, len(partners))

    def spread(g, dz):
        slot = tok_buf.at[h, g, flip(z, dz), y, parity]
        k = dz // block
        send(slot, slot, quad_ss.at[2], quad_rs.at[g, 2, k], across, other)
        send(slot, slot, quad_ss.at[0], quad_rs.at[g, 0, k], across, h)
        send(slot, slot, quad_ss.at[1], quad_rs.at[g, 1, k], e, other)
        send(slot, slot, twin_ss, twin_rs.at[g, h], sibling, h)

    for g in range(groups):
        loads[g].wait()
        mine = tok_buf.at[h, g, z, y, parity]
        for dz in reversed(range(1, columns)):
            send(mine, mine, line_ss, line_rs.at[g, dz], 4 * flip(z, dz) + 2 * y + parity, h)
        spread(g, 0)

    for c in loads[groups:-3]:
        c.wait()
    eye = (
        lax.broadcasted_iota(jnp.int32, (tok, tok), 0)
        == lax.broadcasted_iota(jnp.int32, (tok, tok), 1)
    )
    top = ids_ref.shape[0]
    lane = lax.broadcasted_iota(jnp.int32, (tok, top), 1)

    def column(row):
        return jnp.sum(jnp.where(eye, jnp.broadcast_to(row, (tok, tok)), 0.0), axis=1, keepdims=True)

    ids = jnp.zeros((tok, top), jnp.float32)
    probs = jnp.zeros((tok, top), jnp.float32)
    for j in range(top):
        ids = jnp.where(lane == j, column(ids_ref[j:j + 1, :].astype(jnp.float32)), ids)
        probs = jnp.where(lane == j, column(probs_ref[j:j + 1, :]), probs)
    pad = column(pad_ref[...].astype(jnp.float32))
    shares = probs / jnp.sum(probs, axis=1, keepdims=True)
    for i in range(n):
        share = jnp.sum(jnp.where(ids == float(i), shares, 0.0), axis=1, keepdims=True)
        for g in range(groups):
            share_s[g, i // 2, i % 2] = jnp.broadcast_to(
                share[g * sub:(g + 1) * sub], (sub, share_s.shape[4])
            )

    def lines(g):
        for dz in range(1, columns):
            zz = flip(z, dz)
            arrived(tok_buf.at[h, g, zz, y, parity], line_rs.at[g, dz])
            spread(g, dz)

    def gathered(g):
        for far in range(2):
            for k, ph, yy in ((0, h, 1 - y), (1, other, y), (2, other, 1 - y)):
                slots = tok_buf.at[ph, g, blocks(far), yy, parity]
                arrived(slots, quad_rs.at[g, k, far])
                send(slots, slots, twin_ss, twin_rs.at[g, ph], sibling, h)

    def twins(g, ph):
        arrived(tok_buf.at[ph, g, :, :, 0], twin_rs.at[g, ph])

    def column_tiles(size):
        return [slice(i, i + size) for i in range(0, hidden, size)]

    def own_rows(g):
        at = pl.ds(g * rows, rows)
        depth = pl.ds(pl.multiple_of(h * width, width), width)
        for cols in column_tiles(block_of(hidden, 256)):
            x = tok_buf[h, g].reshape(rows, width)
            gate_v[at, cols] = dot(x, wg[depth, cols])
            up_v[at, cols] = dot(x, wu[depth, cols])

    def hidden_rows(g, first, last):
        at = pl.ds(g * rows, rows)
        depth = pl.ds(pl.multiple_of(other * width, width), width)
        every = column_tiles(block_of(hidden, 256))
        for cols in every[first * len(every) // 3:last * len(every) // 3]:
            x = tok_buf[other, g].reshape(rows, width)
            gate = gate_v[at, cols] + dot(x, wg[depth, cols])
            up = up_v[at, cols] + dot(x, wu[depth, cols])
            gate_v[at, cols] = gate
            up_v[at, cols] = up
            hid[at, cols] = (gate / (1.0 + jnp.exp(-gate)) * up).astype(jnp.bfloat16)

    def down(g, far):
        start = (other if far else h) * width

        def down_step(cols, size):
            at = pl.ds(pl.multiple_of(cols.start + start, size), size)
            part = dot(hid[pl.ds(g * rows, rows), :], wd[:, at])
            osend[g, far, :, :, :, cols] = part.reshape(chips, 2, sub, size).astype(jnp.bfloat16)

        tiles(width, down_step, 1024)

    def cross_parts(g):
        for d in outer + [0]:
            pm = flip(chip, d)
            send(osend.at[g, 1, pm], orecv.at[g, pm], part_ss, part_rs.at[g, d], e, other)

    def forward(g, first, last):
        for d in (outer + [0])[first:last]:
            pm = flip(chip, d)
            arrived(orecv.at[g, pm], part_rs.at[g, d])
            total = osend[g, 0, pm].astype(jnp.float32) + orecv[g, pm].astype(jnp.float32)
            ored[g, pm] = total.astype(jnp.bfloat16)
            home = xrecv.at[g, chip, parity]
            if d:
                for q in range(2):
                    send(ored.at[g, pm, q], home, out_ss.at[0], out_rs.at[g, d], 2 * pm + q, h)
            else:
                send(ored.at[g, pm, 1 - parity], home, out_ss.at[1], out_rs.at[g, d], sibling, h)
                xrecv[g, chip, parity] = ored[g, chip, parity]

    same = (
        lax.rem(lax.broadcasted_iota(jnp.int32, (sub, rows), 1), sub)
        == lax.broadcasted_iota(jnp.int32, (sub, rows), 0)
    ).astype(jnp.float32)
    apart = (
        lax.div(lax.broadcasted_iota(jnp.int32, (n, rows), 1), sub)
        != lax.broadcasted_iota(jnp.int32, (n, rows), 0)
    ).astype(jnp.float32)

    def share_of(g, pm):
        return share_s[g, pm][:, :, :1]

    def taken(g, first, last):
        part = jnp.zeros((sub, width), jnp.float32)
        for d in range(first, last):
            pm = flip(chip, d)
            share = share_of(g, pm)
            arrived(xrecv.at[g, pm] if d else xrecv.at[g, chip, 1 - parity], out_rs.at[g, d])
            value = jnp.where(share > 0.0, xrecv[g, pm].astype(jnp.float32), 0.0)
            xs[g, pm] = value.astype(jnp.bfloat16)
            part = part + jnp.sum(share * value, axis=0)
        layer_s[g] = layer_s[g] + part if first else part

    def products(g):
        x_all = xs[g].reshape(rows, width)
        gram = dot_t(x_all, x_all).reshape(n, sub, rows) * same[None]
        gram_s[g, h] = jnp.sum(gram, axis=1)
        send(gram_s.at[g, h], gram_s.at[g, h], gram_ss, gram_rs.at[g], e, other)

    def mix(g):
        arrived(gram_s.at[g, other], gram_rs.at[g])
        whole = (gram_s[g, 0] + gram_s[g, 1]) * (apart * (orth_weight / math.sqrt(full)))
        x_all = xs[g].reshape(rows, width)
        coeffs = (whole[:, None, :] * same[None]).reshape(rows, rows)
        mixed = dot(coeffs.astype(jnp.bfloat16), x_all).reshape(chips, 2, sub, width)
        upstream = up_ref[g].astype(jnp.float32)
        real = pad[g * sub:(g + 1) * sub]
        for i in range(chips):
            gsend[g, i] = (
                real[None] * (share_of(g, i) * upstream[None] + mixed[i])
            ).astype(jnp.bfloat16)
        slot = grows.at[h, g, chip, parity]
        send(gsend.at[g, chip, 1 - parity], slot, grad_ss.at[1], grad_rs.at[g, 0], sibling, h)
        send(gsend.at[g, chip, parity], slot, relay_ss, relay_rs.at[g], e, other)
        for d in near:
            pm = flip(chip, d)
            for q in range(2):
                send(gsend.at[g, pm, q], slot, grad_ss.at[0], grad_rs.at[g, d], 2 * pm + q, h)
        grows[h, g, chip, parity] = gsend[g, chip, parity]

    def relay(g, first, last):
        for d in range(first, last):
            slot = grows.at[h, g, flip(chip, d)] if d else grows.at[h, g, chip, 1 - parity]
            arrived(slot, grad_rs.at[g, d])
            send(slot, slot, relay_ss, relay_rs.at[g], e, other)

    def act(g, dh):
        ph = lax.rem(h + dh, 2)
        at = pl.ds(g * rows, rows)
        if dh:
            arrived(grows.at[other, g], relay_rs.at[g])

        depth = pl.ds(pl.multiple_of(ph * width, width), width)
        for cols in column_tiles(block_of(hidden, 384)):
            part = dot(grows[ph, g].reshape(rows, width), wd_t[depth, cols])
            if dh:
                part = part + act_v[at, cols]
                gate = gate_v[at, cols]
                sigma = 1.0 / (1.0 + jnp.exp(-gate))
                gg[at, cols] = (
                    part * up_v[at, cols] * sigma * (1.0 + gate * (1.0 - sigma))
                ).astype(jnp.bfloat16)
                gu[at, cols] = (part * gate * sigma).astype(jnp.bfloat16)
            else:
                act_v[at, cols] = part

    def turn(first, last):
        for i in range(first, last):
            at = slice((i // 3) * half_width, (i // 3 + 1) * half_width)
            if i % 3 == 0:
                wd_t[at, :] = wd[:, at].T
            elif i % 3 == 1:
                wg_t[:, at] = wg[at, :].T
            else:
                wu_t[:, at] = wu[at, :].T

    left, right = slice(0, half_width), slice(half_width, width)

    def back(g, far):
        rows_at = pl.ds(g * rows, rows)
        start = (other if far else h) * width
        for k, cols in ((0, left), (1, right)) if far else ((1, right), (0, left)):
            at = pl.ds(pl.multiple_of(start + k * half_width, half_width), half_width)
            part = dot(gg[rows_at, :], wg_t[:, at]) + dot(gu[rows_at, :], wu_t[:, at])
            part = part.astype(jnp.bfloat16).reshape(columns, 2, 2, sub, half_width)
            for q in range(2):
                psend[g, far, k, q] = part[:, :, q]
            send(
                psend.at[g, far, k, 1 - parity], prec.at[g, far, k],
                pair_ss, pair_rs.at[g, far, k], sibling, h,
            )

    def pairs(g):
        arrived(prec.at[g, 1, 0], pair_rs.at[g, 1, 0])
        for dz in reversed(range(columns)):
            zz = flip(z, dz)
            lsend[g, zz] = (
                psend[g, 1, 0, parity, zz].astype(jnp.float32)
                + prec[g, 1, 0, zz].astype(jnp.float32)
            ).astype(jnp.bfloat16)
            send(lsend.at[g, zz], lrecv.at[g, zz], lpart_ss, line_rs.at[g, dz], e, other)
        for far in (1, 0):
            arrived(prec.at[g, far, 1], pair_rs.at[g, far, 1])
            for k in (1, 0):
                zs = blocks(k)
                rsend[g, far, zs] = (
                    psend[g, far, 1, parity, zs, 1 - y].astype(jnp.float32)
                    + prec[g, far, 1, zs, 1 - y].astype(jnp.float32)
                ).astype(jnp.bfloat16)
                send(
                    rsend.at[g, far, zs], rrecv.at[g, far, zs],
                    rpart_ss, quad_rs.at[g, far, k], across, h,
                )

    def finish_left(g, dz):
        zz = flip(z, dz)
        total = (
            psend[g, 0, 0, parity, zz].astype(jnp.float32)
            + prec[g, 0, 0, zz].astype(jnp.float32)
        )
        arrived(lrecv.at[g, zz], line_rs.at[g, dz])
        lsum[g, zz] = (total + lrecv[g, zz].astype(jnp.float32)).astype(jnp.bfloat16)
        for dy in (1, 0):
            yy = flip(y, dy)
            if dz or dy:
                send(
                    lsum.at[g, zz, yy], lfin.at[g, chip],
                    fin_ss.at[0], quad_rs.at[g, 2, 0], 4 * zz + 2 * yy + parity, h,
                )
            else:
                lfin[g, chip] = lsum[g, z, y]

    def finish_right(g, far, k):
        zs = blocks(k)
        total = (
            psend[g, far, 1, parity, zs, y].astype(jnp.float32)
            + prec[g, far, 1, zs, y].astype(jnp.float32)
        )
        arrived(rrecv.at[g, far, zs], quad_rs.at[g, far, k])
        rsum[g, far, zs] = (total + rrecv[g, far, zs].astype(jnp.float32)).astype(jnp.bfloat16)
        for dz in reversed(range(k * block, (k + 1) * block)):
            zz = flip(z, dz)
            if dz or far:
                send(
                    rsum.at[g, far, zz], rfin.at[g, columns * h + z],
                    fin_ss.at[1], quad_rs.at[g, 2, 1], 4 * zz + 2 * y + parity, other if far else h,
                )
            else:
                rfin[g, columns * h + z] = rsum[g, far, z]

    def finish(g):
        arrived(prec.at[g, 0, 0], pair_rs.at[g, 0, 0])
        for k in (1, 0):
            for far in (1, 0):
                for dz in reversed(range((2 * k + far) * block // 2, (2 * k + far + 1) * block // 2)):
                    finish_left(g, dz)
                finish_right(g, far, k)

    def collect(g):
        arrived(lfin.at[g, pl.ds(0, chips - 1)], quad_rs.at[g, 2, 0])
        arrived(rfin.at[g, pl.ds(0, chips - 1)], quad_rs.at[g, 2, 1])
        return [jnp.sum(fin[g].astype(jnp.float32), axis=0) for fin in (lfin, rfin)]

    lines(0)
    lines(1)
    gathered(0)
    twins(0, h)
    for c in loads[-3:-1]:
        c.wait()
    own_rows(0)
    twins(0, other)
    hidden_rows(0, 0, 3)
    loads[-1].wait()
    down(0, 1)
    cross_parts(0)
    gathered(1)
    down(0, 0)
    twins(1, h)
    own_rows(1)
    twins(1, other)
    hidden_rows(1, 0, 2)
    forward(0, 0, chips // 8)
    hidden_rows(1, 2, 3)
    forward(0, chips // 8, 3 * chips // 8)
    down(1, 1)
    cross_parts(1)
    turn(0, 1)
    forward(0, 3 * chips // 8, chips // 2)
    turn(1, 2)
    forward(0, chips // 2, 5 * chips // 8)
    turn(2, 3)
    forward(0, 5 * chips // 8, 3 * chips // 4)
    turn(3, 4)
    forward(0, 3 * chips // 4, 7 * chips // 8)
    turn(4, 5)
    forward(0, 7 * chips // 8, chips)
    down(1, 0)
    forward(1, 0, chips // 8)
    turn(5, 6)
    forward(1, chips // 8, chips // 4)
    turn(6, 7)
    forward(1, chips // 4, 3 * chips // 8)
    turn(7, 8)
    taken(0, 0, chips // 2)
    forward(1, 3 * chips // 8, chips // 2)
    turn(8, 9)
    taken(0, chips // 2, chips)
    products(0)
    forward(1, chips // 2, chips)
    mix(0)
    turn(9, 12)
    taken(1, 0, chips)
    products(1)
    relay(0, 0, 3 * chips // 8)
    mix(1)
    layer_ref[...] = layer_s[...].reshape(tok, width).astype(jnp.bfloat16)
    relay(0, 3 * chips // 8, chips)
    relay(1, 0, 5 * chips // 8)
    act(0, 0)
    relay(1, 5 * chips // 8, 6 * chips // 8)
    act(0, 1)
    relay(1, 6 * chips // 8, chips)
    back(0, 1)
    back(0, 0)
    act(1, 0)
    pairs(0)
    act(1, 1)
    back(1, 1)
    back(1, 0)
    finish(0)
    pairs(1)
    finish(1)
    total_a = collect(0)
    total_b = collect(1)
    for k, at in enumerate((left, right)):
        gtok_ref[:, at] = jnp.concatenate([total_a[k], total_b[k]], axis=0).astype(jnp.bfloat16)
    drained(tok_buf.at[0, :, pl.ds(0, columns - 1), 0, 0], line_ss)
    for k in range(3):
        drained(tok_buf.at[0, :, :, 0, 0], quad_ss.at[k])
    drained(tok_buf.at[0], twin_ss)
    drained(osend.at[:, 1], part_ss)
    drained(ored.at[:, pl.ds(0, chips - 1)], out_ss.at[0])
    drained(ored.at[:, 0, 0], out_ss.at[1])
    drained(gram_s.at[:, 0], gram_ss)
    drained(gsend.at[:, pl.ds(0, chips - 1)], grad_ss.at[0])
    drained(gsend.at[:, 0, 0], grad_ss.at[1])
    drained(grows.at[0], relay_ss)
    drained(psend.at[:, :, :, 0], pair_ss)
    drained(lsend, lpart_ss)
    drained(rsend, rpart_ss)
    drained(lfin.at[:, pl.ds(0, chips - 1)], fin_ss.at[0])
    drained(rfin.at[:, pl.ds(0, chips - 1)], fin_ss.at[1])


def fused(tokens, upstream, expert_ids, gate_probs, pad_mask, gate_weight, up_weight, down_weight):
    n, groups = lax.axis_size("expert"), 2
    tok, width = tokens.shape
    hidden = gate_weight.shape[2]
    sub, full, chips = tok // groups, 2 * width, n // 2
    columns, every = chips // 2, n * tok
    top = expert_ids.shape[1]
    low, wide = jnp.bfloat16, jnp.float32
    vmem, dma = pltpu.VMEM, pltpu.SemaphoreType.DMA
    local = pl.BlockSpec(memory_space=pltpu.VMEM)
    remain = pl.BlockSpec(memory_space=pl.ANY)
    outs = pl.pallas_call(
        functools.partial(fused_kernel, n, groups),
        out_shape=[vmem((tok, width), low)] * 2,
        in_specs=[remain] * 8,
        out_specs=[local] * 2,
        scratch_shapes=[
            vmem((groups, sub, width), low),
            vmem((top, tok), jnp.int32),
            vmem((top, tok), wide),
            vmem((1, tok), jnp.int32),
            vmem((2, groups, columns, 2, 2, sub, width), low),
            vmem((full, hidden), low),
            vmem((full, hidden), low),
            vmem((hidden, full), low),
            vmem((every, hidden), wide),
            vmem((every, hidden), wide),
            vmem((every, hidden), wide),
            vmem((every, hidden), low),
            vmem((every, hidden), low),
            vmem((every, hidden), low),
            vmem((hidden, full), low),
            vmem((hidden, full), low),
            vmem((full, hidden), low),
            vmem((groups, 2, chips, 2, sub, width), low),
            vmem((groups, chips, 2, sub, width), low),
            vmem((groups, chips, 2, sub, width), low),
            vmem((groups, chips, 2, sub, width), low),
            vmem((groups, chips, 2, sub, width), low),
            vmem((groups, 2, n, n * sub), wide),
            vmem((groups, chips, 2, sub, 128), wide),
            vmem((groups, sub, width), wide),
            vmem((groups, chips, 2, sub, width), low),
            vmem((2, groups, chips, 2, sub, width), low),
            vmem((groups, 2, 2, 2, columns, 2, sub, width // 2), low),
            vmem((groups, 2, 2, columns, 2, sub, width // 2), low),
            vmem((groups, columns, 2, sub, width // 2), low),
            vmem((groups, columns, 2, sub, width // 2), low),
            vmem((groups, columns, 2, sub, width // 2), low),
            vmem((groups, chips, sub, width // 2), low),
            vmem((groups, 2, columns, sub, width // 2), low),
            vmem((groups, 2, columns, sub, width // 2), low),
            vmem((groups, 2, columns, sub, width // 2), low),
            vmem((groups, chips, sub, width // 2), low),
            dma((2 * groups + 6,)),
            dma(()),
            dma((3,)),
            dma(()),
            dma((groups, columns)),
            dma((groups, 3, 2)),
            dma((groups, 2)),
            dma(()),
            dma((groups, chips)),
            dma((2,)),
            dma((groups, chips)),
            dma(()),
            dma((groups,)),
            dma((2,)),
            dma((groups, chips)),
            dma(()),
            dma((groups,)),
            dma(()),
            dma((groups, 2, 2)),
            dma(()),
            dma(()),
            dma((2,)),
        ],
        compiler_params=pltpu.CompilerParams(
            collective_id=0, has_side_effects=True, vmem_limit_bytes=56 * 1024 * 1024
        ),
        name="experts",
    )(
        tokens, upstream, expert_ids.T, gate_probs.T, pad_mask.reshape(1, tok),
        gate_weight, up_weight, down_weight,
    )
    result = [jax.ShapeDtypeStruct((tok, width), low)] * 2
    return pl.pallas_call(
        copy_kernel, out_shape=result, in_specs=[local] * 2, out_specs=[local] * 2, name="results"
    )(*[pltpu.with_memory_space_constraint(out, pltpu.VMEM) for out in outs])


def shards(tokens, upstream, expert_ids, gate_probs, pad_mask, gate_weight, up_weight, down_weight):
    tok_count, top_count = expert_ids.shape
    experts = lax.axis_size("expert")
    capacity = min(tok_count, 2 * tok_count * top_count // experts)
    paired = experts > 15 and experts & (experts - 1) == 0 and lax.axis_size("half") == 2
    if capacity == tok_count and tok_count % 16 == 0 and paired:
        return fused(
            tokens, upstream, expert_ids, gate_probs, pad_mask, gate_weight, up_weight, down_weight
        )
    slots_total = experts * capacity
    full_width = tokens.shape[1] * lax.axis_size("half")
    slot_dest = assign_slots(expert_ids, experts, capacity)
    place_items = placement_matrix(slot_dest, slots_total)
    place_tokens = jnp.sum(place_items.reshape(slots_total, tok_count, top_count), axis=2)
    weight_gate = gate_weight[0]
    weight_up = up_weight[0]
    weight_down = down_weight[0]
    rows_in = to_experts(place_tokens, tokens)
    gate_val = jnp.dot(rows_in, weight_gate, preferred_element_type=jnp.float32)
    up_val = jnp.dot(rows_in, weight_up, preferred_element_type=jnp.float32)
    hidden_act = (jax.nn.silu(gate_val) * up_val).astype(jnp.bfloat16)
    partial_value = jnp.dot(hidden_act, weight_down, preferred_element_type=jnp.float32)
    out_home = to_homes(partial_value)
    outputs = jnp.take(out_home, slot_dest, axis=0).reshape(tok_count, top_count, -1)
    out_float = outputs.astype(jnp.float32)
    shares = gate_probs / jnp.sum(gate_probs, axis=1, keepdims=True)
    layer_out = jnp.sum(shares[:, :, None] * out_float, axis=1).astype(jnp.bfloat16)
    gram_part = jnp.einsum("tjd,tkd->tjk", out_float, out_float) / math.sqrt(full_width)
    gram = lax.psum(gram_part, "half")
    off_diag = 1.0 - jnp.eye(top_count, dtype=jnp.float32)
    coeffs = orth_weight * gram * off_diag
    grad_out = pad_mask.astype(jnp.float32)[:, None, None] * (
        shares[:, :, None] * upstream.astype(jnp.float32)[:, None, :]
        + jnp.einsum("tjk,tkd->tjd", coeffs, out_float)
    )
    grad_items = grad_out.astype(jnp.bfloat16).reshape(tok_count * top_count, -1)
    grad_rows = to_experts(place_items, grad_items)
    grad_act = jnp.einsum("rd,hd->rh", grad_rows, weight_down, preferred_element_type=jnp.float32)
    sigma = jax.nn.sigmoid(gate_val)
    grad_gate = (grad_act * up_val * sigma * (1.0 + gate_val * (1.0 - sigma))).astype(jnp.bfloat16)
    grad_up = (grad_act * gate_val * sigma).astype(jnp.bfloat16)
    grad_partial = jnp.einsum(
        "rh,dh->rd", grad_gate, weight_gate, preferred_element_type=jnp.float32
    )
    grad_partial = grad_partial + jnp.einsum(
        "rh,dh->rd", grad_up, weight_up, preferred_element_type=jnp.float32
    )
    grad_home = to_homes(grad_partial)
    grad_pairs = jnp.take(grad_home, slot_dest, axis=0).reshape(tok_count, top_count, -1)
    grad_tokens = jnp.sum(grad_pairs.astype(jnp.float32), axis=1).astype(jnp.bfloat16)
    return (layer_out, grad_tokens)


def solution(mesh):
    in_specs = (
        P("expert", "half"),
        P("expert", "half"),
        P("expert", None),
        P("expert", None),
        P("expert"),
        P("expert", None, "half"),
        P("expert", None, "half"),
        P("expert", "half", None),
    )
    out_specs = (P("expert", "half"), P("expert", "half"))
    return jax.shard_map(shards, mesh=mesh, in_specs=in_specs, out_specs=out_specs, check_vma=False)
```

```python
import functools
import math

import jax
import jax.numpy as jnp
from jax import lax
from jax.experimental import pallas as pl
from jax.experimental.pallas import tpu as pltpu
from jax.sharding import PartitionSpec as P

orth_weight = 0.25


def assign_slots(expert_ids, experts, capacity):
    tok_count, top_count = expert_ids.shape
    flat_ids = expert_ids.reshape(tok_count * top_count)
    onehot = (flat_ids[:, None] == jnp.arange(experts, dtype=jnp.int32)[None, :]).astype(jnp.int32)
    before = jnp.cumsum(onehot, axis=0) - onehot
    slot_index = jnp.sum(before * onehot, axis=1)
    return flat_ids * capacity + slot_index


def placement_matrix(slot_dest, slots_total):
    row_index = jnp.arange(slots_total, dtype=jnp.int32)
    return (row_index[:, None] == slot_dest[None, :]).astype(jnp.bfloat16)


def to_experts(place, items):
    whole = lax.all_gather(items, "half", axis=1, tiled=True)
    buckets = jnp.dot(place, whole, preferred_element_type=jnp.float32).astype(jnp.bfloat16)
    return lax.all_to_all(buckets, "expert", split_axis=0, concat_axis=0, tiled=True)


def to_homes(partial_value):
    summed = lax.psum_scatter(
        partial_value.astype(jnp.bfloat16), "half", scatter_dimension=1, tiled=True
    )
    return lax.all_to_all(summed, "expert", split_axis=0, concat_axis=0, tiled=True)


def block_of(width, most):
    return next((b for b in (1024, 512, 384, 256, 128) if b <= most and width % b == 0), width)


def tiles(width, body, most=256):
    size = block_of(width, most)

    def step(j, carry):
        body(pl.ds(pl.multiple_of(j * size, size), size), size)
        return carry

    lax.fori_loop(0, width // size, step, 0)


def dot(a, b):
    return jnp.dot(a, b, preferred_element_type=jnp.float32)


def dot_t(a, b):
    return lax.dot_general(a, b, (((1,), (1,)), ((), ())), preferred_element_type=jnp.float32)


def copy_kernel(a_ref, b_ref, a_out, b_out):
    a_out[...] = a_ref[...]
    b_out[...] = b_ref[...]


def fused_kernel(
    n, groups,
    tok_hbm, up_hbm, ids_hbm, probs_hbm, pad_hbm, wg_hbm, wu_hbm, wd_hbm,
    layer_ref, gtok_ref,
    up_ref, ids_ref, probs_ref, pad_ref,
    tok_buf, wg, wu, wd, gate_v, up_v, act_v, hid, gg, gu,
    wg_t, wu_t, wd_t,
    osend, orecv, ored, xrecv, xmore, xs, gram_s, share_s, layer_s, gsend, grows, psend, prec,
    lsend, lrecv, lsum, lfin, rsend, rrecv, rsum, rfin,
    w_sem, line_ss, quad_ss, twin_ss, line_rs, quad_rs, twin_rs, part_ss, part_rs, out_ss, out_rs,
    gram_ss, gram_rs, grad_ss, grad_rs, relay_ss, relay_rs, pair_ss, pair_rs, lpart_ss, rpart_ss, fin_ss,
):
    e = lax.axis_index("expert")
    h = lax.axis_index("half")
    sub, width = tok_buf.shape[5:]
    hidden = wg.shape[1]
    tok = groups * sub
    rows = n * sub
    chips = n // 2
    columns = chips // 2
    parity = lax.rem(e, 2)
    chip = lax.div(e, 2)
    y = lax.rem(chip, 2)
    z = lax.div(chip, 2)
    sibling = e + 1 - 2 * parity
    other = 1 - h
    full = 2 * width
    half_width = width // 2
    block = columns // 2
    own_block = lax.div(z, block)

    def blocks(far):
        return pl.ds((1 - own_block if far else own_block) * block, block)

    def remote(src, dst, ssem, rsem, pe, ph):
        return pltpu.make_async_remote_copy(
            src_ref=src, dst_ref=dst, send_sem=ssem, recv_sem=rsem,
            device_id=(pe, ph), device_id_type=pl.DeviceIdType.MESH,
        )

    def send(*args):
        remote(*args).start()

    def flip(a, d):
        bit = 1
        out = a
        while bit <= d:
            if d & bit:
                out = out + bit * (1 - 2 * lax.rem(lax.div(a, bit), 2))
            bit *= 2
        return out

    def arrived(slot, rsem):
        remote(slot, slot, line_ss, rsem, sibling, h).wait_recv()

    def drained(sent, ssem):
        remote(sent, sent, ssem, twin_rs.at[0, 0], sibling, h).wait_send()

    moves = [(tok_hbm.at[pl.ds(g * sub, sub)], tok_buf.at[h, g, z, y, parity]) for g in range(groups)]
    moves += [(ids_hbm, ids_ref), (probs_hbm, probs_ref), (pad_hbm, pad_ref)]
    moves += [(up_hbm.at[pl.ds(g * sub, sub)], up_ref.at[g]) for g in range(groups)]
    moves += [(wg_hbm.at[0], wg), (wu_hbm.at[0], wu), (wd_hbm.at[0], wd)]
    loads = [pltpu.make_async_copy(src, dst, w_sem.at[i]) for i, (src, dst) in enumerate(moves)]
    for c in loads:
        c.start()

    near = list(range(1, chips))
    outer = near[::-1]

    across = 4 * z + 2 * (1 - y) + parity
    barrier = pltpu.get_barrier_semaphore()
    partners = [(4 * flip(z, dz) + 2 * y + parity, h) for dz in reversed(range(1, columns))]
    partners += [(across, other), (across, h), (e, other), (sibling, h)]
    for partner in partners:
        pl.semaphore_signal(
            barrier, inc=1, device_id=partner, device_id_type=pl.DeviceIdType.MESH
        )
    pl.semaphore_wait(barrier, len(partners))

    def spread(g, dz):
        slot = tok_buf.at[h, g, flip(z, dz), y, parity]
        k = dz // block
        send(slot, slot, quad_ss.at[2], quad_rs.at[g, 2, k], across, other)
        send(slot, slot, quad_ss.at[0], quad_rs.at[g, 0, k], across, h)
        send(slot, slot, quad_ss.at[1], quad_rs.at[g, 1, k], e, other)
        send(slot, slot, twin_ss, twin_rs.at[g, h], sibling, h)

    for g in range(groups):
        loads[g].wait()
        mine = tok_buf.at[h, g, z, y, parity]
        for dz in reversed(range(1, columns)):
            send(mine, mine, line_ss, line_rs.at[g, dz], 4 * flip(z, dz) + 2 * y + parity, h)
        spread(g, 0)

    for c in loads[groups:-3]:
        c.wait()
    eye = (
        lax.broadcasted_iota(jnp.int32, (tok, tok), 0)
        == lax.broadcasted_iota(jnp.int32, (tok, tok), 1)
    )
    top = ids_ref.shape[0]
    lane = lax.broadcasted_iota(jnp.int32, (tok, top), 1)

    def column(row):
        return jnp.sum(jnp.where(eye, jnp.broadcast_to(row, (tok, tok)), 0.0), axis=1, keepdims=True)

    ids = jnp.zeros((tok, top), jnp.float32)
    probs = jnp.zeros((tok, top), jnp.float32)
    for j in range(top):
        ids = jnp.where(lane == j, column(ids_ref[j:j + 1, :].astype(jnp.float32)), ids)
        probs = jnp.where(lane == j, column(probs_ref[j:j + 1, :]), probs)
    pad = column(pad_ref[...].astype(jnp.float32))
    shares = probs / jnp.sum(probs, axis=1, keepdims=True)
    for i in range(n):
        share = jnp.sum(jnp.where(ids == float(i), shares, 0.0), axis=1, keepdims=True)
        for g in range(groups):
            share_s[g, i // 2, i % 2] = jnp.broadcast_to(
                share[g * sub:(g + 1) * sub], (sub, share_s.shape[4])
            )

    def lines(g):
        for dz in range(1, columns):
            zz = flip(z, dz)
            arrived(tok_buf.at[h, g, zz, y, parity], line_rs.at[g, dz])
            spread(g, dz)

    def gathered(g):
        for far in range(2):
            for k, ph, yy in ((0, h, 1 - y), (1, other, y), (2, other, 1 - y)):
                slots = tok_buf.at[ph, g, blocks(far), yy, parity]
                arrived(slots, quad_rs.at[g, k, far])
                send(slots, slots, twin_ss, twin_rs.at[g, ph], sibling, h)

    def twins(g, ph):
        arrived(tok_buf.at[ph, g, :, :, 0], twin_rs.at[g, ph])

    def column_tiles(size):
        return [slice(i, i + size) for i in range(0, hidden, size)]

    def own_rows(g):
        at = pl.ds(g * rows, rows)
        depth = pl.ds(pl.multiple_of(h * width, width), width)
        for cols in column_tiles(block_of(hidden, 256)):
            x = tok_buf[h, g].reshape(rows, width)
            gate_v[at, cols] = dot(x, wg[depth, cols])
            up_v[at, cols] = dot(x, wu[depth, cols])

    def hidden_rows(g, first, last):
        at = pl.ds(g * rows, rows)
        depth = pl.ds(pl.multiple_of(other * width, width), width)
        every = column_tiles(block_of(hidden, 256))
        for cols in every[first * len(every) // 3:last * len(every) // 3]:
            x = tok_buf[other, g].reshape(rows, width)
            gate = gate_v[at, cols] + dot(x, wg[depth, cols])
            up = up_v[at, cols] + dot(x, wu[depth, cols])
            gate_v[at, cols] = gate
            up_v[at, cols] = up
            hid[at, cols] = (gate / (1.0 + jnp.exp(-gate)) * up).astype(jnp.bfloat16)

    def down(g, far):
        start = (other if far else h) * width

        def down_step(cols, size):
            at = pl.ds(pl.multiple_of(cols.start + start, size), size)
            part = dot(hid[pl.ds(g * rows, rows), :], wd[:, at])
            osend[g, far, :, :, :, cols] = part.reshape(chips, 2, sub, size).astype(jnp.bfloat16)

        tiles(width, down_step, 1024)

    def straight(g, d):
        return g == 0 and d == chips - 1

    def cross_parts(g):
        for d in outer + [0]:
            pm = flip(chip, d)
            if straight(g, d):
                for q in range(2):
                    send(
                        osend.at[g, 1, pm, q], xmore.at[parity],
                        part_ss, out_rs.at[g, d], 2 * pm + q, other,
                    )
            else:
                send(osend.at[g, 1, pm], orecv.at[g, pm], part_ss, part_rs.at[g, d], e, other)

    def own_parts(g):
        pm = flip(chip, chips - 1)
        for q in range(2):
            send(
                osend.at[g, 0, pm, q], xrecv.at[g, chip, parity],
                out_ss.at[0], out_rs.at[g, chips - 1], 2 * pm + q, h,
            )

    def forward(g, first, last):
        for d in (outer + [0])[first:last]:
            if straight(g, d):
                continue
            pm = flip(chip, d)
            arrived(orecv.at[g, pm], part_rs.at[g, d])
            total = osend[g, 0, pm].astype(jnp.float32) + orecv[g, pm].astype(jnp.float32)
            ored[g, pm] = total.astype(jnp.bfloat16)
            home = xrecv.at[g, chip, parity]
            if d:
                for q in range(2):
                    send(ored.at[g, pm, q], home, out_ss.at[0], out_rs.at[g, d], 2 * pm + q, h)
            else:
                send(ored.at[g, pm, 1 - parity], home, out_ss.at[1], out_rs.at[g, d], sibling, h)
                xrecv[g, chip, parity] = ored[g, chip, parity]

    same = (
        lax.rem(lax.broadcasted_iota(jnp.int32, (sub, rows), 1), sub)
        == lax.broadcasted_iota(jnp.int32, (sub, rows), 0)
    ).astype(jnp.float32)
    apart = (
        lax.div(lax.broadcasted_iota(jnp.int32, (n, rows), 1), sub)
        != lax.broadcasted_iota(jnp.int32, (n, rows), 0)
    ).astype(jnp.float32)

    def share_of(g, pm):
        return share_s[g, pm][:, :, :1]

    def taken(g, first, last):
        part = jnp.zeros((sub, width), jnp.float32)
        for d in range(first, last):
            pm = flip(chip, d)
            share = share_of(g, pm)
            result = xrecv.at[g, pl.ds(0, 2)] if straight(g, d) else xrecv.at[g, pm]
            arrived(result if d else xrecv.at[g, chip, 1 - parity], out_rs.at[g, d])
            value = xrecv[g, pm].astype(jnp.float32)
            if straight(g, d):
                value = (value + xmore[...].astype(jnp.float32)).astype(jnp.bfloat16).astype(jnp.float32)
            value = jnp.where(share > 0.0, value, 0.0)
            xs[g, pm] = value.astype(jnp.bfloat16)
            part = part + jnp.sum(share * value, axis=0)
        layer_s[g] = layer_s[g] + part if first else part

    def products(g):
        x_all = xs[g].reshape(rows, width)
        gram = dot_t(x_all, x_all).reshape(n, sub, rows) * same[None]
        gram_s[g, h] = jnp.sum(gram, axis=1)
        send(gram_s.at[g, h], gram_s.at[g, h], gram_ss, gram_rs.at[g], e, other)

    def mix(g):
        arrived(gram_s.at[g, other], gram_rs.at[g])
        whole = (gram_s[g, 0] + gram_s[g, 1]) * (apart * (orth_weight / math.sqrt(full)))
        x_all = xs[g].reshape(rows, width)
        coeffs = (whole[:, None, :] * same[None]).reshape(rows, rows)
        mixed = dot(coeffs.astype(jnp.bfloat16), x_all).reshape(chips, 2, sub, width)
        upstream = up_ref[g].astype(jnp.float32)
        real = pad[g * sub:(g + 1) * sub]
        for i in range(chips):
            gsend[g, i] = (
                real[None] * (share_of(g, i) * upstream[None] + mixed[i])
            ).astype(jnp.bfloat16)
        slot = grows.at[h, g, chip, parity]
        send(gsend.at[g, chip, 1 - parity], slot, grad_ss.at[1], grad_rs.at[g, 0], sibling, h)
        send(gsend.at[g, chip, parity], slot, relay_ss, relay_rs.at[g], e, other)
        for d in near:
            pm = flip(chip, d)
            for q in range(2):
                send(gsend.at[g, pm, q], slot, grad_ss.at[0], grad_rs.at[g, d], 2 * pm + q, h)
        grows[h, g, chip, parity] = gsend[g, chip, parity]

    def relay(g, first, last):
        for d in range(first, last):
            slot = grows.at[h, g, flip(chip, d)] if d else grows.at[h, g, chip, 1 - parity]
            arrived(slot, grad_rs.at[g, d])
            send(slot, slot, relay_ss, relay_rs.at[g], e, other)

    def act(g, dh):
        ph = lax.rem(h + dh, 2)
        at = pl.ds(g * rows, rows)
        if dh:
            arrived(grows.at[other, g], relay_rs.at[g])

        depth = pl.ds(pl.multiple_of(ph * width, width), width)
        for cols in column_tiles(block_of(hidden, 384)):
            part = dot(grows[ph, g].reshape(rows, width), wd_t[depth, cols])
            if dh:
                part = part + act_v[at, cols]
                gate = gate_v[at, cols]
                sigma = 1.0 / (1.0 + jnp.exp(-gate))
                gg[at, cols] = (
                    part * up_v[at, cols] * sigma * (1.0 + gate * (1.0 - sigma))
                ).astype(jnp.bfloat16)
                gu[at, cols] = (part * gate * sigma).astype(jnp.bfloat16)
            else:
                act_v[at, cols] = part

    def turn(first, last):
        for i in range(first, last):
            at = slice((i // 3) * half_width, (i // 3 + 1) * half_width)
            if i % 3 == 0:
                wd_t[at, :] = wd[:, at].T
            elif i % 3 == 1:
                wg_t[:, at] = wg[at, :].T
            else:
                wu_t[:, at] = wu[at, :].T

    left, right = slice(0, half_width), slice(half_width, width)

    def back(g, far):
        rows_at = pl.ds(g * rows, rows)
        start = (other if far else h) * width
        for k, cols in ((0, left), (1, right)) if far else ((1, right), (0, left)):
            at = pl.ds(pl.multiple_of(start + k * half_width, half_width), half_width)
            part = dot(gg[rows_at, :], wg_t[:, at]) + dot(gu[rows_at, :], wu_t[:, at])
            part = part.astype(jnp.bfloat16).reshape(columns, 2, 2, sub, half_width)
            for q in range(2):
                psend[g, far, k, q] = part[:, :, q]
            send(
                psend.at[g, far, k, 1 - parity], prec.at[g, far, k],
                pair_ss, pair_rs.at[g, far, k], sibling, h,
            )

    def pairs_left(g):
        arrived(prec.at[g, 1, 0], pair_rs.at[g, 1, 0])
        for dz in reversed(range(columns)):
            zz = flip(z, dz)
            lsend[g, zz] = (
                psend[g, 1, 0, parity, zz].astype(jnp.float32)
                + prec[g, 1, 0, zz].astype(jnp.float32)
            ).astype(jnp.bfloat16)
            send(lsend.at[g, zz], lrecv.at[g, zz], lpart_ss, line_rs.at[g, dz], e, other)

    def pairs_right(g):
        for far in (1, 0):
            arrived(prec.at[g, far, 1], pair_rs.at[g, far, 1])
            for k in (1, 0):
                zs = blocks(k)
                rsend[g, far, zs] = (
                    psend[g, far, 1, parity, zs, 1 - y].astype(jnp.float32)
                    + prec[g, far, 1, zs, 1 - y].astype(jnp.float32)
                ).astype(jnp.bfloat16)
                send(
                    rsend.at[g, far, zs], rrecv.at[g, far, zs],
                    rpart_ss, quad_rs.at[g, far, k], across, h,
                )

    def finish_left(g, dz):
        zz = flip(z, dz)
        total = (
            psend[g, 0, 0, parity, zz].astype(jnp.float32)
            + prec[g, 0, 0, zz].astype(jnp.float32)
        )
        arrived(lrecv.at[g, zz], line_rs.at[g, dz])
        lsum[g, zz] = (total + lrecv[g, zz].astype(jnp.float32)).astype(jnp.bfloat16)
        for dy in (1, 0):
            yy = flip(y, dy)
            if dz or dy:
                send(
                    lsum.at[g, zz, yy], lfin.at[g, chip],
                    fin_ss.at[0], quad_rs.at[g, 2, 0], 4 * zz + 2 * yy + parity, h,
                )
            else:
                lfin[g, chip] = lsum[g, z, y]

    def finish_right(g, far, k):
        zs = blocks(k)
        total = (
            psend[g, far, 1, parity, zs, y].astype(jnp.float32)
            + prec[g, far, 1, zs, y].astype(jnp.float32)
        )
        arrived(rrecv.at[g, far, zs], quad_rs.at[g, far, k])
        rsum[g, far, zs] = (total + rrecv[g, far, zs].astype(jnp.float32)).astype(jnp.bfloat16)
        for dz in reversed(range(k * block, (k + 1) * block)):
            zz = flip(z, dz)
            if dz or far:
                send(
                    rsum.at[g, far, zz], rfin.at[g, columns * h + z],
                    fin_ss.at[1], quad_rs.at[g, 2, 1], 4 * zz + 2 * y + parity, other if far else h,
                )
            else:
                rfin[g, columns * h + z] = rsum[g, far, z]

    def finish(g):
        arrived(prec.at[g, 0, 0], pair_rs.at[g, 0, 0])
        for k in (1, 0):
            for far in (1, 0):
                for dz in reversed(range((2 * k + far) * block // 2, (2 * k + far + 1) * block // 2)):
                    finish_left(g, dz)
                finish_right(g, far, k)

    def collect(g):
        arrived(lfin.at[g, pl.ds(0, chips - 1)], quad_rs.at[g, 2, 0])
        arrived(rfin.at[g, pl.ds(0, chips - 1)], quad_rs.at[g, 2, 1])
        return [jnp.sum(fin[g].astype(jnp.float32), axis=0) for fin in (lfin, rfin)]

    lines(0)
    lines(1)
    gathered(0)
    twins(0, h)
    for c in loads[-3:-1]:
        c.wait()
    own_rows(0)
    twins(0, other)
    hidden_rows(0, 0, 3)
    loads[-1].wait()
    down(0, 1)
    cross_parts(0)
    down(0, 0)
    own_parts(0)
    gathered(1)
    twins(1, h)
    own_rows(1)
    twins(1, other)
    hidden_rows(1, 0, 2)
    forward(0, 0, chips // 8)
    hidden_rows(1, 2, 3)
    forward(0, chips // 8, 3 * chips // 8)
    down(1, 1)
    cross_parts(1)
    turn(0, 1)
    forward(0, 3 * chips // 8, chips // 2)
    turn(1, 2)
    forward(0, chips // 2, 5 * chips // 8)
    turn(2, 3)
    forward(0, 5 * chips // 8, 3 * chips // 4)
    turn(3, 4)
    forward(0, 3 * chips // 4, 7 * chips // 8)
    turn(4, 5)
    forward(0, 7 * chips // 8, chips)
    down(1, 0)
    forward(1, 0, chips // 8)
    turn(5, 6)
    forward(1, chips // 8, chips // 4)
    taken(0, 0, chips // 2)
    forward(1, chips // 4, 3 * chips // 8)
    taken(0, chips // 2, chips)
    products(0)
    forward(1, 3 * chips // 8, 5 * chips // 8)
    turn(6, 7)
    forward(1, 5 * chips // 8, 3 * chips // 4)
    turn(7, 8)
    forward(1, 3 * chips // 4, 7 * chips // 8)
    turn(8, 9)
    forward(1, 7 * chips // 8, chips)
    mix(0)
    turn(9, 12)
    taken(1, 0, chips)
    products(1)
    relay(0, 0, 3 * chips // 8)
    mix(1)
    layer_ref[...] = layer_s[...].reshape(tok, width).astype(jnp.bfloat16)
    relay(0, 3 * chips // 8, chips)
    relay(1, 0, 5 * chips // 8)
    act(0, 0)
    relay(1, 5 * chips // 8, 6 * chips // 8)
    act(0, 1)
    relay(1, 6 * chips // 8, chips)
    back(0, 1)
    back(0, 0)
    act(1, 0)
    pairs_left(0)
    pairs_right(0)
    act(1, 1)
    back(1, 1)
    back(1, 0)
    pairs_left(1)
    finish(0)
    pairs_right(1)
    finish(1)
    total_a = collect(0)
    total_b = collect(1)
    for k, at in enumerate((left, right)):
        gtok_ref[:, at] = jnp.concatenate([total_a[k], total_b[k]], axis=0).astype(jnp.bfloat16)
    drained(tok_buf.at[0, :, pl.ds(0, columns - 1), 0, 0], line_ss)
    for k in range(3):
        drained(tok_buf.at[0, :, :, 0, 0], quad_ss.at[k])
    drained(tok_buf.at[0], twin_ss)
    drained(osend.at[:, 1], part_ss)
    drained(ored.at[:, pl.ds(0, chips - 1)], out_ss.at[0])
    drained(ored.at[:, 0, 0], out_ss.at[1])
    drained(gram_s.at[:, 0], gram_ss)
    drained(gsend.at[:, pl.ds(0, chips - 1)], grad_ss.at[0])
    drained(gsend.at[:, 0, 0], grad_ss.at[1])
    drained(grows.at[0], relay_ss)
    drained(psend.at[:, :, :, 0], pair_ss)
    drained(lsend, lpart_ss)
    drained(rsend, rpart_ss)
    drained(lfin.at[:, pl.ds(0, chips - 1)], fin_ss.at[0])
    drained(rfin.at[:, pl.ds(0, chips - 1)], fin_ss.at[1])


def fused(tokens, upstream, expert_ids, gate_probs, pad_mask, gate_weight, up_weight, down_weight):
    n, groups = lax.axis_size("expert"), 2
    tok, width = tokens.shape
    hidden = gate_weight.shape[2]
    sub, full, chips = tok // groups, 2 * width, n // 2
    columns, every = chips // 2, n * tok
    top = expert_ids.shape[1]
    low, wide = jnp.bfloat16, jnp.float32
    vmem, dma = pltpu.VMEM, pltpu.SemaphoreType.DMA
    local = pl.BlockSpec(memory_space=pltpu.VMEM)
    remain = pl.BlockSpec(memory_space=pl.ANY)
    outs = pl.pallas_call(
        functools.partial(fused_kernel, n, groups),
        out_shape=[vmem((tok, width), low)] * 2,
        in_specs=[remain] * 8,
        out_specs=[local] * 2,
        scratch_shapes=[
            vmem((groups, sub, width), low),
            vmem((top, tok), jnp.int32),
            vmem((top, tok), wide),
            vmem((1, tok), jnp.int32),
            vmem((2, groups, columns, 2, 2, sub, width), low),
            vmem((full, hidden), low),
            vmem((full, hidden), low),
            vmem((hidden, full), low),
            vmem((every, hidden), wide),
            vmem((every, hidden), wide),
            vmem((every, hidden), wide),
            vmem((every, hidden), low),
            vmem((every, hidden), low),
            vmem((every, hidden), low),
            vmem((hidden, full), low),
            vmem((hidden, full), low),
            vmem((full, hidden), low),
            vmem((groups, 2, chips, 2, sub, width), low),
            vmem((groups, chips, 2, sub, width), low),
            vmem((groups, chips, 2, sub, width), low),
            vmem((groups, chips, 2, sub, width), low),
            vmem((2, sub, width), low),
            vmem((groups, chips, 2, sub, width), low),
            vmem((groups, 2, n, n * sub), wide),
            vmem((groups, chips, 2, sub, 128), wide),
            vmem((groups, sub, width), wide),
            vmem((groups, chips, 2, sub, width), low),
            vmem((2, groups, chips, 2, sub, width), low),
            vmem((groups, 2, 2, 2, columns, 2, sub, width // 2), low),
            vmem((groups, 2, 2, columns, 2, sub, width // 2), low),
            vmem((groups, columns, 2, sub, width // 2), low),
            vmem((groups, columns, 2, sub, width // 2), low),
            vmem((groups, columns, 2, sub, width // 2), low),
            vmem((groups, chips, sub, width // 2), low),
            vmem((groups, 2, columns, sub, width // 2), low),
            vmem((groups, 2, columns, sub, width // 2), low),
            vmem((groups, 2, columns, sub, width // 2), low),
            vmem((groups, chips, sub, width // 2), low),
            dma((2 * groups + 6,)),
            dma(()),
            dma((3,)),
            dma(()),
            dma((groups, columns)),
            dma((groups, 3, 2)),
            dma((groups, 2)),
            dma(()),
            dma((groups, chips)),
            dma((2,)),
            dma((groups, chips)),
            dma(()),
            dma((groups,)),
            dma((2,)),
            dma((groups, chips)),
            dma(()),
            dma((groups,)),
            dma(()),
            dma((groups, 2, 2)),
            dma(()),
            dma(()),
            dma((2,)),
        ],
        compiler_params=pltpu.CompilerParams(
            collective_id=0, has_side_effects=True, vmem_limit_bytes=56 * 1024 * 1024
        ),
        name="experts",
    )(
        tokens, upstream, expert_ids.T, gate_probs.T, pad_mask.reshape(1, tok),
        gate_weight, up_weight, down_weight,
    )
    result = [jax.ShapeDtypeStruct((tok, width), low)] * 2
    return pl.pallas_call(
        copy_kernel, out_shape=result, in_specs=[local] * 2, out_specs=[local] * 2, name="results"
    )(*[pltpu.with_memory_space_constraint(out, pltpu.VMEM) for out in outs])


def shards(tokens, upstream, expert_ids, gate_probs, pad_mask, gate_weight, up_weight, down_weight):
    tok_count, top_count = expert_ids.shape
    experts = lax.axis_size("expert")
    capacity = min(tok_count, 2 * tok_count * top_count // experts)
    paired = experts > 15 and experts & (experts - 1) == 0 and lax.axis_size("half") == 2
    if capacity == tok_count and tok_count % 16 == 0 and paired:
        return fused(
            tokens, upstream, expert_ids, gate_probs, pad_mask, gate_weight, up_weight, down_weight
        )
    slots_total = experts * capacity
    full_width = tokens.shape[1] * lax.axis_size("half")
    slot_dest = assign_slots(expert_ids, experts, capacity)
    place_items = placement_matrix(slot_dest, slots_total)
    place_tokens = jnp.sum(place_items.reshape(slots_total, tok_count, top_count), axis=2)
    weight_gate = gate_weight[0]
    weight_up = up_weight[0]
    weight_down = down_weight[0]
    rows_in = to_experts(place_tokens, tokens)
    gate_val = jnp.dot(rows_in, weight_gate, preferred_element_type=jnp.float32)
    up_val = jnp.dot(rows_in, weight_up, preferred_element_type=jnp.float32)
    hidden_act = (jax.nn.silu(gate_val) * up_val).astype(jnp.bfloat16)
    partial_value = jnp.dot(hidden_act, weight_down, preferred_element_type=jnp.float32)
    out_home = to_homes(partial_value)
    outputs = jnp.take(out_home, slot_dest, axis=0).reshape(tok_count, top_count, -1)
    out_float = outputs.astype(jnp.float32)
    shares = gate_probs / jnp.sum(gate_probs, axis=1, keepdims=True)
    layer_out = jnp.sum(shares[:, :, None] * out_float, axis=1).astype(jnp.bfloat16)
    gram_part = jnp.einsum("tjd,tkd->tjk", out_float, out_float) / math.sqrt(full_width)
    gram = lax.psum(gram_part, "half")
    off_diag = 1.0 - jnp.eye(top_count, dtype=jnp.float32)
    coeffs = orth_weight * gram * off_diag
    grad_out = pad_mask.astype(jnp.float32)[:, None, None] * (
        shares[:, :, None] * upstream.astype(jnp.float32)[:, None, :]
        + jnp.einsum("tjk,tkd->tjd", coeffs, out_float)
    )
    grad_items = grad_out.astype(jnp.bfloat16).reshape(tok_count * top_count, -1)
    grad_rows = to_experts(place_items, grad_items)
    grad_act = jnp.einsum("rd,hd->rh", grad_rows, weight_down, preferred_element_type=jnp.float32)
    sigma = jax.nn.sigmoid(gate_val)
    grad_gate = (grad_act * up_val * sigma * (1.0 + gate_val * (1.0 - sigma))).astype(jnp.bfloat16)
    grad_up = (grad_act * gate_val * sigma).astype(jnp.bfloat16)
    grad_partial = jnp.einsum(
        "rh,dh->rd", grad_gate, weight_gate, preferred_element_type=jnp.float32
    )
    grad_partial = grad_partial + jnp.einsum(
        "rh,dh->rd", grad_up, weight_up, preferred_element_type=jnp.float32
    )
    grad_home = to_homes(grad_partial)
    grad_pairs = jnp.take(grad_home, slot_dest, axis=0).reshape(tok_count, top_count, -1)
    grad_tokens = jnp.sum(grad_pairs.astype(jnp.float32), axis=1).astype(jnp.bfloat16)
    return (layer_out, grad_tokens)


def solution(mesh):
    in_specs = (
        P("expert", "half"),
        P("expert", "half"),
        P("expert", None),
        P("expert", None),
        P("expert"),
        P("expert", None, "half"),
        P("expert", None, "half"),
        P("expert", "half", None),
    )
    out_specs = (P("expert", "half"), P("expert", "half"))
    return jax.shard_map(shards, mesh=mesh, in_specs=in_specs, out_specs=out_specs, check_vma=False)
```

```python
import functools
import math

import jax
import jax.numpy as jnp
from jax import lax
from jax.experimental import pallas as pl
from jax.experimental.pallas import tpu as pltpu
from jax.sharding import PartitionSpec as P

orth_weight = 0.25


def assign_slots(expert_ids, experts, capacity):
    tok_count, top_count = expert_ids.shape
    flat_ids = expert_ids.reshape(tok_count * top_count)
    onehot = (flat_ids[:, None] == jnp.arange(experts, dtype=jnp.int32)[None, :]).astype(jnp.int32)
    before = jnp.cumsum(onehot, axis=0) - onehot
    slot_index = jnp.sum(before * onehot, axis=1)
    return flat_ids * capacity + slot_index


def placement_matrix(slot_dest, slots_total):
    row_index = jnp.arange(slots_total, dtype=jnp.int32)
    return (row_index[:, None] == slot_dest[None, :]).astype(jnp.bfloat16)


def to_experts(place, items):
    whole = lax.all_gather(items, "half", axis=1, tiled=True)
    buckets = jnp.dot(place, whole, preferred_element_type=jnp.float32).astype(jnp.bfloat16)
    return lax.all_to_all(buckets, "expert", split_axis=0, concat_axis=0, tiled=True)


def to_homes(partial_value):
    summed = lax.psum_scatter(
        partial_value.astype(jnp.bfloat16), "half", scatter_dimension=1, tiled=True
    )
    return lax.all_to_all(summed, "expert", split_axis=0, concat_axis=0, tiled=True)


def block_of(width, most):
    return next((b for b in (1024, 512, 384, 256, 128) if b <= most and width % b == 0), width)


def tiles(width, body, most=256):
    size = block_of(width, most)

    def step(j, carry):
        body(pl.ds(pl.multiple_of(j * size, size), size), size)
        return carry

    lax.fori_loop(0, width // size, step, 0)


def dot(a, b):
    return jnp.dot(a, b, preferred_element_type=jnp.float32)


def dot_t(a, b):
    return lax.dot_general(a, b, (((1,), (1,)), ((), ())), preferred_element_type=jnp.float32)


def copy_kernel(a_ref, b_ref, a_out, b_out):
    a_out[...] = a_ref[...]
    b_out[...] = b_ref[...]


def fused_kernel(
    n, groups,
    tok_hbm, up_hbm, ids_hbm, probs_hbm, pad_hbm, wg_hbm, wu_hbm, wd_hbm,
    layer_ref, gtok_ref,
    up_ref, ids_ref, probs_ref, pad_ref,
    tok_buf, wg, wu, wd, gate_v, up_v, act_v, hid, gg, gu,
    wg_t, wu_t, wd_t,
    osend, orecv, ored, xrecv, xmore, xs, gram_s, share_s, layer_s, gsend, grows, psend, prec,
    lsend, lrecv, lsum, lfin, rsend, rrecv, rsum, rfin,
    w_sem, line_ss, quad_ss, twin_ss, line_rs, quad_rs, twin_rs, part_ss, part_rs, out_ss, out_rs,
    gram_ss, gram_rs, grad_ss, grad_rs, relay_ss, relay_rs, pair_ss, pair_rs, lpart_ss, rpart_ss, fin_ss,
):
    e = lax.axis_index("expert")
    h = lax.axis_index("half")
    sub, width = tok_buf.shape[5:]
    hidden = wg.shape[1]
    tok = groups * sub
    rows = n * sub
    chips = n // 2
    columns = chips // 2
    parity = lax.rem(e, 2)
    chip = lax.div(e, 2)
    y = lax.rem(chip, 2)
    z = lax.div(chip, 2)
    sibling = e + 1 - 2 * parity
    other = 1 - h
    full = 2 * width
    half_width = width // 2
    block = columns // 2
    own_block = lax.div(z, block)

    def blocks(far):
        return pl.ds((1 - own_block if far else own_block) * block, block)

    def remote(src, dst, ssem, rsem, pe, ph):
        return pltpu.make_async_remote_copy(
            src_ref=src, dst_ref=dst, send_sem=ssem, recv_sem=rsem,
            device_id=(pe, ph), device_id_type=pl.DeviceIdType.MESH,
        )

    def send(*args):
        remote(*args).start()

    def flip(a, d):
        bit = 1
        out = a
        while bit <= d:
            if d & bit:
                out = out + bit * (1 - 2 * lax.rem(lax.div(a, bit), 2))
            bit *= 2
        return out

    def arrived(slot, rsem):
        remote(slot, slot, line_ss, rsem, sibling, h).wait_recv()

    def drained(sent, ssem):
        remote(sent, sent, ssem, twin_rs.at[0, 0], sibling, h).wait_send()

    moves = [(tok_hbm.at[pl.ds(g * sub, sub)], tok_buf.at[h, g, z, y, parity]) for g in range(groups)]
    moves += [(ids_hbm, ids_ref), (probs_hbm, probs_ref), (pad_hbm, pad_ref)]
    moves += [(up_hbm.at[pl.ds(g * sub, sub)], up_ref.at[g]) for g in range(groups)]
    moves += [(wg_hbm.at[0], wg), (wu_hbm.at[0], wu), (wd_hbm.at[0], wd)]
    loads = [pltpu.make_async_copy(src, dst, w_sem.at[i]) for i, (src, dst) in enumerate(moves)]
    for c in loads:
        c.start()

    near = list(range(1, chips))
    outer = near[::-1]

    across = 4 * z + 2 * (1 - y) + parity
    barrier = pltpu.get_barrier_semaphore()
    partners = [(4 * flip(z, dz) + 2 * y + parity, h) for dz in reversed(range(1, columns))]
    partners += [(across, other), (across, h), (e, other), (sibling, h)]
    for partner in partners:
        pl.semaphore_signal(
            barrier, inc=1, device_id=partner, device_id_type=pl.DeviceIdType.MESH
        )
    pl.semaphore_wait(barrier, len(partners))

    def spread(g, dz):
        slot = tok_buf.at[h, g, flip(z, dz), y, parity]
        k = dz // block
        send(slot, slot, quad_ss.at[2], quad_rs.at[g, 2, k], across, other)
        send(slot, slot, quad_ss.at[0], quad_rs.at[g, 0, k], across, h)
        send(slot, slot, quad_ss.at[1], quad_rs.at[g, 1, k], e, other)
        send(slot, slot, twin_ss, twin_rs.at[g, h], sibling, h)

    for g in range(groups):
        loads[g].wait()
        mine = tok_buf.at[h, g, z, y, parity]
        for dz in reversed(range(1, columns)):
            send(mine, mine, line_ss, line_rs.at[g, dz], 4 * flip(z, dz) + 2 * y + parity, h)
        spread(g, 0)

    for c in loads[groups:-3]:
        c.wait()
    eye = (
        lax.broadcasted_iota(jnp.int32, (tok, tok), 0)
        == lax.broadcasted_iota(jnp.int32, (tok, tok), 1)
    )
    top = ids_ref.shape[0]
    lane = lax.broadcasted_iota(jnp.int32, (tok, top), 1)

    def column(row):
        return jnp.sum(jnp.where(eye, jnp.broadcast_to(row, (tok, tok)), 0.0), axis=1, keepdims=True)

    ids = jnp.zeros((tok, top), jnp.float32)
    probs = jnp.zeros((tok, top), jnp.float32)
    for j in range(top):
        ids = jnp.where(lane == j, column(ids_ref[j:j + 1, :].astype(jnp.float32)), ids)
        probs = jnp.where(lane == j, column(probs_ref[j:j + 1, :]), probs)
    pad = column(pad_ref[...].astype(jnp.float32))
    shares = probs / jnp.sum(probs, axis=1, keepdims=True)
    for i in range(n):
        share = jnp.sum(jnp.where(ids == float(i), shares, 0.0), axis=1, keepdims=True)
        for g in range(groups):
            share_s[g, i // 2, i % 2] = jnp.broadcast_to(
                share[g * sub:(g + 1) * sub], (sub, share_s.shape[4])
            )

    def lines(g):
        for dz in range(1, columns):
            zz = flip(z, dz)
            arrived(tok_buf.at[h, g, zz, y, parity], line_rs.at[g, dz])
            spread(g, dz)

    def gathered(g):
        for far in range(2):
            for k, ph, yy in ((0, h, 1 - y), (1, other, y), (2, other, 1 - y)):
                slots = tok_buf.at[ph, g, blocks(far), yy, parity]
                arrived(slots, quad_rs.at[g, k, far])
                send(slots, slots, twin_ss, twin_rs.at[g, ph], sibling, h)

    def twins(g, ph):
        arrived(tok_buf.at[ph, g, :, :, 0], twin_rs.at[g, ph])

    def column_tiles(size):
        return [slice(i, i + size) for i in range(0, hidden, size)]

    def own_rows(g):
        at = pl.ds(g * rows, rows)
        depth = pl.ds(pl.multiple_of(h * width, width), width)
        for cols in column_tiles(block_of(hidden, 256)):
            x = tok_buf[h, g].reshape(rows, width)
            gate_v[at, cols] = dot(x, wg[depth, cols])
            up_v[at, cols] = dot(x, wu[depth, cols])

    def hidden_rows(g, first, last):
        at = pl.ds(g * rows, rows)
        depth = pl.ds(pl.multiple_of(other * width, width), width)
        every = column_tiles(block_of(hidden, 256))
        for cols in every[first * len(every) // 3:last * len(every) // 3]:
            x = tok_buf[other, g].reshape(rows, width)
            gate = gate_v[at, cols] + dot(x, wg[depth, cols])
            up = up_v[at, cols] + dot(x, wu[depth, cols])
            gate_v[at, cols] = gate
            up_v[at, cols] = up
            hid[at, cols] = (gate / (1.0 + jnp.exp(-gate)) * up).astype(jnp.bfloat16)

    def down(g, far):
        start = (other if far else h) * width

        def down_step(cols, size):
            at = pl.ds(pl.multiple_of(cols.start + start, size), size)
            part = dot(hid[pl.ds(g * rows, rows), :], wd[:, at])
            osend[g, far, :, :, :, cols] = part.reshape(chips, 2, sub, size).astype(jnp.bfloat16)

        tiles(width, down_step, 1024)

    def straight(g, d):
        return g == 0 and d == chips - 1

    def cross_parts(g):
        for d in outer + [0]:
            pm = flip(chip, d)
            if straight(g, d):
                for q in range(2):
                    send(
                        osend.at[g, 1, pm, q], xmore.at[parity],
                        part_ss, out_rs.at[g, d], 2 * pm + q, other,
                    )
            else:
                send(osend.at[g, 1, pm], orecv.at[g, pm], part_ss, part_rs.at[g, d], e, other)

    def own_parts(g):
        pm = flip(chip, chips - 1)
        for q in range(2):
            send(
                osend.at[g, 0, pm, q], xrecv.at[g, chip, parity],
                out_ss.at[0], out_rs.at[g, chips - 1], 2 * pm + q, h,
            )

    def forward(g, first, last):
        for d in (outer + [0])[first:last]:
            if straight(g, d):
                continue
            pm = flip(chip, d)
            arrived(orecv.at[g, pm], part_rs.at[g, d])
            total = osend[g, 0, pm].astype(jnp.float32) + orecv[g, pm].astype(jnp.float32)
            ored[g, pm] = total.astype(jnp.bfloat16)
            home = xrecv.at[g, chip, parity]
            if d:
                for q in range(2):
                    send(ored.at[g, pm, q], home, out_ss.at[0], out_rs.at[g, d], 2 * pm + q, h)
            else:
                send(ored.at[g, pm, 1 - parity], home, out_ss.at[1], out_rs.at[g, d], sibling, h)
                xrecv[g, chip, parity] = ored[g, chip, parity]

    same = (
        lax.rem(lax.broadcasted_iota(jnp.int32, (sub, rows), 1), sub)
        == lax.broadcasted_iota(jnp.int32, (sub, rows), 0)
    ).astype(jnp.float32)
    apart = (
        lax.div(lax.broadcasted_iota(jnp.int32, (n, rows), 1), sub)
        != lax.broadcasted_iota(jnp.int32, (n, rows), 0)
    ).astype(jnp.float32)

    def share_of(g, pm):
        return share_s[g, pm][:, :, :1]

    def taken(g, first, last):
        part = jnp.zeros((sub, width), jnp.float32)
        for d in range(first, last):
            pm = flip(chip, d)
            share = share_of(g, pm)
            result = xrecv.at[g, pl.ds(0, 2)] if straight(g, d) else xrecv.at[g, pm]
            arrived(result if d else xrecv.at[g, chip, 1 - parity], out_rs.at[g, d])
            value = xrecv[g, pm].astype(jnp.float32)
            if straight(g, d):
                value = (value + xmore[...].astype(jnp.float32)).astype(jnp.bfloat16).astype(jnp.float32)
            value = jnp.where(share > 0.0, value, 0.0)
            xs[g, pm] = value.astype(jnp.bfloat16)
            part = part + jnp.sum(share * value, axis=0)
        layer_s[g] = layer_s[g] + part if first else part

    def products(g):
        x_all = xs[g].reshape(rows, width)
        gram = dot_t(x_all, x_all).reshape(n, sub, rows) * same[None]
        gram_s[g, h] = jnp.sum(gram, axis=1)
        send(gram_s.at[g, h], gram_s.at[g, h], gram_ss, gram_rs.at[g], e, other)

    def mix(g):
        arrived(gram_s.at[g, other], gram_rs.at[g])
        whole = (gram_s[g, 0] + gram_s[g, 1]) * (apart * (orth_weight / math.sqrt(full)))
        x_all = xs[g].reshape(rows, width)
        coeffs = (whole[:, None, :] * same[None]).reshape(rows, rows)
        mixed = dot(coeffs.astype(jnp.bfloat16), x_all).reshape(chips, 2, sub, width)
        upstream = up_ref[g].astype(jnp.float32)
        real = pad[g * sub:(g + 1) * sub]
        for i in range(chips):
            gsend[g, i] = (
                real[None] * (share_of(g, i) * upstream[None] + mixed[i])
            ).astype(jnp.bfloat16)
        slot = grows.at[h, g, chip, parity]
        send(gsend.at[g, chip, 1 - parity], slot, grad_ss.at[1], grad_rs.at[g, 0], sibling, h)
        send(gsend.at[g, chip, parity], slot, relay_ss, relay_rs.at[g], e, other)
        for d in near:
            pm = flip(chip, d)
            for q in range(2):
                send(gsend.at[g, pm, q], slot, grad_ss.at[0], grad_rs.at[g, d], 2 * pm + q, h)
        grows[h, g, chip, parity] = gsend[g, chip, parity]

    def relay(g, first, last):
        for d in range(first, last):
            slot = grows.at[h, g, flip(chip, d)] if d else grows.at[h, g, chip, 1 - parity]
            arrived(slot, grad_rs.at[g, d])
            send(slot, slot, relay_ss, relay_rs.at[g], e, other)

    def act(g, dh):
        ph = lax.rem(h + dh, 2)
        at = pl.ds(g * rows, rows)
        if dh:
            arrived(grows.at[other, g], relay_rs.at[g])

        depth = pl.ds(pl.multiple_of(ph * width, width), width)
        for cols in column_tiles(block_of(hidden, 384)):
            part = dot(grows[ph, g].reshape(rows, width), wd_t[depth, cols])
            if dh:
                part = part + act_v[at, cols]
                gate = gate_v[at, cols]
                sigma = 1.0 / (1.0 + jnp.exp(-gate))
                gg[at, cols] = (
                    part * up_v[at, cols] * sigma * (1.0 + gate * (1.0 - sigma))
                ).astype(jnp.bfloat16)
                gu[at, cols] = (part * gate * sigma).astype(jnp.bfloat16)
            else:
                act_v[at, cols] = part

    def turn(first, last):
        for i in range(first, last):
            at = slice((i // 3) * half_width, (i // 3 + 1) * half_width)
            if i % 3 == 0:
                wd_t[at, :] = wd[:, at].T
            elif i % 3 == 1:
                wg_t[:, at] = wg[at, :].T
            else:
                wu_t[:, at] = wu[at, :].T

    left, right = slice(0, half_width), slice(half_width, width)

    def back(g, far):
        rows_at = pl.ds(g * rows, rows)
        start = (other if far else h) * width
        for k, cols in ((0, left), (1, right)) if far else ((1, right), (0, left)):
            at = pl.ds(pl.multiple_of(start + k * half_width, half_width), half_width)
            part = dot(gg[rows_at, :], wg_t[:, at]) + dot(gu[rows_at, :], wu_t[:, at])
            part = part.astype(jnp.bfloat16).reshape(columns, 2, 2, sub, half_width)
            for q in range(2):
                psend[g, far, k, q] = part[:, :, q]
            send(
                psend.at[g, far, k, 1 - parity], prec.at[g, far, k],
                pair_ss, pair_rs.at[g, far, k], sibling, h,
            )

    def pairs_left(g):
        arrived(prec.at[g, 1, 0], pair_rs.at[g, 1, 0])
        for dz in reversed(range(columns)):
            zz = flip(z, dz)
            lsend[g, zz] = (
                psend[g, 1, 0, parity, zz].astype(jnp.float32)
                + prec[g, 1, 0, zz].astype(jnp.float32)
            ).astype(jnp.bfloat16)
            send(lsend.at[g, zz], lrecv.at[g, zz], lpart_ss, line_rs.at[g, dz], e, other)

    def pairs_right(g):
        for far in (1, 0):
            arrived(prec.at[g, far, 1], pair_rs.at[g, far, 1])
            for k in (1, 0):
                zs = blocks(k)
                rsend[g, far, zs] = (
                    psend[g, far, 1, parity, zs, 1 - y].astype(jnp.float32)
                    + prec[g, far, 1, zs, 1 - y].astype(jnp.float32)
                ).astype(jnp.bfloat16)
                send(
                    rsend.at[g, far, zs], rrecv.at[g, far, zs],
                    rpart_ss, quad_rs.at[g, far, k], across, h,
                )

    def finish_left(g, dz):
        zz = flip(z, dz)
        total = (
            psend[g, 0, 0, parity, zz].astype(jnp.float32)
            + prec[g, 0, 0, zz].astype(jnp.float32)
        )
        arrived(lrecv.at[g, zz], line_rs.at[g, dz])
        lsum[g, zz] = (total + lrecv[g, zz].astype(jnp.float32)).astype(jnp.bfloat16)
        for dy in (1, 0):
            yy = flip(y, dy)
            if dz or dy:
                send(
                    lsum.at[g, zz, yy], lfin.at[g, chip],
                    fin_ss.at[0], quad_rs.at[g, 2, 0], 4 * zz + 2 * yy + parity, h,
                )
            else:
                lfin[g, chip] = lsum[g, z, y]

    def finish_right(g, far, k):
        zs = blocks(k)
        total = (
            psend[g, far, 1, parity, zs, y].astype(jnp.float32)
            + prec[g, far, 1, zs, y].astype(jnp.float32)
        )
        arrived(rrecv.at[g, far, zs], quad_rs.at[g, far, k])
        rsum[g, far, zs] = (total + rrecv[g, far, zs].astype(jnp.float32)).astype(jnp.bfloat16)
        for dz in reversed(range(k * block, (k + 1) * block)):
            zz = flip(z, dz)
            if dz or far:
                send(
                    rsum.at[g, far, zz], rfin.at[g, columns * h + z],
                    fin_ss.at[1], quad_rs.at[g, 2, 1], 4 * zz + 2 * y + parity, other if far else h,
                )
            else:
                rfin[g, columns * h + z] = rsum[g, far, z]

    def finish(g):
        arrived(prec.at[g, 0, 0], pair_rs.at[g, 0, 0])
        for k in (1, 0):
            for far in (1, 0):
                for dz in reversed(range((2 * k + far) * block // 2, (2 * k + far + 1) * block // 2)):
                    finish_left(g, dz)
                finish_right(g, far, k)

    def collect(g):
        arrived(lfin.at[g, pl.ds(0, chips - 1)], quad_rs.at[g, 2, 0])
        arrived(rfin.at[g, pl.ds(0, chips - 1)], quad_rs.at[g, 2, 1])
        return [jnp.sum(fin[g].astype(jnp.float32), axis=0) for fin in (lfin, rfin)]

    lines(0)
    lines(1)
    gathered(0)
    twins(0, h)
    for c in loads[-3:-1]:
        c.wait()
    own_rows(0)
    twins(0, other)
    hidden_rows(0, 0, 3)
    loads[-1].wait()
    down(0, 1)
    cross_parts(0)
    down(0, 0)
    own_parts(0)
    gathered(1)
    twins(1, h)
    own_rows(1)
    twins(1, other)
    hidden_rows(1, 0, 2)
    forward(0, 0, chips // 8)
    hidden_rows(1, 2, 3)
    forward(0, chips // 8, 3 * chips // 8)
    down(1, 1)
    cross_parts(1)
    turn(0, 1)
    forward(0, 3 * chips // 8, chips // 2)
    turn(1, 2)
    forward(0, chips // 2, 5 * chips // 8)
    turn(2, 3)
    forward(0, 5 * chips // 8, 3 * chips // 4)
    turn(3, 4)
    forward(0, 3 * chips // 4, 7 * chips // 8)
    turn(4, 5)
    forward(0, 7 * chips // 8, chips)
    down(1, 0)
    forward(1, 0, chips // 8)
    turn(5, 6)
    forward(1, chips // 8, chips // 4)
    taken(0, 0, chips // 2)
    forward(1, chips // 4, 3 * chips // 8)
    taken(0, chips // 2, chips)
    products(0)
    forward(1, 3 * chips // 8, 5 * chips // 8)
    turn(6, 7)
    forward(1, 5 * chips // 8, 3 * chips // 4)
    turn(7, 8)
    forward(1, 3 * chips // 4, 7 * chips // 8)
    turn(8, 9)
    forward(1, 7 * chips // 8, chips)
    mix(0)
    turn(9, 12)
    taken(1, 0, chips)
    products(1)
    relay(0, 0, 3 * chips // 8)
    mix(1)
    layer_ref[...] = layer_s[...].reshape(tok, width).astype(jnp.bfloat16)
    relay(0, 3 * chips // 8, chips)
    relay(1, 0, 5 * chips // 8)
    act(0, 0)
    relay(1, 5 * chips // 8, 6 * chips // 8)
    act(0, 1)
    relay(1, 6 * chips // 8, chips)
    back(0, 1)
    back(0, 0)
    pairs_left(0)
    act(1, 0)
    pairs_right(0)
    act(1, 1)
    back(1, 1)
    back(1, 0)
    pairs_left(1)
    finish(0)
    pairs_right(1)
    finish(1)
    total_a = collect(0)
    total_b = collect(1)
    for k, at in enumerate((left, right)):
        gtok_ref[:, at] = jnp.concatenate([total_a[k], total_b[k]], axis=0).astype(jnp.bfloat16)
    drained(tok_buf.at[0, :, pl.ds(0, columns - 1), 0, 0], line_ss)
    for k in range(3):
        drained(tok_buf.at[0, :, :, 0, 0], quad_ss.at[k])
    drained(tok_buf.at[0], twin_ss)
    drained(osend.at[:, 1], part_ss)
    drained(ored.at[:, pl.ds(0, chips - 1)], out_ss.at[0])
    drained(ored.at[:, 0, 0], out_ss.at[1])
    drained(gram_s.at[:, 0], gram_ss)
    drained(gsend.at[:, pl.ds(0, chips - 1)], grad_ss.at[0])
    drained(gsend.at[:, 0, 0], grad_ss.at[1])
    drained(grows.at[0], relay_ss)
    drained(psend.at[:, :, :, 0], pair_ss)
    drained(lsend, lpart_ss)
    drained(rsend, rpart_ss)
    drained(lfin.at[:, pl.ds(0, chips - 1)], fin_ss.at[0])
    drained(rfin.at[:, pl.ds(0, chips - 1)], fin_ss.at[1])


def fused(tokens, upstream, expert_ids, gate_probs, pad_mask, gate_weight, up_weight, down_weight):
    n, groups = lax.axis_size("expert"), 2
    tok, width = tokens.shape
    hidden = gate_weight.shape[2]
    sub, full, chips = tok // groups, 2 * width, n // 2
    columns, every = chips // 2, n * tok
    top = expert_ids.shape[1]
    low, wide = jnp.bfloat16, jnp.float32
    vmem, dma = pltpu.VMEM, pltpu.SemaphoreType.DMA
    local = pl.BlockSpec(memory_space=pltpu.VMEM)
    remain = pl.BlockSpec(memory_space=pl.ANY)
    outs = pl.pallas_call(
        functools.partial(fused_kernel, n, groups),
        out_shape=[vmem((tok, width), low)] * 2,
        in_specs=[remain] * 8,
        out_specs=[local] * 2,
        scratch_shapes=[
            vmem((groups, sub, width), low),
            vmem((top, tok), jnp.int32),
            vmem((top, tok), wide),
            vmem((1, tok), jnp.int32),
            vmem((2, groups, columns, 2, 2, sub, width), low),
            vmem((full, hidden), low),
            vmem((full, hidden), low),
            vmem((hidden, full), low),
            vmem((every, hidden), wide),
            vmem((every, hidden), wide),
            vmem((every, hidden), wide),
            vmem((every, hidden), low),
            vmem((every, hidden), low),
            vmem((every, hidden), low),
            vmem((hidden, full), low),
            vmem((hidden, full), low),
            vmem((full, hidden), low),
            vmem((groups, 2, chips, 2, sub, width), low),
            vmem((groups, chips, 2, sub, width), low),
            vmem((groups, chips, 2, sub, width), low),
            vmem((groups, chips, 2, sub, width), low),
            vmem((2, sub, width), low),
            vmem((groups, chips, 2, sub, width), low),
            vmem((groups, 2, n, n * sub), wide),
            vmem((groups, chips, 2, sub, 128), wide),
            vmem((groups, sub, width), wide),
            vmem((groups, chips, 2, sub, width), low),
            vmem((2, groups, chips, 2, sub, width), low),
            vmem((groups, 2, 2, 2, columns, 2, sub, width // 2), low),
            vmem((groups, 2, 2, columns, 2, sub, width // 2), low),
            vmem((groups, columns, 2, sub, width // 2), low),
            vmem((groups, columns, 2, sub, width // 2), low),
            vmem((groups, columns, 2, sub, width // 2), low),
            vmem((groups, chips, sub, width // 2), low),
            vmem((groups, 2, columns, sub, width // 2), low),
            vmem((groups, 2, columns, sub, width // 2), low),
            vmem((groups, 2, columns, sub, width // 2), low),
            vmem((groups, chips, sub, width // 2), low),
            dma((2 * groups + 6,)),
            dma(()),
            dma((3,)),
            dma(()),
            dma((groups, columns)),
            dma((groups, 3, 2)),
            dma((groups, 2)),
            dma(()),
            dma((groups, chips)),
            dma((2,)),
            dma((groups, chips)),
            dma(()),
            dma((groups,)),
            dma((2,)),
            dma((groups, chips)),
            dma(()),
            dma((groups,)),
            dma(()),
            dma((groups, 2, 2)),
            dma(()),
            dma(()),
            dma((2,)),
        ],
        compiler_params=pltpu.CompilerParams(
            collective_id=0, has_side_effects=True, vmem_limit_bytes=56 * 1024 * 1024,
        ),
        name="experts",
    )(
        tokens, upstream, expert_ids.T, gate_probs.T, pad_mask.reshape(1, tok),
        gate_weight, up_weight, down_weight,
    )
    result = [jax.ShapeDtypeStruct((tok, width), low)] * 2
    return pl.pallas_call(
        copy_kernel, out_shape=result, in_specs=[local] * 2, out_specs=[local] * 2, name="results"
    )(*[pltpu.with_memory_space_constraint(out, pltpu.VMEM) for out in outs])


def shards(tokens, upstream, expert_ids, gate_probs, pad_mask, gate_weight, up_weight, down_weight):
    tok_count, top_count = expert_ids.shape
    experts = lax.axis_size("expert")
    capacity = min(tok_count, 2 * tok_count * top_count // experts)
    paired = experts > 15 and experts & (experts - 1) == 0 and lax.axis_size("half") == 2
    if capacity == tok_count and tok_count % 16 == 0 and paired:
        return fused(
            tokens, upstream, expert_ids, gate_probs, pad_mask, gate_weight, up_weight, down_weight
        )
    slots_total = experts * capacity
    full_width = tokens.shape[1] * lax.axis_size("half")
    slot_dest = assign_slots(expert_ids, experts, capacity)
    place_items = placement_matrix(slot_dest, slots_total)
    place_tokens = jnp.sum(place_items.reshape(slots_total, tok_count, top_count), axis=2)
    weight_gate = gate_weight[0]
    weight_up = up_weight[0]
    weight_down = down_weight[0]
    rows_in = to_experts(place_tokens, tokens)
    gate_val = jnp.dot(rows_in, weight_gate, preferred_element_type=jnp.float32)
    up_val = jnp.dot(rows_in, weight_up, preferred_element_type=jnp.float32)
    hidden_act = (jax.nn.silu(gate_val) * up_val).astype(jnp.bfloat16)
    partial_value = jnp.dot(hidden_act, weight_down, preferred_element_type=jnp.float32)
    out_home = to_homes(partial_value)
    outputs = jnp.take(out_home, slot_dest, axis=0).reshape(tok_count, top_count, -1)
    out_float = outputs.astype(jnp.float32)
    shares = gate_probs / jnp.sum(gate_probs, axis=1, keepdims=True)
    layer_out = jnp.sum(shares[:, :, None] * out_float, axis=1).astype(jnp.bfloat16)
    gram_part = jnp.einsum("tjd,tkd->tjk", out_float, out_float) / math.sqrt(full_width)
    gram = lax.psum(gram_part, "half")
    off_diag = 1.0 - jnp.eye(top_count, dtype=jnp.float32)
    coeffs = orth_weight * gram * off_diag
    grad_out = pad_mask.astype(jnp.float32)[:, None, None] * (
        shares[:, :, None] * upstream.astype(jnp.float32)[:, None, :]
        + jnp.einsum("tjk,tkd->tjd", coeffs, out_float)
    )
    grad_items = grad_out.astype(jnp.bfloat16).reshape(tok_count * top_count, -1)
    grad_rows = to_experts(place_items, grad_items)
    grad_act = jnp.einsum("rd,hd->rh", grad_rows, weight_down, preferred_element_type=jnp.float32)
    sigma = jax.nn.sigmoid(gate_val)
    grad_gate = (grad_act * up_val * sigma * (1.0 + gate_val * (1.0 - sigma))).astype(jnp.bfloat16)
    grad_up = (grad_act * gate_val * sigma).astype(jnp.bfloat16)
    grad_partial = jnp.einsum(
        "rh,dh->rd", grad_gate, weight_gate, preferred_element_type=jnp.float32
    )
    grad_partial = grad_partial + jnp.einsum(
        "rh,dh->rd", grad_up, weight_up, preferred_element_type=jnp.float32
    )
    grad_home = to_homes(grad_partial)
    grad_pairs = jnp.take(grad_home, slot_dest, axis=0).reshape(tok_count, top_count, -1)
    grad_tokens = jnp.sum(grad_pairs.astype(jnp.float32), axis=1).astype(jnp.bfloat16)
    return (layer_out, grad_tokens)


def solution(mesh):
    in_specs = (
        P("expert", "half"),
        P("expert", "half"),
        P("expert", None),
        P("expert", None),
        P("expert"),
        P("expert", None, "half"),
        P("expert", None, "half"),
        P("expert", "half", None),
    )
    out_specs = (P("expert", "half"), P("expert", "half"))
    return jax.shard_map(shards, mesh=mesh, in_specs=in_specs, out_specs=out_specs, check_vma=False)
```

```python
import functools
import math

import jax
import jax.numpy as jnp
from jax import lax
from jax.experimental import pallas as pl
from jax.experimental.pallas import tpu as pltpu
from jax.sharding import PartitionSpec as P

orth_weight = 0.25


def assign_slots(expert_ids, experts, capacity):
    tok_count, top_count = expert_ids.shape
    flat_ids = expert_ids.reshape(tok_count * top_count)
    onehot = (flat_ids[:, None] == jnp.arange(experts, dtype=jnp.int32)[None, :]).astype(jnp.int32)
    before = jnp.cumsum(onehot, axis=0) - onehot
    slot_index = jnp.sum(before * onehot, axis=1)
    return flat_ids * capacity + slot_index


def placement_matrix(slot_dest, slots_total):
    row_index = jnp.arange(slots_total, dtype=jnp.int32)
    return (row_index[:, None] == slot_dest[None, :]).astype(jnp.bfloat16)


def to_experts(place, items):
    whole = lax.all_gather(items, "half", axis=1, tiled=True)
    buckets = jnp.dot(place, whole, preferred_element_type=jnp.float32).astype(jnp.bfloat16)
    return lax.all_to_all(buckets, "expert", split_axis=0, concat_axis=0, tiled=True)


def to_homes(partial_value):
    summed = lax.psum_scatter(
        partial_value.astype(jnp.bfloat16), "half", scatter_dimension=1, tiled=True
    )
    return lax.all_to_all(summed, "expert", split_axis=0, concat_axis=0, tiled=True)


def block_of(width, most):
    return next((b for b in (1024, 512, 384, 256, 128) if b <= most and width % b == 0), width)


def tiles(width, body, most=256):
    size = block_of(width, most)

    def step(j, carry):
        body(pl.ds(pl.multiple_of(j * size, size), size), size)
        return carry

    lax.fori_loop(0, width // size, step, 0)


def dot(a, b):
    return jnp.dot(a, b, preferred_element_type=jnp.float32)


def dot_t(a, b):
    return lax.dot_general(a, b, (((1,), (1,)), ((), ())), preferred_element_type=jnp.float32)


def copy_kernel(a_ref, b_ref, a_out, b_out):
    a_out[...] = a_ref[...]
    b_out[...] = b_ref[...]


def fused_kernel(
    n, groups,
    tok_hbm, up_hbm, ids_hbm, probs_hbm, pad_hbm, wg_hbm, wu_hbm, wd_hbm,
    layer_ref, gtok_ref,
    up_ref, ids_ref, probs_ref, pad_ref,
    tok_buf, wg, wu, wd, gate_v, up_v, act_v, hid, gg, gu,
    wg_t, wu_t, wd_t,
    osend, orecv, ored, xrecv, xmore, xs, gram_s, share_s, layer_s, gsend, grows, psend, prec,
    lsend, lrecv, lsum, lfin, rsend, rrecv, rsum, rfin,
    w_sem, line_ss, quad_ss, twin_ss, line_rs, quad_rs, twin_rs, part_ss, part_rs, out_ss, out_rs,
    gram_ss, gram_rs, grad_ss, grad_rs, relay_ss, relay_rs, pair_ss, pair_rs, lpart_ss, rpart_ss, fin_ss,
):
    e = lax.axis_index("expert")
    h = lax.axis_index("half")
    sub, width = tok_buf.shape[5:]
    hidden = wg.shape[1]
    tok = groups * sub
    rows = n * sub
    chips = n // 2
    columns = chips // 2
    parity = lax.rem(e, 2)
    chip = lax.div(e, 2)
    y = lax.rem(chip, 2)
    z = lax.div(chip, 2)
    sibling = e + 1 - 2 * parity
    other = 1 - h
    full = 2 * width
    half_width = width // 2
    block = columns // 2
    own_block = lax.div(z, block)

    def blocks(far):
        return pl.ds((1 - own_block if far else own_block) * block, block)

    def remote(src, dst, ssem, rsem, pe, ph):
        return pltpu.make_async_remote_copy(
            src_ref=src, dst_ref=dst, send_sem=ssem, recv_sem=rsem,
            device_id=(pe, ph), device_id_type=pl.DeviceIdType.MESH,
        )

    def send(*args):
        remote(*args).start()

    def flip(a, d):
        bit = 1
        out = a
        while bit <= d:
            if d & bit:
                out = out + bit * (1 - 2 * lax.rem(lax.div(a, bit), 2))
            bit *= 2
        return out

    def arrived(slot, rsem):
        remote(slot, slot, line_ss, rsem, sibling, h).wait_recv()

    def drained(sent, ssem):
        remote(sent, sent, ssem, twin_rs.at[0, 0], sibling, h).wait_send()

    moves = [(tok_hbm.at[pl.ds(g * sub, sub)], tok_buf.at[h, g, z, y, parity]) for g in range(groups)]
    moves += [(ids_hbm, ids_ref), (probs_hbm, probs_ref), (pad_hbm, pad_ref)]
    moves += [(up_hbm.at[pl.ds(g * sub, sub)], up_ref.at[g]) for g in range(groups)]
    moves += [(wg_hbm.at[0], wg), (wu_hbm.at[0], wu), (wd_hbm.at[0], wd)]
    loads = [pltpu.make_async_copy(src, dst, w_sem.at[i]) for i, (src, dst) in enumerate(moves)]
    for c in loads:
        c.start()

    near = list(range(1, chips))
    outer = near[::-1]

    across = 4 * z + 2 * (1 - y) + parity
    barrier = pltpu.get_barrier_semaphore()
    partners = [(4 * flip(z, dz) + 2 * y + parity, h) for dz in reversed(range(1, columns))]
    partners += [(across, other), (across, h), (e, other), (sibling, h)]
    for partner in partners:
        pl.semaphore_signal(
            barrier, inc=1, device_id=partner, device_id_type=pl.DeviceIdType.MESH
        )
    pl.semaphore_wait(barrier, len(partners))

    def spread(g, dz):
        slot = tok_buf.at[h, g, flip(z, dz), y, parity]
        k = dz // block
        send(slot, slot, quad_ss.at[2], quad_rs.at[g, 2, k], across, other)
        send(slot, slot, quad_ss.at[0], quad_rs.at[g, 0, k], across, h)
        send(slot, slot, quad_ss.at[1], quad_rs.at[g, 1, k], e, other)
        send(slot, slot, twin_ss, twin_rs.at[g, h], sibling, h)

    for g in range(groups):
        loads[g].wait()
        mine = tok_buf.at[h, g, z, y, parity]
        for dz in reversed(range(1, columns)):
            send(mine, mine, line_ss, line_rs.at[g, dz], 4 * flip(z, dz) + 2 * y + parity, h)
        spread(g, 0)

    for c in loads[groups:-3]:
        c.wait()
    eye = (
        lax.broadcasted_iota(jnp.int32, (tok, tok), 0)
        == lax.broadcasted_iota(jnp.int32, (tok, tok), 1)
    )
    top = ids_ref.shape[0]
    lane = lax.broadcasted_iota(jnp.int32, (tok, top), 1)

    def column(row):
        return jnp.sum(jnp.where(eye, jnp.broadcast_to(row, (tok, tok)), 0.0), axis=1, keepdims=True)

    ids = jnp.zeros((tok, top), jnp.float32)
    probs = jnp.zeros((tok, top), jnp.float32)
    for j in range(top):
        ids = jnp.where(lane == j, column(ids_ref[j:j + 1, :].astype(jnp.float32)), ids)
        probs = jnp.where(lane == j, column(probs_ref[j:j + 1, :]), probs)
    pad = column(pad_ref[...].astype(jnp.float32))
    shares = probs / jnp.sum(probs, axis=1, keepdims=True)
    for i in range(n):
        share = jnp.sum(jnp.where(ids == float(i), shares, 0.0), axis=1, keepdims=True)
        for g in range(groups):
            share_s[g, i // 2, i % 2] = jnp.broadcast_to(
                share[g * sub:(g + 1) * sub], (sub, share_s.shape[4])
            )

    def lines(g):
        for dz in range(1, columns):
            zz = flip(z, dz)
            arrived(tok_buf.at[h, g, zz, y, parity], line_rs.at[g, dz])
            spread(g, dz)

    def gathered(g):
        for far in range(2):
            for k, ph, yy in ((0, h, 1 - y), (1, other, y), (2, other, 1 - y)):
                slots = tok_buf.at[ph, g, blocks(far), yy, parity]
                arrived(slots, quad_rs.at[g, k, far])
                send(slots, slots, twin_ss, twin_rs.at[g, ph], sibling, h)

    def twins(g, ph):
        arrived(tok_buf.at[ph, g, :, :, 0], twin_rs.at[g, ph])

    def column_tiles(size):
        return [slice(i, i + size) for i in range(0, hidden, size)]

    def own_rows(g):
        at = pl.ds(g * rows, rows)
        depth = pl.ds(pl.multiple_of(h * width, width), width)
        for cols in column_tiles(block_of(hidden, 256)):
            x = tok_buf[h, g].reshape(rows, width)
            gate_v[at, cols] = dot(x, wg[depth, cols])
            up_v[at, cols] = dot(x, wu[depth, cols])

    def hidden_rows(g, first, last):
        at = pl.ds(g * rows, rows)
        depth = pl.ds(pl.multiple_of(other * width, width), width)
        every = column_tiles(block_of(hidden, 256))
        for cols in every[first * len(every) // 3:last * len(every) // 3]:
            x = tok_buf[other, g].reshape(rows, width)
            gate = gate_v[at, cols] + dot(x, wg[depth, cols])
            up = up_v[at, cols] + dot(x, wu[depth, cols])
            gate_v[at, cols] = gate
            up_v[at, cols] = up
            hid[at, cols] = (gate / (1.0 + jnp.exp(-gate)) * up).astype(jnp.bfloat16)

    def down(g, far):
        start = (other if far else h) * width

        def down_step(cols, size):
            at = pl.ds(pl.multiple_of(cols.start + start, size), size)
            part = dot(hid[pl.ds(g * rows, rows), :], wd[:, at])
            osend[g, far, :, :, :, cols] = part.reshape(chips, 2, sub, size).astype(jnp.bfloat16)

        tiles(width, down_step, 1024)

    def straight(g, d):
        return g == 0 and d == chips - 1

    def cross_parts(g):
        for d in outer + [0]:
            pm = flip(chip, d)
            if straight(g, d):
                for q in range(2):
                    send(
                        osend.at[g, 1, pm, q], xmore.at[parity],
                        part_ss, out_rs.at[g, d], 2 * pm + q, other,
                    )
            else:
                send(osend.at[g, 1, pm], orecv.at[g, pm], part_ss, part_rs.at[g, d], e, other)

    def own_parts(g):
        pm = flip(chip, chips - 1)
        for q in range(2):
            send(
                osend.at[g, 0, pm, q], xrecv.at[g, chip, parity],
                out_ss.at[0], out_rs.at[g, chips - 1], 2 * pm + q, h,
            )

    def forward(g, first, last):
        for d in (outer + [0])[first:last]:
            if straight(g, d):
                continue
            pm = flip(chip, d)
            arrived(orecv.at[g, pm], part_rs.at[g, d])
            total = osend[g, 0, pm].astype(jnp.float32) + orecv[g, pm].astype(jnp.float32)
            ored[g, pm] = total.astype(jnp.bfloat16)
            home = xrecv.at[g, chip, parity]
            if d:
                for q in range(2):
                    send(ored.at[g, pm, q], home, out_ss.at[0], out_rs.at[g, d], 2 * pm + q, h)
            else:
                send(ored.at[g, pm, 1 - parity], home, out_ss.at[1], out_rs.at[g, d], sibling, h)
                xrecv[g, chip, parity] = ored[g, chip, parity]

    same = (
        lax.rem(lax.broadcasted_iota(jnp.int32, (sub, rows), 1), sub)
        == lax.broadcasted_iota(jnp.int32, (sub, rows), 0)
    ).astype(jnp.float32)
    apart = (
        lax.div(lax.broadcasted_iota(jnp.int32, (n, rows), 1), sub)
        != lax.broadcasted_iota(jnp.int32, (n, rows), 0)
    ).astype(jnp.float32)

    def share_of(g, pm):
        return share_s[g, pm][:, :, :1]

    def taken(g, first, last, fresh):
        part = jnp.zeros((sub, width), jnp.float32)
        for d in range(first, last):
            pm = flip(chip, d)
            share = share_of(g, pm)
            result = xrecv.at[g, pl.ds(0, 2)] if straight(g, d) else xrecv.at[g, pm]
            arrived(result if d else xrecv.at[g, chip, 1 - parity], out_rs.at[g, d])
            value = xrecv[g, pm].astype(jnp.float32)
            if straight(g, d):
                value = (value + xmore[...].astype(jnp.float32)).astype(jnp.bfloat16).astype(jnp.float32)
            value = jnp.where(share > 0.0, value, 0.0)
            xs[g, pm] = value.astype(jnp.bfloat16)
            part = part + jnp.sum(share * value, axis=0)
        layer_s[g] = part if fresh else layer_s[g] + part

    def products(g):
        x_all = xs[g].reshape(rows, width)
        gram = dot_t(x_all, x_all).reshape(n, sub, rows) * same[None]
        gram_s[g, h] = jnp.sum(gram, axis=1)
        send(gram_s.at[g, h], gram_s.at[g, h], gram_ss, gram_rs.at[g], e, other)

    def mix(g):
        arrived(gram_s.at[g, other], gram_rs.at[g])
        whole = (gram_s[g, 0] + gram_s[g, 1]) * (apart * (orth_weight / math.sqrt(full)))
        x_all = xs[g].reshape(rows, width)
        coeffs = (whole[:, None, :] * same[None]).reshape(rows, rows)
        mixed = dot(coeffs.astype(jnp.bfloat16), x_all).reshape(chips, 2, sub, width)
        upstream = up_ref[g].astype(jnp.float32)
        real = pad[g * sub:(g + 1) * sub]
        for i in range(chips):
            gsend[g, i] = (
                real[None] * (share_of(g, i) * upstream[None] + mixed[i])
            ).astype(jnp.bfloat16)
        slot = grows.at[h, g, chip, parity]
        send(gsend.at[g, chip, 1 - parity], slot, grad_ss.at[1], grad_rs.at[g, 0], sibling, h)
        send(gsend.at[g, chip, parity], slot, relay_ss, relay_rs.at[g], e, other)
        for d in near:
            pm = flip(chip, d)
            for q in range(2):
                send(gsend.at[g, pm, q], slot, grad_ss.at[0], grad_rs.at[g, d], 2 * pm + q, h)
        grows[h, g, chip, parity] = gsend[g, chip, parity]

    def relay(g, first, last):
        for d in range(first, last):
            slot = grows.at[h, g, flip(chip, d)] if d else grows.at[h, g, chip, 1 - parity]
            arrived(slot, grad_rs.at[g, d])
            send(slot, slot, relay_ss, relay_rs.at[g], e, other)

    def act(g, dh):
        ph = lax.rem(h + dh, 2)
        at = pl.ds(g * rows, rows)
        if dh:
            arrived(grows.at[other, g], relay_rs.at[g])

        depth = pl.ds(pl.multiple_of(ph * width, width), width)
        for cols in column_tiles(block_of(hidden, 384)):
            part = dot(grows[ph, g].reshape(rows, width), wd_t[depth, cols])
            if dh:
                part = part + act_v[at, cols]
                gate = gate_v[at, cols]
                sigma = 1.0 / (1.0 + jnp.exp(-gate))
                gg[at, cols] = (
                    part * up_v[at, cols] * sigma * (1.0 + gate * (1.0 - sigma))
                ).astype(jnp.bfloat16)
                gu[at, cols] = (part * gate * sigma).astype(jnp.bfloat16)
            else:
                act_v[at, cols] = part

    def turn(first, last):
        for i in range(first, last):
            at = slice((i // 3) * half_width, (i // 3 + 1) * half_width)
            if i % 3 == 0:
                wd_t[at, :] = wd[:, at].T
            elif i % 3 == 1:
                wg_t[:, at] = wg[at, :].T
            else:
                wu_t[:, at] = wu[at, :].T

    left, right = slice(0, half_width), slice(half_width, width)

    def back(g, far):
        rows_at = pl.ds(g * rows, rows)
        start = (other if far else h) * width
        for k, cols in ((0, left), (1, right)) if far else ((1, right), (0, left)):
            at = pl.ds(pl.multiple_of(start + k * half_width, half_width), half_width)
            part = dot(gg[rows_at, :], wg_t[:, at]) + dot(gu[rows_at, :], wu_t[:, at])
            part = part.astype(jnp.bfloat16).reshape(columns, 2, 2, sub, half_width)
            for q in range(2):
                psend[g, far, k, q] = part[:, :, q]
            send(
                psend.at[g, far, k, 1 - parity], prec.at[g, far, k],
                pair_ss, pair_rs.at[g, far, k], sibling, h,
            )

    def pairs_left(g):
        arrived(prec.at[g, 1, 0], pair_rs.at[g, 1, 0])
        for dz in reversed(range(columns)):
            zz = flip(z, dz)
            lsend[g, zz] = (
                psend[g, 1, 0, parity, zz].astype(jnp.float32)
                + prec[g, 1, 0, zz].astype(jnp.float32)
            ).astype(jnp.bfloat16)
            send(lsend.at[g, zz], lrecv.at[g, zz], lpart_ss, line_rs.at[g, dz], e, other)

    def pairs_right(g):
        for far in (1, 0):
            arrived(prec.at[g, far, 1], pair_rs.at[g, far, 1])
            for k in (1, 0):
                zs = blocks(k)
                rsend[g, far, zs] = (
                    psend[g, far, 1, parity, zs, 1 - y].astype(jnp.float32)
                    + prec[g, far, 1, zs, 1 - y].astype(jnp.float32)
                ).astype(jnp.bfloat16)
                send(
                    rsend.at[g, far, zs], rrecv.at[g, far, zs],
                    rpart_ss, quad_rs.at[g, far, k], across, h,
                )

    def finish_left(g, dz):
        zz = flip(z, dz)
        total = (
            psend[g, 0, 0, parity, zz].astype(jnp.float32)
            + prec[g, 0, 0, zz].astype(jnp.float32)
        )
        arrived(lrecv.at[g, zz], line_rs.at[g, dz])
        lsum[g, zz] = (total + lrecv[g, zz].astype(jnp.float32)).astype(jnp.bfloat16)
        for dy in (1, 0):
            yy = flip(y, dy)
            if dz or dy:
                send(
                    lsum.at[g, zz, yy], lfin.at[g, chip],
                    fin_ss.at[0], quad_rs.at[g, 2, 0], 4 * zz + 2 * yy + parity, h,
                )
            else:
                lfin[g, chip] = lsum[g, z, y]

    def finish_right(g, far, k):
        zs = blocks(k)
        total = (
            psend[g, far, 1, parity, zs, y].astype(jnp.float32)
            + prec[g, far, 1, zs, y].astype(jnp.float32)
        )
        arrived(rrecv.at[g, far, zs], quad_rs.at[g, far, k])
        rsum[g, far, zs] = (total + rrecv[g, far, zs].astype(jnp.float32)).astype(jnp.bfloat16)
        for dz in reversed(range(k * block, (k + 1) * block)):
            zz = flip(z, dz)
            if dz or far:
                send(
                    rsum.at[g, far, zz], rfin.at[g, columns * h + z],
                    fin_ss.at[1], quad_rs.at[g, 2, 1], 4 * zz + 2 * y + parity, other if far else h,
                )
            else:
                rfin[g, columns * h + z] = rsum[g, far, z]

    def finish(g):
        arrived(prec.at[g, 0, 0], pair_rs.at[g, 0, 0])
        for k in (1, 0):
            for far in (1, 0):
                for dz in reversed(range((2 * k + far) * block // 2, (2 * k + far + 1) * block // 2)):
                    finish_left(g, dz)
                finish_right(g, far, k)

    def collect(g):
        arrived(lfin.at[g, pl.ds(0, chips - 1)], quad_rs.at[g, 2, 0])
        arrived(rfin.at[g, pl.ds(0, chips - 1)], quad_rs.at[g, 2, 1])
        return [jnp.sum(fin[g].astype(jnp.float32), axis=0) for fin in (lfin, rfin)]

    lines(0)
    lines(1)
    gathered(0)
    twins(0, h)
    for c in loads[-3:-1]:
        c.wait()
    own_rows(0)
    twins(0, other)
    hidden_rows(0, 0, 3)
    loads[-1].wait()
    down(0, 1)
    cross_parts(0)
    down(0, 0)
    own_parts(0)
    gathered(1)
    twins(1, h)
    own_rows(1)
    twins(1, other)
    hidden_rows(1, 0, 2)
    forward(0, 0, chips // 8)
    hidden_rows(1, 2, 3)
    forward(0, chips // 8, 3 * chips // 8)
    down(1, 1)
    cross_parts(1)
    turn(0, 1)
    forward(0, 3 * chips // 8, chips // 2)
    turn(1, 2)
    forward(0, chips // 2, 5 * chips // 8)
    turn(2, 3)
    forward(0, 5 * chips // 8, 3 * chips // 4)
    turn(3, 4)
    forward(0, 3 * chips // 4, 7 * chips // 8)
    turn(4, 5)
    forward(0, 7 * chips // 8, chips)
    down(1, 0)
    forward(1, 0, chips // 8)
    turn(5, 6)
    forward(1, chips // 8, chips // 4)
    taken(0, chips // 2, chips, True)
    forward(1, chips // 4, 3 * chips // 8)
    taken(0, 0, chips // 2, False)
    products(0)
    forward(1, 3 * chips // 8, 5 * chips // 8)
    turn(6, 7)
    forward(1, 5 * chips // 8, 3 * chips // 4)
    turn(7, 8)
    forward(1, 3 * chips // 4, 7 * chips // 8)
    turn(8, 9)
    forward(1, 7 * chips // 8, chips)
    mix(0)
    turn(9, 12)
    taken(1, 0, chips, True)
    products(1)
    relay(0, 0, 3 * chips // 8)
    mix(1)
    layer_ref[...] = layer_s[...].reshape(tok, width).astype(jnp.bfloat16)
    relay(0, 3 * chips // 8, chips)
    relay(1, 0, 5 * chips // 8)
    act(0, 0)
    relay(1, 5 * chips // 8, 6 * chips // 8)
    act(0, 1)
    relay(1, 6 * chips // 8, chips)
    back(0, 1)
    back(0, 0)
    pairs_left(0)
    act(1, 0)
    pairs_right(0)
    act(1, 1)
    back(1, 1)
    back(1, 0)
    pairs_left(1)
    finish(0)
    pairs_right(1)
    finish(1)
    total_a = collect(0)
    total_b = collect(1)
    for k, at in enumerate((left, right)):
        gtok_ref[:, at] = jnp.concatenate([total_a[k], total_b[k]], axis=0).astype(jnp.bfloat16)
    drained(tok_buf.at[0, :, pl.ds(0, columns - 1), 0, 0], line_ss)
    for k in range(3):
        drained(tok_buf.at[0, :, :, 0, 0], quad_ss.at[k])
    drained(tok_buf.at[0], twin_ss)
    drained(osend.at[:, 1], part_ss)
    drained(ored.at[:, pl.ds(0, chips - 1)], out_ss.at[0])
    drained(ored.at[:, 0, 0], out_ss.at[1])
    drained(gram_s.at[:, 0], gram_ss)
    drained(gsend.at[:, pl.ds(0, chips - 1)], grad_ss.at[0])
    drained(gsend.at[:, 0, 0], grad_ss.at[1])
    drained(grows.at[0], relay_ss)
    drained(psend.at[:, :, :, 0], pair_ss)
    drained(lsend, lpart_ss)
    drained(rsend, rpart_ss)
    drained(lfin.at[:, pl.ds(0, chips - 1)], fin_ss.at[0])
    drained(rfin.at[:, pl.ds(0, chips - 1)], fin_ss.at[1])


def fused(tokens, upstream, expert_ids, gate_probs, pad_mask, gate_weight, up_weight, down_weight):
    n, groups = lax.axis_size("expert"), 2
    tok, width = tokens.shape
    hidden = gate_weight.shape[2]
    sub, full, chips = tok // groups, 2 * width, n // 2
    columns, every = chips // 2, n * tok
    top = expert_ids.shape[1]
    low, wide = jnp.bfloat16, jnp.float32
    vmem, dma = pltpu.VMEM, pltpu.SemaphoreType.DMA
    local = pl.BlockSpec(memory_space=pltpu.VMEM)
    remain = pl.BlockSpec(memory_space=pl.ANY)
    outs = pl.pallas_call(
        functools.partial(fused_kernel, n, groups),
        out_shape=[vmem((tok, width), low)] * 2,
        in_specs=[remain] * 8,
        out_specs=[local] * 2,
        scratch_shapes=[
            vmem((groups, sub, width), low),
            vmem((top, tok), jnp.int32),
            vmem((top, tok), wide),
            vmem((1, tok), jnp.int32),
            vmem((2, groups, columns, 2, 2, sub, width), low),
            vmem((full, hidden), low),
            vmem((full, hidden), low),
            vmem((hidden, full), low),
            vmem((every, hidden), wide),
            vmem((every, hidden), wide),
            vmem((every, hidden), wide),
            vmem((every, hidden), low),
            vmem((every, hidden), low),
            vmem((every, hidden), low),
            vmem((hidden, full), low),
            vmem((hidden, full), low),
            vmem((full, hidden), low),
            vmem((groups, 2, chips, 2, sub, width), low),
            vmem((groups, chips, 2, sub, width), low),
            vmem((groups, chips, 2, sub, width), low),
            vmem((groups, chips, 2, sub, width), low),
            vmem((2, sub, width), low),
            vmem((groups, chips, 2, sub, width), low),
            vmem((groups, 2, n, n * sub), wide),
            vmem((groups, chips, 2, sub, 128), wide),
            vmem((groups, sub, width), wide),
            vmem((groups, chips, 2, sub, width), low),
            vmem((2, groups, chips, 2, sub, width), low),
            vmem((groups, 2, 2, 2, columns, 2, sub, width // 2), low),
            vmem((groups, 2, 2, columns, 2, sub, width // 2), low),
            vmem((groups, columns, 2, sub, width // 2), low),
            vmem((groups, columns, 2, sub, width // 2), low),
            vmem((groups, columns, 2, sub, width // 2), low),
            vmem((groups, chips, sub, width // 2), low),
            vmem((groups, 2, columns, sub, width // 2), low),
            vmem((groups, 2, columns, sub, width // 2), low),
            vmem((groups, 2, columns, sub, width // 2), low),
            vmem((groups, chips, sub, width // 2), low),
            dma((2 * groups + 6,)),
            dma(()),
            dma((3,)),
            dma(()),
            dma((groups, columns)),
            dma((groups, 3, 2)),
            dma((groups, 2)),
            dma(()),
            dma((groups, chips)),
            dma((2,)),
            dma((groups, chips)),
            dma(()),
            dma((groups,)),
            dma((2,)),
            dma((groups, chips)),
            dma(()),
            dma((groups,)),
            dma(()),
            dma((groups, 2, 2)),
            dma(()),
            dma(()),
            dma((2,)),
        ],
        compiler_params=pltpu.CompilerParams(
            collective_id=0, has_side_effects=True, vmem_limit_bytes=56 * 1024 * 1024,
        ),
        name="experts",
    )(
        tokens, upstream, expert_ids.T, gate_probs.T, pad_mask.reshape(1, tok),
        gate_weight, up_weight, down_weight,
    )
    result = [jax.ShapeDtypeStruct((tok, width), low)] * 2
    return pl.pallas_call(
        copy_kernel, out_shape=result, in_specs=[local] * 2, out_specs=[local] * 2, name="results"
    )(*[pltpu.with_memory_space_constraint(out, pltpu.VMEM) for out in outs])


def shards(tokens, upstream, expert_ids, gate_probs, pad_mask, gate_weight, up_weight, down_weight):
    tok_count, top_count = expert_ids.shape
    experts = lax.axis_size("expert")
    capacity = min(tok_count, 2 * tok_count * top_count // experts)
    paired = experts > 15 and experts & (experts - 1) == 0 and lax.axis_size("half") == 2
    if capacity == tok_count and tok_count % 16 == 0 and paired:
        return fused(
            tokens, upstream, expert_ids, gate_probs, pad_mask, gate_weight, up_weight, down_weight
        )
    slots_total = experts * capacity
    full_width = tokens.shape[1] * lax.axis_size("half")
    slot_dest = assign_slots(expert_ids, experts, capacity)
    place_items = placement_matrix(slot_dest, slots_total)
    place_tokens = jnp.sum(place_items.reshape(slots_total, tok_count, top_count), axis=2)
    weight_gate = gate_weight[0]
    weight_up = up_weight[0]
    weight_down = down_weight[0]
    rows_in = to_experts(place_tokens, tokens)
    gate_val = jnp.dot(rows_in, weight_gate, preferred_element_type=jnp.float32)
    up_val = jnp.dot(rows_in, weight_up, preferred_element_type=jnp.float32)
    hidden_act = (jax.nn.silu(gate_val) * up_val).astype(jnp.bfloat16)
    partial_value = jnp.dot(hidden_act, weight_down, preferred_element_type=jnp.float32)
    out_home = to_homes(partial_value)
    outputs = jnp.take(out_home, slot_dest, axis=0).reshape(tok_count, top_count, -1)
    out_float = outputs.astype(jnp.float32)
    shares = gate_probs / jnp.sum(gate_probs, axis=1, keepdims=True)
    layer_out = jnp.sum(shares[:, :, None] * out_float, axis=1).astype(jnp.bfloat16)
    gram_part = jnp.einsum("tjd,tkd->tjk", out_float, out_float) / math.sqrt(full_width)
    gram = lax.psum(gram_part, "half")
    off_diag = 1.0 - jnp.eye(top_count, dtype=jnp.float32)
    coeffs = orth_weight * gram * off_diag
    grad_out = pad_mask.astype(jnp.float32)[:, None, None] * (
        shares[:, :, None] * upstream.astype(jnp.float32)[:, None, :]
        + jnp.einsum("tjk,tkd->tjd", coeffs, out_float)
    )
    grad_items = grad_out.astype(jnp.bfloat16).reshape(tok_count * top_count, -1)
    grad_rows = to_experts(place_items, grad_items)
    grad_act = jnp.einsum("rd,hd->rh", grad_rows, weight_down, preferred_element_type=jnp.float32)
    sigma = jax.nn.sigmoid(gate_val)
    grad_gate = (grad_act * up_val * sigma * (1.0 + gate_val * (1.0 - sigma))).astype(jnp.bfloat16)
    grad_up = (grad_act * gate_val * sigma).astype(jnp.bfloat16)
    grad_partial = jnp.einsum(
        "rh,dh->rd", grad_gate, weight_gate, preferred_element_type=jnp.float32
    )
    grad_partial = grad_partial + jnp.einsum(
        "rh,dh->rd", grad_up, weight_up, preferred_element_type=jnp.float32
    )
    grad_home = to_homes(grad_partial)
    grad_pairs = jnp.take(grad_home, slot_dest, axis=0).reshape(tok_count, top_count, -1)
    grad_tokens = jnp.sum(grad_pairs.astype(jnp.float32), axis=1).astype(jnp.bfloat16)
    return (layer_out, grad_tokens)


def solution(mesh):
    in_specs = (
        P("expert", "half"),
        P("expert", "half"),
        P("expert", None),
        P("expert", None),
        P("expert"),
        P("expert", None, "half"),
        P("expert", None, "half"),
        P("expert", "half", None),
    )
    out_specs = (P("expert", "half"), P("expert", "half"))
    return jax.shard_map(shards, mesh=mesh, in_specs=in_specs, out_specs=out_specs, check_vma=False)
```
